128 devices in a mesh: seq: 4 (over x), tp: 32 (over z, y, core).
Axes of the slice: x: 4, y: 4, z: 4, core: 2. Of those that a mesh axis runs over, the one named last changes fastest.
Arguments:
- hidden_in: bfloat16 [96, 4, 1024], P('tp'), may hold values from -6 to 6
- new_query: bfloat16 [96, 4, 1024], P('tp'), may hold values from -70 to 70
- new_key: bfloat16 [96, 4, 1024], P('tp'), may hold values from -15 to 15
- new_value: bfloat16 [96, 4, 1024], P('tp'), may hold values from -6 to 6
- key_cache: bfloat16 [96, 4096, 1024], P('tp', 'seq'), may hold values from -16 to 16
- value_cache: bfloat16 [96, 4096, 1024], P('tp', 'seq'), may hold values from -6 to 6
- lengths: int32 [96], P('tp'), may hold values from 64 to 4096, as said below
- out_weight: bfloat16 [1024, 1024], replicated, may hold values from -0.1875 to 0.1875
- norm_gain: float32 [1024], replicated, may hold values from 0.5 to 1.5
- router_weight: bfloat16 [1024, 16], replicated, may hold values from -0.1875 to 0.1875
- expert_ids: int32 [96, 4, 2], P('tp'), may hold values from 0 to 15, all different within a row
- gate_weight: bfloat16 [45056, 1024], P(('seq', 'tp')), may hold values from -0.1875 to 0.1875
- up_weight: bfloat16 [45056, 1024], P(('seq', 'tp')), may hold values from -0.1875 to 0.1875
- down_weight: bfloat16 [45056, 1024], P(('seq', 'tp')), may hold values from -0.109375 to 0.109375
Outputs:
- attn_out: bfloat16 [96, 4, 1024], P('tp', None, 'seq')
- layer_out: bfloat16 [96, 4, 1024], P('tp', None, 'seq')
The draws below stay inside these ranges and needn't reach their ends.
Inputs may be any that keep to these rules, and one draw needn't show every extreme that they name: `lengths`: each length is 4096 or between 64 and 128; some request has 4096.
All inputs are finite; a program needn't handle non-finite values.
Results may differ from the reference program's by a relative error of at most 0.014.
Values may be sent and summed in bfloat16 or wider, within the bound.
A program may use at most 64 MiB of HBM per device.

```python
import jax
import jax.numpy as jnp
from jax import lax

D = 1024
HEADS = 16
FF = 2816
EXPERTS = 16
TOPK = 2
NEW = 4
CACHE = 4096
SHORT = 128
REQUESTS = 96
CAP = 15
N_SEQ = 4


def draw_key_cache(key, part):
    base = jnp.clip(2.5 * jax.random.normal(jax.random.fold_in(key, 3), (REQUESTS, CACHE, D), jnp.float32), -16.0, 16.0)
    return base.astype(jnp.bfloat16)


def draw_new_query(key, part):
    base = jnp.clip(jax.random.normal(jax.random.fold_in(key, 5), (REQUESTS, NEW, D), jnp.float32), -6.0, 6.0)
    return base.astype(jnp.bfloat16)


def draw_lengths(key, part):
    picked = jax.random.randint(jax.random.fold_in(key, 1), (REQUESTS,), 0, 4)
    shorter = jax.random.randint(jax.random.fold_in(key, 2), (REQUESTS,), SHORT // 2, SHORT + 1)
    result = jnp.where(picked == 0, CACHE, shorter)
    forced = jax.random.randint(jax.random.fold_in(key, 4), (), 0, REQUESTS)
    return result.at[forced].set(CACHE).astype(jnp.int32)


def level_of(rng, extent, split, least, largest):
    def one(dim, blocks):
        steps = jax.random.uniform(jax.random.fold_in(jax.random.fold_in(rng, 6), dim), (blocks,), jnp.float32, least / len(split), largest / len(split))
        return jnp.repeat(jnp.exp(steps), extent[dim] // blocks).reshape((-1,) + (1,) * (len(extent) - dim - 1))

    gain = one(*split[0])
    for cut in split[1:]:
        gain = gain * one(*cut)
    return gain


def different_ones(own_key, rows, amount, top, lift):
    order = jax.random.permutation(jax.random.fold_in(own_key, 1), amount)
    favour = order
    for power in range(3):
        favour = favour * favour // amount
    favour = favour * lift // amount
    chance = jax.random.randint(jax.random.fold_in(own_key, 2), (rows, amount), 0, 4096) + favour
    holders = jax.random.permutation(jax.random.fold_in(own_key, 3), rows)[jnp.arange(amount) % rows]
    chance = jnp.where(jnp.arange(rows)[:, None] == holders[None, :], 1 << 14, chance)
    priority = chance * amount + jnp.arange(amount)
    return lax.top_k(priority.astype(jnp.int32), top)[1].astype(jnp.int32)


def noise(rng, shape, spread, most, pieces=(), held_as=jnp.bfloat16):
    level = level_of(rng, shape, pieces, -0.22, 0.18) if pieces else 1.0
    entries = jax.random.normal(rng, shape, jnp.float32) * spread * level
    return jnp.minimum(jnp.maximum(entries, -most), most).astype(held_as)


def setup_inputs(seed: int = 0) -> dict:
    arg_keys = jax.random.split(jax.random.key(seed), 15)
    hidden_in = noise(arg_keys[0], (REQUESTS, NEW, D), 1.0, 6.0, ((0, 32),))
    new_query = draw_new_query(jax.random.fold_in(arg_keys[14], 71), 0)
    new_key = noise(arg_keys[2], (REQUESTS, NEW, D), 2.5, 15.0, ((0, 32),))
    new_value = noise(arg_keys[3], (REQUESTS, NEW, D), 1.0, 6.0, ((0, 32),))
    key_cache = draw_key_cache(jax.random.fold_in(arg_keys[14], 71), 0)
    value_cache = noise(arg_keys[5], (REQUESTS, CACHE, D), 1.0, 6.0, ((0, 32), (1, 4)))
    lengths = draw_lengths(jax.random.fold_in(arg_keys[14], 71), 0)
    out_weight = noise(arg_keys[7], (D, D), D ** -0.5, 0.1875)
    norm_gain = jnp.clip(1.0 + 0.1 * jax.random.normal(arg_keys[8], (D,), jnp.float32), 0.5, 1.5)
    router_weight = noise(arg_keys[9], (D, EXPERTS), D ** -0.5, 0.1875)
    expert_ids = different_ones(arg_keys[10], REQUESTS * NEW, EXPERTS, TOPK, 1024).reshape((REQUESTS, NEW, TOPK))
    gate_weight = noise(arg_keys[11], (EXPERTS * FF, D), D ** -0.5, 0.1875, ((0, 128),))
    up_weight = noise(arg_keys[12], (EXPERTS * FF, D), D ** -0.5, 0.1875, ((0, 128),))
    down_weight = noise(arg_keys[13], (EXPERTS * FF, D), FF ** -0.5, 0.109375, ((0, 128),))
    return {"hidden_in": hidden_in, "new_query": new_query, "new_key": new_key, "new_value": new_value, "key_cache": key_cache, "value_cache": value_cache, "lengths": lengths, "out_weight": out_weight, "norm_gain": norm_gain, "router_weight": router_weight, "expert_ids": expert_ids, "gate_weight": gate_weight, "up_weight": up_weight, "down_weight": down_weight}


masked_score = -1e+30
norm_epsilon = 1e-06

def attend_request(packed):
    query, fresh_key, fresh_value, keys, values, length = packed
    head_size = D // HEADS
    block = CACHE // N_SEQ
    scale = head_size ** (-0.5)
    query_heads = query.reshape(NEW, HEADS, head_size).astype(jnp.float32)
    cache_keys = keys.reshape(N_SEQ, block, HEADS, head_size).astype(jnp.float32)
    cache_values = values.reshape(N_SEQ, block, HEADS, head_size).astype(jnp.float32)
    fresh_keys = fresh_key.reshape(NEW, HEADS, head_size).astype(jnp.float32)
    fresh_values = fresh_value.reshape(NEW, HEADS, head_size).astype(jnp.float32)
    scores = jnp.einsum('the,bphe->bhtp', query_heads, cache_keys) * scale
    positions = jnp.arange(CACHE, dtype=jnp.int32).reshape(N_SEQ, block)
    usable = (positions < length)[:, None, None, :]
    scores = jnp.where(usable, scores, masked_score)
    fresh_scores = jnp.einsum('the,she->hts', query_heads, fresh_keys) * scale
    causal = (jnp.arange(NEW)[:, None] >= jnp.arange(NEW)[None, :])[None]
    fresh_scores = jnp.where(causal, fresh_scores, masked_score)
    block_max = lax.optimization_barrier(jnp.max(scores, axis=3))
    first_max = jnp.maximum(block_max[0], lax.optimization_barrier(jnp.max(fresh_scores, axis=2)))
    block_max = jnp.concatenate([first_max[None], block_max[1:]], axis=0)
    weights = jnp.where(usable, jnp.exp(scores - block_max[..., None]), 0.0)
    fresh_weights = jnp.where(causal, jnp.exp(fresh_scores - first_max[..., None]), 0.0)
    totals = lax.optimization_barrier(jnp.sum(weights, axis=3))
    first_total = totals[0] + lax.optimization_barrier(jnp.sum(fresh_weights, axis=2))
    totals = jnp.concatenate([first_total[None], totals[1:]], axis=0)
    rounded = lax.optimization_barrier(weights.astype(jnp.bfloat16)).astype(jnp.float32)
    fresh_rounded = lax.optimization_barrier(fresh_weights.astype(jnp.bfloat16)).astype(jnp.float32)
    partial_sums = jnp.einsum('bhtp,bphe->bhte', rounded, cache_values)
    first_sum = partial_sums[0] + jnp.einsum('hts,she->hte', fresh_rounded, fresh_values)
    partial_sums = jnp.concatenate([first_sum[None], partial_sums[1:]], axis=0)
    overall = lax.optimization_barrier(jnp.max(block_max, axis=0))
    factors = jnp.exp(block_max - overall)
    context = lax.optimization_barrier(jnp.sum(factors[..., None] * partial_sums, axis=0)) / lax.optimization_barrier(jnp.sum(factors * totals, axis=0))[..., None]
    return context.transpose(1, 0, 2).reshape(NEW, D)

def pick_slot(chosen_ids, earlier):
    onehot = chosen_ids[..., None] == jnp.arange(earlier.shape[2], dtype=jnp.int32)
    return lax.optimization_barrier(jnp.sum(jnp.where(onehot, earlier[:, :, None, :], 0), axis=3)).astype(jnp.int32)

def reference(hidden_in, new_query, new_key, new_value, key_cache, value_cache, lengths, out_weight, norm_gain, router_weight, expert_ids, gate_weight, up_weight, down_weight):
    contexts = lax.map(attend_request, (new_query, new_key, new_value, key_cache, value_cache, lengths))
    context = contexts.astype(jnp.bfloat16)
    attention = jnp.dot(context.reshape(REQUESTS * NEW, D), out_weight, preferred_element_type=jnp.float32).reshape(REQUESTS, NEW, D)
    residual = hidden_in.astype(jnp.float32) + attention
    normed = (residual * lax.rsqrt(lax.optimization_barrier(jnp.mean(residual * residual, axis=-1, keepdims=True)) + norm_epsilon) * norm_gain).astype(jnp.bfloat16)
    logits = jnp.dot(normed.reshape(REQUESTS * NEW, D), router_weight, preferred_element_type=jnp.float32).reshape(REQUESTS, NEW, EXPERTS)
    onehot = expert_ids[..., None] == jnp.arange(EXPERTS, dtype=jnp.int32)
    chosen = lax.optimization_barrier(jnp.sum(jnp.where(onehot, logits[:, :, None, :], 0.0), axis=3))
    share = 1.0 / (1.0 + jnp.exp(chosen[:, :, ::-1] - chosen))
    hits = lax.optimization_barrier(jnp.sum(onehot.astype(jnp.int32), axis=2)).astype(jnp.int32)
    earlier = (jnp.cumsum(hits, axis=0) - hits).astype(jnp.int32)
    slots = pick_slot(expert_ids, earlier)
    slot_range = jnp.arange(CAP, dtype=jnp.int32)
    normed_wide = normed.astype(jnp.float32)
    mixture = jnp.zeros((REQUESTS, NEW, D), jnp.float32)
    for expert in range(EXPERTS):
        match = expert_ids == expert
        slot_mine = lax.optimization_barrier(jnp.sum(jnp.where(match, slots, 0), axis=2)).astype(jnp.int32)
        share_mine = lax.optimization_barrier(jnp.sum(jnp.where(match, share, 0.0), axis=2))
        kept = jnp.any(match, axis=2) & (slot_mine < CAP)
        select = kept[None] & (slot_mine[None] == slot_range[:, None, None])
        buffer = jnp.einsum('crt,rtd->tcd', select.astype(jnp.float32), normed_wide, precision=lax.Precision.HIGHEST).astype(jnp.bfloat16).reshape(NEW * CAP, D)
        gate_rows = gate_weight[expert * FF:(expert + 1) * FF]
        up_rows = up_weight[expert * FF:(expert + 1) * FF]
        down_rows = down_weight[expert * FF:(expert + 1) * FF]
        gate = jnp.dot(buffer, gate_rows.T, preferred_element_type=jnp.float32)
        upward = jnp.dot(buffer, up_rows.T, preferred_element_type=jnp.float32)
        inner = (jax.nn.gelu(gate) * upward).astype(jnp.bfloat16)
        produced = jnp.dot(inner, down_rows, preferred_element_type=jnp.float32).reshape(NEW, CAP, D)
        placed = select.astype(jnp.float32) * share_mine[None]
        mixture = mixture + jnp.einsum('crt,tcd->rtd', placed, produced, precision=lax.Precision.HIGHEST)
    layer_out = (residual + mixture).astype(jnp.bfloat16)
    return (attention.astype(jnp.bfloat16), layer_out)
```

```python
import jax
import jax.numpy as jnp
from jax import lax
from jax.sharding import PartitionSpec as P

HEADS = 16


masked_score = -1e30
norm_epsilon = 1e-06


def body(
    hidden_in,
    new_query,
    new_key,
    new_value,
    key_cache,
    value_cache,
    lengths,
    out_weight,
    norm_gain,
    router_weight,
    expert_ids,
    gate_weight,
    up_weight,
    down_weight,
):
    req_dev, steps, width = hidden_in.shape
    block = key_cache.shape[1]
    head_size = width // HEADS
    scale = head_size ** (-0.5)
    seq_index = lax.axis_index("seq")
    tp_index = lax.axis_index("tp")
    seq_size = lax.axis_size("seq")
    tp_size = lax.axis_size("tp")
    rows = steps * HEADS

    head_mask = (jnp.arange(width) // head_size)[None, :] == jnp.arange(HEADS)[:, None]
    q_wide = jnp.where(head_mask[None, None], new_query[:, :, None, :], 0).reshape(
        req_dev, rows, width
    )
    with jax.named_scope("cache_scores"):
        scores = (
            jnp.einsum("rqd,rpd->rqp", q_wide, key_cache, preferred_element_type=jnp.float32)
            * scale
        )
    positions = seq_index * block + jnp.arange(block, dtype=jnp.int32)
    usable = (positions[None, :] < lengths[:, None])[:, None, :]
    scores = jnp.where(usable, scores, masked_score)
    fresh_scores = (
        jnp.einsum("rqd,rsd->rqs", q_wide, new_key, preferred_element_type=jnp.float32) * scale
    )
    causal = (
        (jnp.arange(rows)[:, None] // HEADS) >= jnp.arange(steps)[None, :]
    ) & (seq_index == 0)
    fresh_scores = jnp.where(causal, fresh_scores, masked_score)
    local_max = jnp.maximum(jnp.max(scores, axis=2), jnp.max(fresh_scores, axis=2))
    weights = jnp.where(usable, jnp.exp(scores - local_max[..., None]), 0.0)
    fresh_weights = jnp.where(causal, jnp.exp(fresh_scores - local_max[..., None]), 0.0)
    totals = jnp.sum(weights, axis=2) + jnp.sum(fresh_weights, axis=2)
    with jax.named_scope("cache_values"):
        wide_values = jnp.einsum(
            "rqp,rpd->rqd",
            weights.astype(jnp.bfloat16),
            value_cache,
            preferred_element_type=jnp.float32,
        )
    wide_values = wide_values + jnp.einsum(
        "rqs,rsd->rqd",
        fresh_weights.astype(jnp.bfloat16),
        new_value,
        preferred_element_type=jnp.float32,
    )
    partial = jnp.sum(
        jnp.where(head_mask[None, None], wide_values.reshape(req_dev, steps, HEADS, width), 0.0),
        axis=2,
    )
    stats = jnp.concatenate(
        [
            partial,
            local_max.reshape(req_dev, steps, HEADS),
            totals.reshape(req_dev, steps, HEADS),
        ],
        axis=2,
    )
    every = lax.all_gather(stats, "seq")
    block_sums = every[..., :width]
    block_max = every[..., width : width + HEADS]
    block_totals = every[..., width + HEADS :]
    overall = jnp.max(block_max, axis=0)
    factors = jnp.exp(block_max - overall[None])
    numer = jnp.sum(jnp.repeat(factors, head_size, axis=-1) * block_sums, axis=0)
    denom = jnp.sum(factors * block_totals, axis=0)
    context = (numer / jnp.repeat(denom, head_size, axis=-1)).astype(jnp.bfloat16)
    attention = jnp.einsum("rtd,de->rte", context, out_weight, preferred_element_type=jnp.float32)
    feature_block = width // seq_size
    attn_out = lax.dynamic_slice_in_dim(
        attention, seq_index * feature_block, feature_block, 2
    ).astype(jnp.bfloat16)
    residual = hidden_in.astype(jnp.float32) + attention
    normed = (
        residual
        * lax.rsqrt(jnp.mean(residual * residual, axis=-1, keepdims=True) + norm_epsilon)
        * norm_gain
    ).astype(jnp.bfloat16)
    experts = router_weight.shape[1]
    topk = expert_ids.shape[2]
    requests = req_dev * tp_size
    capacity = (5 * requests * topk + 4 * experts - 1) // (4 * experts)
    expert_range = jnp.arange(experts, dtype=jnp.int32)
    packed = jnp.concatenate([normed, expert_ids.astype(jnp.bfloat16)], axis=2)
    all_packed = lax.all_gather(packed, "tp", axis=0, tiled=True)
    all_normed = all_packed[:, :, :width]
    all_ids = all_packed[:, :, width:].astype(jnp.int32)
    onehot = all_ids[..., None] == expert_range
    hits = jnp.sum(onehot.astype(jnp.int32), axis=2)
    earlier = jnp.cumsum(hits, axis=0) - hits
    all_slots = jnp.sum(jnp.where(onehot, earlier[:, :, None, :], 0), axis=3)
    logits = jnp.einsum(
        "rtd,de->rte", all_normed, router_weight, preferred_element_type=jnp.float32
    )
    chosen = jnp.sum(jnp.where(onehot, logits[:, :, None, :], 0.0), axis=3)
    share = 1.0 / (1.0 + jnp.exp(chosen[:, :, ::-1] - chosen))
    slices = seq_size * tp_size // experts
    mine = (seq_index * tp_size + tp_index) // slices
    match = all_ids == mine
    slot_mine = jnp.sum(jnp.where(match, all_slots, 0), axis=2)
    share_mine = jnp.sum(jnp.where(match, share, 0.0), axis=2)
    kept = jnp.any(match, axis=2) & (slot_mine < capacity)
    select = kept[None] & (slot_mine[None] == jnp.arange(capacity, dtype=jnp.int32)[:, None, None])
    buffer = (
        jnp.einsum(
            "crt,rtd->tcd",
            select.astype(jnp.bfloat16),
            all_normed,
            preferred_element_type=jnp.float32,
        )
        .astype(jnp.bfloat16)
        .reshape(steps * capacity, width)
    )
    contract = (((1,), (1,)), ((), ()))
    gate = lax.dot_general(buffer, gate_weight, contract, preferred_element_type=jnp.float32)
    upward = lax.dot_general(buffer, up_weight, contract, preferred_element_type=jnp.float32)
    inner = (jax.nn.gelu(gate) * upward).astype(jnp.bfloat16)
    produced = jnp.dot(inner, down_weight, preferred_element_type=jnp.float32)
    placed = select.astype(jnp.float32) * share_mine[None]
    term = jnp.einsum(
        "crt,tcd->rtd",
        placed,
        produced.reshape(steps, capacity, width),
        precision=lax.Precision.HIGHEST,
    )
    term = (
        term.astype(jnp.bfloat16)
        .reshape(tp_size, req_dev, steps, seq_size, feature_block)
        .transpose(0, 3, 1, 2, 4)
        .reshape(tp_size * seq_size, req_dev, steps, feature_block)
    )
    term = term.reshape(tp_size * seq_size, req_dev * steps, feature_block).transpose(1, 0, 2)
    term = term.reshape(req_dev * steps, tp_size * seq_size * feature_block)
    mixture = lax.psum_scatter(term, ("tp", "seq"), scatter_dimension=1, tiled=True)
    mixture = mixture.reshape(req_dev, steps, feature_block).astype(jnp.float32)
    own_residual = lax.dynamic_slice_in_dim(residual, seq_index * feature_block, feature_block, 2)
    layer_out = (own_residual + mixture).astype(jnp.bfloat16)
    return (attn_out, layer_out)


def solution(mesh):
    return jax.shard_map(
        body,
        mesh=mesh,
        in_specs=(
            P("tp", None, None),
            P("tp", None, None),
            P("tp", None, None),
            P("tp", None, None),
            P("tp", "seq", None),
            P("tp", "seq", None),
            P("tp"),
            P(),
            P(),
            P(),
            P("tp", None, None),
            P(("seq", "tp"), None),
            P(("seq", "tp"), None),
            P(("seq", "tp"), None),
        ),
        out_specs=(P("tp", None, "seq"), P("tp", None, "seq")),
        check_vma=False,
    )
```

```python
import functools

import jax
import jax.numpy as jnp
from jax import lax
from jax.experimental import pallas as pl
from jax.experimental.pallas import tpu as pltpu
from jax.sharding import PartitionSpec as P

HEADS = 16


masked_score = -1e30
norm_epsilon = 1e-06


def combine_kernel(seq_size, tp_size, slices, experts, part_ref, out_ref, recv, summed, landing,
                   send1, recv1, send2, recv2):
    mesh_type = pl.DeviceIdType.MESH
    s = lax.axis_index("seq")
    t = lax.axis_index("tp")
    groups = tp_size // slices
    g = t // slices
    j = t % slices
    chunk = recv.shape[2]
    halves = slices // seq_size
    expert = s * groups + g

    def stage1(i):
        return pltpu.make_async_remote_copy(
            part_ref.at[:, pl.ds(i * chunk, chunk)],
            recv.at[j],
            send1.at[i],
            recv1.at[j],
            device_id=(s, g * slices + i),
            device_id_type=mesh_type,
        )

    def stage1_local(i):
        return pltpu.make_async_copy(part_ref.at[:, pl.ds(i * chunk, chunk)], recv.at[i], recv1.at[i])

    for i in range(slices):
        @pl.when(j == i)
        def _():
            stage1_local(i).start()

        @pl.when(j != i)
        def _():
            stage1(i).start()

    for i in range(slices):
        @pl.when(j == i)
        def _():
            stage1_local(i).wait()

        @pl.when(j != i)
        def _():
            stage1(i).wait_send()
            pltpu.make_async_remote_copy(
                part_ref.at[:, pl.ds(0, chunk)],
                recv.at[i],
                send1.at[i],
                recv1.at[i],
                device_id=(s, g * slices + i),
                device_id_type=mesh_type,
            ).wait_recv()

    total = recv[0]
    for i in range(1, slices):
        total = total + recv[i]
    summed[...] = total

    dest_seq = j // halves
    half = j % halves
    slot = expert * halves + half

    def stage2(u):
        return pltpu.make_async_remote_copy(
            summed,
            landing.at[expert, half],
            send2.at[u],
            recv2.at[slot],
            device_id=(dest_seq, u),
            device_id_type=mesh_type,
        )

    def stage2_local():
        return pltpu.make_async_copy(summed, landing.at[expert, half], recv2.at[slot])

    for u in range(tp_size):
        mine = (dest_seq == s) & (t == u)

        @pl.when(mine)
        def _():
            stage2_local().start()

        @pl.when(jnp.logical_not(mine))
        def _():
            stage2(u).start()

    for u in range(tp_size):
        mine = (dest_seq == s) & (t == u)

        @pl.when(jnp.logical_not(mine))
        def _():
            stage2(u).wait_send()

    for e in range(experts):
        for h in range(halves):
            src_seq = e // groups
            src_t = (e % groups) * slices + s * halves + h
            mine = (src_seq == s) & (src_t == t)
            at = e * halves + h

            @pl.when(mine)
            def _():
                pltpu.make_async_copy(summed, landing.at[e, h], recv2.at[at]).wait()

            @pl.when(jnp.logical_not(mine))
            def _():
                pltpu.make_async_remote_copy(
                    summed,
                    landing.at[e, h],
                    send2.at[0],
                    recv2.at[at],
                    device_id=(src_seq, src_t),
                    device_id_type=mesh_type,
                ).wait_recv()

    out_ref[...] = landing[...]


def combine_rows(part, seq_size, tp_size, slices, experts):
    rows, width = part.shape
    chunk = width // slices
    halves = slices // seq_size
    return pl.pallas_call(
        functools.partial(combine_kernel, seq_size, tp_size, slices, experts),
        out_shape=jax.ShapeDtypeStruct((experts, halves, rows, chunk), jnp.float32),
        in_specs=[pl.BlockSpec(memory_space=pltpu.VMEM)],
        out_specs=pl.BlockSpec(memory_space=pltpu.VMEM),
        scratch_shapes=[
            pltpu.VMEM((slices, rows, chunk), jnp.float32),
            pltpu.VMEM((rows, chunk), jnp.float32),
            pltpu.VMEM((experts, halves, rows, chunk), jnp.float32),
            pltpu.SemaphoreType.DMA((slices,)),
            pltpu.SemaphoreType.DMA((slices,)),
            pltpu.SemaphoreType.DMA((tp_size,)),
            pltpu.SemaphoreType.DMA((experts * halves,)),
        ],
        compiler_params=pltpu.CompilerParams(has_side_effects=True),
    )(part)


def body(
    hidden_in,
    new_query,
    new_key,
    new_value,
    key_cache,
    value_cache,
    lengths,
    out_weight,
    norm_gain,
    router_weight,
    expert_ids,
    gate_weight,
    up_weight,
    down_weight,
):
    req_dev, steps, width = hidden_in.shape
    block = key_cache.shape[1]
    head_size = width // HEADS
    scale = head_size ** (-0.5)
    seq_index = lax.axis_index("seq")
    tp_index = lax.axis_index("tp")
    seq_size = lax.axis_size("seq")
    tp_size = lax.axis_size("tp")
    rows = steps * HEADS

    head_mask = (jnp.arange(width) // head_size)[None, :] == jnp.arange(HEADS)[:, None]
    q_wide = jnp.where(head_mask[None, None], new_query[:, :, None, :], 0).reshape(
        req_dev, rows, width
    )
    with jax.named_scope("cache_scores"):
        scores = (
            jnp.einsum("rqd,rpd->rqp", q_wide, key_cache, preferred_element_type=jnp.float32)
            * scale
        )
    positions = seq_index * block + jnp.arange(block, dtype=jnp.int32)
    usable = (positions[None, :] < lengths[:, None])[:, None, :]
    scores = jnp.where(usable, scores, masked_score)
    fresh_scores = (
        jnp.einsum("rqd,rsd->rqs", q_wide, new_key, preferred_element_type=jnp.float32) * scale
    )
    causal = (
        (jnp.arange(rows)[:, None] // HEADS) >= jnp.arange(steps)[None, :]
    ) & (seq_index == 0)
    fresh_scores = jnp.where(causal, fresh_scores, masked_score)
    local_max = jnp.maximum(jnp.max(scores, axis=2), jnp.max(fresh_scores, axis=2))
    weights = jnp.where(usable, jnp.exp(scores - local_max[..., None]), 0.0)
    fresh_weights = jnp.where(causal, jnp.exp(fresh_scores - local_max[..., None]), 0.0)
    totals = jnp.sum(weights, axis=2) + jnp.sum(fresh_weights, axis=2)
    with jax.named_scope("cache_values"):
        wide_values = jnp.einsum(
            "rqp,rpd->rqd",
            weights.astype(jnp.bfloat16),
            value_cache,
            preferred_element_type=jnp.float32,
        )
    wide_values = wide_values + jnp.einsum(
        "rqs,rsd->rqd",
        fresh_weights.astype(jnp.bfloat16),
        new_value,
        preferred_element_type=jnp.float32,
    )
    partial = jnp.sum(
        jnp.where(head_mask[None, None], wide_values.reshape(req_dev, steps, HEADS, width), 0.0),
        axis=2,
    )
    stats = jnp.concatenate(
        [
            partial,
            local_max.reshape(req_dev, steps, HEADS),
            totals.reshape(req_dev, steps, HEADS),
        ],
        axis=2,
    )
    every = lax.all_gather(stats, "seq")
    block_sums = every[..., :width]
    block_max = every[..., width : width + HEADS]
    block_totals = every[..., width + HEADS :]
    overall = jnp.max(block_max, axis=0)
    factors = jnp.exp(block_max - overall[None])
    numer = jnp.sum(jnp.repeat(factors, head_size, axis=-1) * block_sums, axis=0)
    denom = jnp.sum(factors * block_totals, axis=0)
    context = (numer / jnp.repeat(denom, head_size, axis=-1)).astype(jnp.bfloat16)
    attention = jnp.einsum("rtd,de->rte", context, out_weight, preferred_element_type=jnp.float32)
    feature_block = width // seq_size
    attn_out = lax.dynamic_slice_in_dim(
        attention, seq_index * feature_block, feature_block, 2
    ).astype(jnp.bfloat16)
    residual = hidden_in.astype(jnp.float32) + attention
    normed = (
        residual
        * lax.rsqrt(jnp.mean(residual * residual, axis=-1, keepdims=True) + norm_epsilon)
        * norm_gain
    ).astype(jnp.bfloat16)
    experts = router_weight.shape[1]
    topk = expert_ids.shape[2]
    requests = req_dev * tp_size
    capacity = (5 * requests * topk + 4 * experts - 1) // (4 * experts)
    expert_range = jnp.arange(experts, dtype=jnp.int32)
    packed = jnp.concatenate([normed, expert_ids.astype(jnp.bfloat16)], axis=2)
    all_packed = lax.all_gather(packed, "tp", axis=0, tiled=True)
    all_normed = all_packed[:, :, :width]
    all_ids = all_packed[:, :, width:].astype(jnp.int32)
    onehot = all_ids[..., None] == expert_range
    hits = jnp.sum(onehot.astype(jnp.int32), axis=2)
    earlier = jnp.cumsum(hits, axis=0) - hits
    all_slots = jnp.sum(jnp.where(onehot, earlier[:, :, None, :], 0), axis=3)
    logits = jnp.einsum(
        "rtd,de->rte", all_normed, router_weight, preferred_element_type=jnp.float32
    )
    chosen = jnp.sum(jnp.where(onehot, logits[:, :, None, :], 0.0), axis=3)
    share = 1.0 / (1.0 + jnp.exp(chosen[:, :, ::-1] - chosen))
    slices = seq_size * tp_size // experts
    mine = (seq_index * tp_size + tp_index) // slices
    match = all_ids == mine
    slot_mine = jnp.sum(jnp.where(match, all_slots, 0), axis=2)
    share_mine = jnp.sum(jnp.where(match, share, 0.0), axis=2)
    kept = jnp.any(match, axis=2) & (slot_mine < capacity)
    select = kept[None] & (slot_mine[None] == jnp.arange(capacity, dtype=jnp.int32)[:, None, None])
    buffer = (
        jnp.einsum(
            "crt,rtd->tcd",
            select.astype(jnp.bfloat16),
            all_normed,
            preferred_element_type=jnp.float32,
        )
        .astype(jnp.bfloat16)
        .reshape(steps * capacity, width)
    )
    contract = (((1,), (1,)), ((), ()))
    gate = lax.dot_general(buffer, gate_weight, contract, preferred_element_type=jnp.float32)
    upward = lax.dot_general(buffer, up_weight, contract, preferred_element_type=jnp.float32)
    inner = (jax.nn.gelu(gate) * upward).astype(jnp.bfloat16)
    produced = jnp.dot(inner, down_weight, preferred_element_type=jnp.float32)
    groups = tp_size // slices
    padded = 8 * ((steps * capacity + 7) // 8)
    part = jnp.pad(produced, ((0, padded - steps * capacity), (0, 0)))
    gathered = combine_rows(part, seq_size, tp_size, slices, experts)
    gathered = gathered.transpose(0, 2, 1, 3).reshape(experts * padded, feature_block)
    own_ids = expert_ids
    own_slots = lax.dynamic_slice_in_dim(all_slots, tp_index * req_dev, req_dev, 0)
    own_share = lax.dynamic_slice_in_dim(share, tp_index * req_dev, req_dev, 0)
    own_kept = own_slots < capacity
    row_of = own_ids * padded + jnp.arange(steps, dtype=jnp.int32)[None, :, None] * capacity + own_slots
    weight = jnp.where(own_kept, own_share, 0.0)
    pick = jnp.sum(
        jnp.where(
            row_of[..., None] == jnp.arange(experts * padded, dtype=jnp.int32),
            weight[..., None],
            0.0,
        ),
        axis=2,
    ).reshape(req_dev * steps, experts * padded)
    mixture = jnp.dot(pick, gathered, precision=lax.Precision.HIGHEST).reshape(
        req_dev, steps, feature_block
    )
    own_residual = lax.dynamic_slice_in_dim(residual, seq_index * feature_block, feature_block, 2)
    layer_out = (own_residual + mixture).astype(jnp.bfloat16)
    return (attn_out, layer_out)


def solution(mesh):
    return jax.shard_map(
        body,
        mesh=mesh,
        in_specs=(
            P("tp", None, None),
            P("tp", None, None),
            P("tp", None, None),
            P("tp", None, None),
            P("tp", "seq", None),
            P("tp", "seq", None),
            P("tp"),
            P(),
            P(),
            P(),
            P("tp", None, None),
            P(("seq", "tp"), None),
            P(("seq", "tp"), None),
            P(("seq", "tp"), None),
        ),
        out_specs=(P("tp", None, "seq"), P("tp", None, "seq")),
        check_vma=False,
    )
```

```python
import functools

import jax
import jax.numpy as jnp
from jax import lax
from jax.experimental import pallas as pl
from jax.experimental.pallas import tpu as pltpu
from jax.sharding import PartitionSpec as P

HEADS = 16


masked_score = -1e30
norm_epsilon = 1e-06


def combine_kernel(seq_size, tp_size, slices, part_ref, out_ref, recv, summed, middle, landing,
                   send1, recv1, send2, recv2, send3, recv3):
    mesh_type = pl.DeviceIdType.MESH
    s = lax.axis_index("seq")
    t = lax.axis_index("tp")
    g = t // slices
    j = t % slices
    chunk = recv.shape[2]
    halves = slices // seq_size

    def stage1(i):
        return pltpu.make_async_remote_copy(
            part_ref.at[:, pl.ds(i * chunk, chunk)],
            recv.at[j],
            send1.at[i],
            recv1.at[j],
            device_id=(s, g * slices + i),
            device_id_type=mesh_type,
        )

    def stage1_local(i):
        return pltpu.make_async_copy(part_ref.at[:, pl.ds(i * chunk, chunk)], recv.at[i], recv1.at[i])

    for i in range(slices):
        @pl.when(j == i)
        def _():
            stage1_local(i).start()

        @pl.when(j != i)
        def _():
            stage1(i).start()

    for i in range(slices):
        @pl.when(j == i)
        def _():
            stage1_local(i).wait()

        @pl.when(j != i)
        def _():
            stage1(i).wait_send()
            pltpu.make_async_remote_copy(
                part_ref.at[:, pl.ds(0, chunk)],
                recv.at[i],
                send1.at[i],
                recv1.at[i],
                device_id=(s, g * slices + i),
                device_id_type=mesh_type,
            ).wait_recv()

    total = recv[0]
    for i in range(1, slices):
        total = total + recv[i]
    summed[...] = total.astype(summed.dtype)

    dest_seq = j // halves
    half = j % halves
    dest_t = g * slices + s * halves + half
    to_self = dest_seq == s

    @pl.when(to_self)
    def _():
        pltpu.make_async_copy(summed, middle, recv2.at[0]).start()
        pltpu.make_async_copy(summed, middle, recv2.at[0]).wait()

    @pl.when(jnp.logical_not(to_self))
    def _():
        copy = pltpu.make_async_remote_copy(
            summed, middle, send2.at[0], recv2.at[0],
            device_id=(dest_seq, dest_t), device_id_type=mesh_type,
        )
        copy.start()
        copy.wait_send()

    src_seq = (t % slices) // halves
    src_t = g * slices + s * halves + t % halves
    from_self = src_seq == s

    @pl.when(jnp.logical_not(from_self))
    def _():
        pltpu.make_async_remote_copy(
            summed, middle, send2.at[0], recv2.at[0],
            device_id=(src_seq, src_t), device_id_type=mesh_type,
        ).wait_recv()

    def stage3(u):
        return pltpu.make_async_remote_copy(
            middle, landing.at[t], send3.at[u], recv3.at[t],
            device_id=(s, u), device_id_type=mesh_type,
        )

    for u in range(tp_size):
        @pl.when(t == u)
        def _():
            pltpu.make_async_copy(middle, landing.at[u], recv3.at[u]).start()

        @pl.when(t != u)
        def _():
            stage3(u).start()

    for u in range(tp_size):
        @pl.when(t == u)
        def _():
            pltpu.make_async_copy(middle, landing.at[u], recv3.at[u]).wait()

        @pl.when(t != u)
        def _():
            stage3(u).wait_send()
            pltpu.make_async_remote_copy(
                middle, landing.at[u], send3.at[u], recv3.at[u],
                device_id=(s, u), device_id_type=mesh_type,
            ).wait_recv()

    out_ref[...] = landing[...]


def combine_rows(part, seq_size, tp_size, slices):
    rows, width = part.shape
    chunk = width // slices
    return pl.pallas_call(
        functools.partial(combine_kernel, seq_size, tp_size, slices),
        out_shape=jax.ShapeDtypeStruct((tp_size, rows, chunk), jnp.bfloat16),
        in_specs=[pl.BlockSpec(memory_space=pltpu.VMEM)],
        out_specs=pl.BlockSpec(memory_space=pltpu.VMEM),
        scratch_shapes=[
            pltpu.VMEM((slices, rows, chunk), jnp.float32),
            pltpu.VMEM((rows, chunk), jnp.bfloat16),
            pltpu.VMEM((rows, chunk), jnp.bfloat16),
            pltpu.VMEM((tp_size, rows, chunk), jnp.bfloat16),
            pltpu.SemaphoreType.DMA((slices,)),
            pltpu.SemaphoreType.DMA((slices,)),
            pltpu.SemaphoreType.DMA((1,)),
            pltpu.SemaphoreType.DMA((1,)),
            pltpu.SemaphoreType.DMA((tp_size,)),
            pltpu.SemaphoreType.DMA((tp_size,)),
        ],
        compiler_params=pltpu.CompilerParams(has_side_effects=True),
    )(part)


def body(
    hidden_in,
    new_query,
    new_key,
    new_value,
    key_cache,
    value_cache,
    lengths,
    out_weight,
    norm_gain,
    router_weight,
    expert_ids,
    gate_weight,
    up_weight,
    down_weight,
):
    req_dev, steps, width = hidden_in.shape
    block = key_cache.shape[1]
    head_size = width // HEADS
    scale = head_size ** (-0.5)
    seq_index = lax.axis_index("seq")
    tp_index = lax.axis_index("tp")
    seq_size = lax.axis_size("seq")
    tp_size = lax.axis_size("tp")
    rows = steps * HEADS

    head_mask = (jnp.arange(width) // head_size)[None, :] == jnp.arange(HEADS)[:, None]
    q_wide = jnp.where(head_mask[None, None], new_query[:, :, None, :], 0).reshape(
        req_dev, rows, width
    )
    with jax.named_scope("cache_scores"):
        scores = (
            jnp.einsum("rqd,rpd->rqp", q_wide, key_cache, preferred_element_type=jnp.float32)
            * scale
        )
    positions = seq_index * block + jnp.arange(block, dtype=jnp.int32)
    usable = (positions[None, :] < lengths[:, None])[:, None, :]
    scores = jnp.where(usable, scores, masked_score)
    fresh_scores = (
        jnp.einsum("rqd,rsd->rqs", q_wide, new_key, preferred_element_type=jnp.float32) * scale
    )
    causal = (
        (jnp.arange(rows)[:, None] // HEADS) >= jnp.arange(steps)[None, :]
    ) & (seq_index == 0)
    fresh_scores = jnp.where(causal, fresh_scores, masked_score)
    local_max = jnp.maximum(jnp.max(scores, axis=2), jnp.max(fresh_scores, axis=2))
    weights = jnp.where(usable, jnp.exp(scores - local_max[..., None]), 0.0)
    fresh_weights = jnp.where(causal, jnp.exp(fresh_scores - local_max[..., None]), 0.0)
    totals = jnp.sum(weights, axis=2) + jnp.sum(fresh_weights, axis=2)
    with jax.named_scope("cache_values"):
        wide_values = jnp.einsum(
            "rqp,rpd->rqd",
            weights.astype(jnp.bfloat16),
            value_cache,
            preferred_element_type=jnp.float32,
        )
    wide_values = wide_values + jnp.einsum(
        "rqs,rsd->rqd",
        fresh_weights.astype(jnp.bfloat16),
        new_value,
        preferred_element_type=jnp.float32,
    )
    partial = jnp.sum(
        jnp.where(head_mask[None, None], wide_values.reshape(req_dev, steps, HEADS, width), 0.0),
        axis=2,
    )
    stats = jnp.concatenate(
        [
            partial,
            local_max.reshape(req_dev, steps, HEADS),
            totals.reshape(req_dev, steps, HEADS),
        ],
        axis=2,
    )
    every = lax.all_gather(stats, "seq")
    block_sums = every[..., :width]
    block_max = every[..., width : width + HEADS]
    block_totals = every[..., width + HEADS :]
    overall = jnp.max(block_max, axis=0)
    factors = jnp.exp(block_max - overall[None])
    numer = jnp.sum(jnp.repeat(factors, head_size, axis=-1) * block_sums, axis=0)
    denom = jnp.sum(factors * block_totals, axis=0)
    context = (numer / jnp.repeat(denom, head_size, axis=-1)).astype(jnp.bfloat16)
    attention = jnp.einsum("rtd,de->rte", context, out_weight, preferred_element_type=jnp.float32)
    feature_block = width // seq_size
    attn_out = lax.dynamic_slice_in_dim(
        attention, seq_index * feature_block, feature_block, 2
    ).astype(jnp.bfloat16)
    residual = hidden_in.astype(jnp.float32) + attention
    normed = (
        residual
        * lax.rsqrt(jnp.mean(residual * residual, axis=-1, keepdims=True) + norm_epsilon)
        * norm_gain
    ).astype(jnp.bfloat16)
    experts = router_weight.shape[1]
    topk = expert_ids.shape[2]
    requests = req_dev * tp_size
    capacity = (5 * requests * topk + 4 * experts - 1) // (4 * experts)
    expert_range = jnp.arange(experts, dtype=jnp.int32)
    packed = jnp.concatenate([normed, expert_ids.astype(jnp.bfloat16)], axis=2)
    all_packed = lax.all_gather(packed, "tp", axis=0, tiled=True)
    all_normed = all_packed[:, :, :width]
    all_ids = all_packed[:, :, width:].astype(jnp.int32)
    onehot = all_ids[..., None] == expert_range
    hits = jnp.sum(onehot.astype(jnp.int32), axis=2)
    earlier = jnp.cumsum(hits, axis=0) - hits
    all_slots = jnp.sum(jnp.where(onehot, earlier[:, :, None, :], 0), axis=3)
    logits = jnp.einsum(
        "rtd,de->rte", all_normed, router_weight, preferred_element_type=jnp.float32
    )
    chosen = jnp.sum(jnp.where(onehot, logits[:, :, None, :], 0.0), axis=3)
    share = 1.0 / (1.0 + jnp.exp(chosen[:, :, ::-1] - chosen))
    slices = seq_size * tp_size // experts
    mine = (seq_index * tp_size + tp_index) // slices
    match = all_ids == mine
    slot_mine = jnp.sum(jnp.where(match, all_slots, 0), axis=2)
    share_mine = jnp.sum(jnp.where(match, share, 0.0), axis=2)
    kept = jnp.any(match, axis=2) & (slot_mine < capacity)
    select = kept[None] & (slot_mine[None] == jnp.arange(capacity, dtype=jnp.int32)[:, None, None])
    buffer = (
        jnp.einsum(
            "crt,rtd->tcd",
            select.astype(jnp.bfloat16),
            all_normed,
            preferred_element_type=jnp.float32,
        )
        .astype(jnp.bfloat16)
        .reshape(steps * capacity, width)
    )
    contract = (((1,), (1,)), ((), ()))
    gate = lax.dot_general(buffer, gate_weight, contract, preferred_element_type=jnp.float32)
    upward = lax.dot_general(buffer, up_weight, contract, preferred_element_type=jnp.float32)
    inner = (jax.nn.gelu(gate) * upward).astype(jnp.bfloat16)
    produced = jnp.dot(inner, down_weight, preferred_element_type=jnp.float32)
    groups = tp_size // slices
    padded = 8 * ((steps * capacity + 7) // 8)
    part = jnp.pad(produced, ((0, padded - steps * capacity), (0, 0)))
    gathered = combine_rows(part, seq_size, tp_size, slices)
    halves = slices // seq_size
    gathered = gathered.astype(jnp.float32).reshape(groups, tp_size // (groups * halves), halves, padded, width // slices)
    own_slots = lax.dynamic_slice_in_dim(all_slots, tp_index * req_dev, req_dev, 0)
    own_share = lax.dynamic_slice_in_dim(share, tp_index * req_dev, req_dev, 0)
    weight = jnp.where(own_slots < capacity, own_share, 0.0)
    row_of = jnp.arange(steps, dtype=jnp.int32)[None, :, None] * capacity + own_slots
    hit = (
        (expert_ids[..., None, None, None] % groups == jnp.arange(groups)[:, None, None])
        & (expert_ids[..., None, None, None] // groups == jnp.arange(tp_size // (groups * halves))[None, :, None])
        & (row_of[..., None, None, None] == jnp.arange(padded)[None, None, :])
    )
    pick = jnp.sum(jnp.where(hit, weight[..., None, None, None], 0.0), axis=2)
    mixture = jnp.einsum(
        "rtzyp,zyhpf->rthf", pick, gathered, precision=lax.Precision.HIGHEST
    ).reshape(req_dev, steps, feature_block)
    own_residual = lax.dynamic_slice_in_dim(residual, seq_index * feature_block, feature_block, 2)
    layer_out = (own_residual + mixture).astype(jnp.bfloat16)
    return (attn_out, layer_out)


def solution(mesh):
    return jax.shard_map(
        body,
        mesh=mesh,
        in_specs=(
            P("tp", None, None),
            P("tp", None, None),
            P("tp", None, None),
            P("tp", None, None),
            P("tp", "seq", None),
            P("tp", "seq", None),
            P("tp"),
            P(),
            P(),
            P(),
            P("tp", None, None),
            P(("seq", "tp"), None),
            P(("seq", "tp"), None),
            P(("seq", "tp"), None),
        ),
        out_specs=(P("tp", None, "seq"), P("tp", None, "seq")),
        check_vma=False,
    )
```

```python
import functools

import jax
import jax.numpy as jnp
from jax import lax
from jax.experimental import pallas as pl
from jax.experimental.pallas import tpu as pltpu
from jax.sharding import PartitionSpec as P

HEADS = 16


masked_score = -1e30
norm_epsilon = 1e-06


def combine_kernel(seq_size, tp_size, slices, part_ref, out_ref, recv, summed, middle, landing,
                   send1, recv1, send2, recv2, send3, recv3):
    mesh_type = pl.DeviceIdType.MESH
    s = lax.axis_index("seq")
    t = lax.axis_index("tp")
    g = t // slices
    j = t % slices
    chunk = recv.shape[2]
    halves = slices // seq_size

    def stage1(i):
        return pltpu.make_async_remote_copy(
            part_ref.at[:, pl.ds(i * chunk, chunk)],
            recv.at[j],
            send1.at[i],
            recv1.at[j],
            device_id=(s, g * slices + i),
            device_id_type=mesh_type,
        )

    def stage1_local(i):
        return pltpu.make_async_copy(part_ref.at[:, pl.ds(i * chunk, chunk)], recv.at[i], recv1.at[i])

    for i in range(slices):
        @pl.when(j == i)
        def _():
            stage1_local(i).start()

        @pl.when(j != i)
        def _():
            stage1(i).start()

    for i in range(slices):
        @pl.when(j == i)
        def _():
            stage1_local(i).wait()

        @pl.when(j != i)
        def _():
            stage1(i).wait_send()
            pltpu.make_async_remote_copy(
                part_ref.at[:, pl.ds(0, chunk)],
                recv.at[i],
                send1.at[i],
                recv1.at[i],
                device_id=(s, g * slices + i),
                device_id_type=mesh_type,
            ).wait_recv()

    total = recv[0]
    for i in range(1, slices):
        total = total + recv[i]
    summed[...] = total.astype(summed.dtype)

    dest_seq = j // halves
    half = j % halves
    dest_t = g * slices + s * halves + half
    to_self = dest_seq == s

    @pl.when(to_self)
    def _():
        pltpu.make_async_copy(summed, middle, recv2.at[0]).start()
        pltpu.make_async_copy(summed, middle, recv2.at[0]).wait()

    @pl.when(jnp.logical_not(to_self))
    def _():
        copy = pltpu.make_async_remote_copy(
            summed, middle, send2.at[0], recv2.at[0],
            device_id=(dest_seq, dest_t), device_id_type=mesh_type,
        )
        copy.start()
        copy.wait_send()

    src_seq = (t % slices) // halves
    src_t = g * slices + s * halves + t % halves
    from_self = src_seq == s

    @pl.when(jnp.logical_not(from_self))
    def _():
        pltpu.make_async_remote_copy(
            summed, middle, send2.at[0], recv2.at[0],
            device_id=(src_seq, src_t), device_id_type=mesh_type,
        ).wait_recv()

    def stage3(u):
        return pltpu.make_async_remote_copy(
            middle, landing.at[t], send3.at[u], recv3.at[t],
            device_id=(s, u), device_id_type=mesh_type,
        )

    for u in range(tp_size):
        @pl.when(t == u)
        def _():
            pltpu.make_async_copy(middle, landing.at[u], recv3.at[u]).start()

        @pl.when(t != u)
        def _():
            stage3(u).start()

    for u in range(tp_size):
        @pl.when(t == u)
        def _():
            pltpu.make_async_copy(middle, landing.at[u], recv3.at[u]).wait()

        @pl.when(t != u)
        def _():
            stage3(u).wait_send()
            pltpu.make_async_remote_copy(
                middle, landing.at[u], send3.at[u], recv3.at[u],
                device_id=(s, u), device_id_type=mesh_type,
            ).wait_recv()

    out_ref[...] = landing[...]


def gather_kernel(axis, size, piece_ref, out_ref, landing, send, recv):
    mesh_type = pl.DeviceIdType.MESH
    me = lax.axis_index(axis)
    other = lax.axis_index("tp" if axis == "seq" else "seq")

    def peer(u):
        return (u, other) if axis == "seq" else (other, u)

    def remote(u, slot):
        return pltpu.make_async_remote_copy(
            piece_ref, landing.at[slot], send.at[u], recv.at[slot],
            device_id=peer(u), device_id_type=mesh_type,
        )

    for u in range(size):
        @pl.when(me == u)
        def _():
            pltpu.make_async_copy(piece_ref, landing.at[u], recv.at[u]).start()

        @pl.when(me != u)
        def _():
            remote(u, me).start()

    for u in range(size):
        @pl.when(me == u)
        def _():
            pltpu.make_async_copy(piece_ref, landing.at[u], recv.at[u]).wait()

        @pl.when(me != u)
        def _():
            remote(u, me).wait_send()
            remote(u, u).wait_recv()

    out_ref[...] = landing[...]


def gather_axis(piece, axis, size):
    return pl.pallas_call(
        functools.partial(gather_kernel, axis, size),
        out_shape=jax.ShapeDtypeStruct((size,) + piece.shape, piece.dtype),
        in_specs=[pl.BlockSpec(memory_space=pltpu.VMEM)],
        out_specs=pl.BlockSpec(memory_space=pltpu.VMEM),
        scratch_shapes=[
            pltpu.VMEM((size,) + piece.shape, piece.dtype),
            pltpu.SemaphoreType.DMA((size,)),
            pltpu.SemaphoreType.DMA((size,)),
        ],
        compiler_params=pltpu.CompilerParams(has_side_effects=True),
    )(piece)


def combine_rows(part, seq_size, tp_size, slices):
    rows, width = part.shape
    chunk = width // slices
    return pl.pallas_call(
        functools.partial(combine_kernel, seq_size, tp_size, slices),
        out_shape=jax.ShapeDtypeStruct((tp_size, rows, chunk), jnp.bfloat16),
        in_specs=[pl.BlockSpec(memory_space=pltpu.VMEM)],
        out_specs=pl.BlockSpec(memory_space=pltpu.VMEM),
        scratch_shapes=[
            pltpu.VMEM((slices, rows, chunk), jnp.float32),
            pltpu.VMEM((rows, chunk), jnp.bfloat16),
            pltpu.VMEM((rows, chunk), jnp.bfloat16),
            pltpu.VMEM((tp_size, rows, chunk), jnp.bfloat16),
            pltpu.SemaphoreType.DMA((slices,)),
            pltpu.SemaphoreType.DMA((slices,)),
            pltpu.SemaphoreType.DMA((1,)),
            pltpu.SemaphoreType.DMA((1,)),
            pltpu.SemaphoreType.DMA((tp_size,)),
            pltpu.SemaphoreType.DMA((tp_size,)),
        ],
        compiler_params=pltpu.CompilerParams(has_side_effects=True),
    )(part)


def body(
    hidden_in,
    new_query,
    new_key,
    new_value,
    key_cache,
    value_cache,
    lengths,
    out_weight,
    norm_gain,
    router_weight,
    expert_ids,
    gate_weight,
    up_weight,
    down_weight,
):
    req_dev, steps, width = hidden_in.shape
    block = key_cache.shape[1]
    head_size = width // HEADS
    scale = head_size ** (-0.5)
    seq_index = lax.axis_index("seq")
    tp_index = lax.axis_index("tp")
    seq_size = lax.axis_size("seq")
    tp_size = lax.axis_size("tp")
    rows = steps * HEADS

    head_mask = (jnp.arange(width) // head_size)[None, :] == jnp.arange(HEADS)[:, None]
    q_wide = jnp.where(head_mask[None, None], new_query[:, :, None, :], 0).reshape(
        req_dev, rows, width
    )
    with jax.named_scope("cache_scores"):
        scores = (
            jnp.einsum("rqd,rpd->rqp", q_wide, key_cache, preferred_element_type=jnp.float32)
            * scale
        )
    positions = seq_index * block + jnp.arange(block, dtype=jnp.int32)
    usable = (positions[None, :] < lengths[:, None])[:, None, :]
    scores = jnp.where(usable, scores, masked_score)
    fresh_scores = (
        jnp.einsum("rqd,rsd->rqs", q_wide, new_key, preferred_element_type=jnp.float32) * scale
    )
    causal = (
        (jnp.arange(rows)[:, None] // HEADS) >= jnp.arange(steps)[None, :]
    ) & (seq_index == 0)
    fresh_scores = jnp.where(causal, fresh_scores, masked_score)
    local_max = jnp.maximum(jnp.max(scores, axis=2), jnp.max(fresh_scores, axis=2))
    weights = jnp.where(usable, jnp.exp(scores - local_max[..., None]), 0.0)
    fresh_weights = jnp.where(causal, jnp.exp(fresh_scores - local_max[..., None]), 0.0)
    totals = jnp.sum(weights, axis=2) + jnp.sum(fresh_weights, axis=2)
    with jax.named_scope("cache_values"):
        wide_values = jnp.einsum(
            "rqp,rpd->rqd",
            weights.astype(jnp.bfloat16),
            value_cache,
            preferred_element_type=jnp.float32,
        )
    wide_values = wide_values + jnp.einsum(
        "rqs,rsd->rqd",
        fresh_weights.astype(jnp.bfloat16),
        new_value,
        preferred_element_type=jnp.float32,
    )
    partial = jnp.sum(
        jnp.where(head_mask[None, None], wide_values.reshape(req_dev, steps, HEADS, width), 0.0),
        axis=2,
    )
    stats = jnp.concatenate(
        [
            partial,
            local_max.reshape(req_dev, steps, HEADS),
            totals.reshape(req_dev, steps, HEADS),
        ],
        axis=2,
    )
    every = gather_axis(stats.reshape(req_dev * steps, -1), "seq", seq_size).reshape(
        (seq_size,) + stats.shape
    )
    block_sums = every[..., :width]
    block_max = every[..., width : width + HEADS]
    block_totals = every[..., width + HEADS :]
    overall = jnp.max(block_max, axis=0)
    factors = jnp.exp(block_max - overall[None])
    numer = jnp.sum(jnp.repeat(factors, head_size, axis=-1) * block_sums, axis=0)
    denom = jnp.sum(factors * block_totals, axis=0)
    context = (numer / jnp.repeat(denom, head_size, axis=-1)).astype(jnp.bfloat16)
    attention = jnp.einsum("rtd,de->rte", context, out_weight, preferred_element_type=jnp.float32)
    feature_block = width // seq_size
    attn_out = lax.dynamic_slice_in_dim(
        attention, seq_index * feature_block, feature_block, 2
    ).astype(jnp.bfloat16)
    residual = hidden_in.astype(jnp.float32) + attention
    normed = (
        residual
        * lax.rsqrt(jnp.mean(residual * residual, axis=-1, keepdims=True) + norm_epsilon)
        * norm_gain
    ).astype(jnp.bfloat16)
    experts = router_weight.shape[1]
    topk = expert_ids.shape[2]
    requests = req_dev * tp_size
    capacity = (5 * requests * topk + 4 * experts - 1) // (4 * experts)
    expert_range = jnp.arange(experts, dtype=jnp.int32)
    packed = jnp.concatenate([normed, expert_ids.astype(jnp.bfloat16)], axis=2)
    all_packed = gather_axis(packed.reshape(req_dev * steps, -1), "tp", tp_size).reshape(
        requests, steps, -1
    )
    all_normed = all_packed[:, :, :width]
    all_ids = all_packed[:, :, width:].astype(jnp.int32)
    onehot = all_ids[..., None] == expert_range
    hits = jnp.sum(onehot.astype(jnp.int32), axis=2)
    earlier = jnp.cumsum(hits, axis=0) - hits
    all_slots = jnp.sum(jnp.where(onehot, earlier[:, :, None, :], 0), axis=3)
    logits = jnp.einsum(
        "rtd,de->rte", all_normed, router_weight, preferred_element_type=jnp.float32
    )
    chosen = jnp.sum(jnp.where(onehot, logits[:, :, None, :], 0.0), axis=3)
    share = 1.0 / (1.0 + jnp.exp(chosen[:, :, ::-1] - chosen))
    slices = seq_size * tp_size // experts
    mine = (seq_index * tp_size + tp_index) // slices
    match = all_ids == mine
    slot_mine = jnp.sum(jnp.where(match, all_slots, 0), axis=2)
    share_mine = jnp.sum(jnp.where(match, share, 0.0), axis=2)
    kept = jnp.any(match, axis=2) & (slot_mine < capacity)
    select = kept[None] & (slot_mine[None] == jnp.arange(capacity, dtype=jnp.int32)[:, None, None])
    buffer = (
        jnp.einsum(
            "crt,rtd->tcd",
            select.astype(jnp.bfloat16),
            all_normed,
            preferred_element_type=jnp.float32,
        )
        .astype(jnp.bfloat16)
        .reshape(steps * capacity, width)
    )
    contract = (((1,), (1,)), ((), ()))
    gate = lax.dot_general(buffer, gate_weight, contract, preferred_element_type=jnp.float32)
    upward = lax.dot_general(buffer, up_weight, contract, preferred_element_type=jnp.float32)
    inner = (jax.nn.gelu(gate) * upward).astype(jnp.bfloat16)
    produced = jnp.dot(inner, down_weight, preferred_element_type=jnp.float32)
    groups = tp_size // slices
    padded = 8 * ((steps * capacity + 7) // 8)
    part = jnp.pad(produced, ((0, padded - steps * capacity), (0, 0)))
    gathered = combine_rows(part, seq_size, tp_size, slices)
    halves = slices // seq_size
    gathered = gathered.astype(jnp.float32).reshape(groups, tp_size // (groups * halves), halves, padded, width // slices)
    own_slots = lax.dynamic_slice_in_dim(all_slots, tp_index * req_dev, req_dev, 0)
    own_share = lax.dynamic_slice_in_dim(share, tp_index * req_dev, req_dev, 0)
    weight = jnp.where(own_slots < capacity, own_share, 0.0)
    row_of = jnp.arange(steps, dtype=jnp.int32)[None, :, None] * capacity + own_slots
    hit = (
        (expert_ids[..., None, None, None] % groups == jnp.arange(groups)[:, None, None])
        & (expert_ids[..., None, None, None] // groups == jnp.arange(tp_size // (groups * halves))[None, :, None])
        & (row_of[..., None, None, None] == jnp.arange(padded)[None, None, :])
    )
    pick = jnp.sum(jnp.where(hit, weight[..., None, None, None], 0.0), axis=2)
    mixture = jnp.einsum(
        "rtzyp,zyhpf->rthf", pick, gathered, precision=lax.Precision.HIGHEST
    ).reshape(req_dev, steps, feature_block)
    own_residual = lax.dynamic_slice_in_dim(residual, seq_index * feature_block, feature_block, 2)
    layer_out = (own_residual + mixture).astype(jnp.bfloat16)
    return (attn_out, layer_out)


def solution(mesh):
    return jax.shard_map(
        body,
        mesh=mesh,
        in_specs=(
            P("tp", None, None),
            P("tp", None, None),
            P("tp", None, None),
            P("tp", None, None),
            P("tp", "seq", None),
            P("tp", "seq", None),
            P("tp"),
            P(),
            P(),
            P(),
            P("tp", None, None),
            P(("seq", "tp"), None),
            P(("seq", "tp"), None),
            P(("seq", "tp"), None),
        ),
        out_specs=(P("tp", None, "seq"), P("tp", None, "seq")),
        check_vma=False,
    )
```

```python
import functools

import jax
import jax.numpy as jnp
from jax import lax
from jax.experimental import pallas as pl
from jax.experimental.pallas import tpu as pltpu
from jax.sharding import PartitionSpec as P

HEADS = 16


masked_score = -1e30
norm_epsilon = 1e-06


def combine_kernel(seq_size, tp_size, slices, part_ref, out_ref, recv, summed, middle, landing,
                   send1, recv1, send2, recv2, send3, recv3):
    mesh_type = pl.DeviceIdType.MESH
    s = lax.axis_index("seq")
    t = lax.axis_index("tp")
    g = t // slices
    j = t % slices
    chunk = recv.shape[2]
    halves = slices // seq_size
    dest_seq = j // halves
    half = j % halves
    dest_t = g * slices + s * halves + half
    to_self = dest_seq == s

    barrier = pltpu.get_barrier_semaphore()
    for u in range(tp_size):
        @pl.when(t != u)
        def _():
            pl.semaphore_signal(barrier, inc=1, device_id=(s, u), device_id_type=mesh_type)

    @pl.when(to_self)
    def _():
        pl.semaphore_wait(barrier, tp_size - 1)

    @pl.when(jnp.logical_not(to_self))
    def _():
        pl.semaphore_signal(
            barrier, inc=1, device_id=(dest_seq, dest_t), device_id_type=mesh_type
        )
        pl.semaphore_wait(barrier, tp_size)

    def stage1(i):
        return pltpu.make_async_remote_copy(
            part_ref.at[:, pl.ds(i * chunk, chunk)],
            recv.at[j],
            send1.at[i],
            recv1.at[j],
            device_id=(s, g * slices + i),
            device_id_type=mesh_type,
        )

    def stage1_local(i):
        return pltpu.make_async_copy(part_ref.at[:, pl.ds(i * chunk, chunk)], recv.at[i], recv1.at[i])

    for i in range(slices):
        @pl.when(j == i)
        def _():
            stage1_local(i).start()

        @pl.when(j != i)
        def _():
            stage1(i).start()

    for i in range(slices):
        @pl.when(j == i)
        def _():
            stage1_local(i).wait()

        @pl.when(j != i)
        def _():
            stage1(i).wait_send()
            pltpu.make_async_remote_copy(
                part_ref.at[:, pl.ds(0, chunk)],
                recv.at[i],
                send1.at[i],
                recv1.at[i],
                device_id=(s, g * slices + i),
                device_id_type=mesh_type,
            ).wait_recv()

    total = recv[0]
    for i in range(1, slices):
        total = total + recv[i]
    summed[...] = total.astype(summed.dtype)


    @pl.when(to_self)
    def _():
        pltpu.make_async_copy(summed, middle, recv2.at[0]).start()
        pltpu.make_async_copy(summed, middle, recv2.at[0]).wait()

    @pl.when(jnp.logical_not(to_self))
    def _():
        copy = pltpu.make_async_remote_copy(
            summed, middle, send2.at[0], recv2.at[0],
            device_id=(dest_seq, dest_t), device_id_type=mesh_type,
        )
        copy.start()
        copy.wait_send()

    src_seq = (t % slices) // halves
    src_t = g * slices + s * halves + t % halves
    from_self = src_seq == s

    @pl.when(jnp.logical_not(from_self))
    def _():
        pltpu.make_async_remote_copy(
            summed, middle, send2.at[0], recv2.at[0],
            device_id=(src_seq, src_t), device_id_type=mesh_type,
        ).wait_recv()

    def stage3(u):
        return pltpu.make_async_remote_copy(
            middle, landing.at[t], send3.at[u], recv3.at[t],
            device_id=(s, u), device_id_type=mesh_type,
        )

    for u in range(tp_size):
        @pl.when(t == u)
        def _():
            pltpu.make_async_copy(middle, landing.at[u], recv3.at[u]).start()

        @pl.when(t != u)
        def _():
            stage3(u).start()

    for u in range(tp_size):
        @pl.when(t == u)
        def _():
            pltpu.make_async_copy(middle, landing.at[u], recv3.at[u]).wait()

        @pl.when(t != u)
        def _():
            stage3(u).wait_send()
            pltpu.make_async_remote_copy(
                middle, landing.at[u], send3.at[u], recv3.at[u],
                device_id=(s, u), device_id_type=mesh_type,
            ).wait_recv()

    out_ref[...] = landing[...]


def gather_kernel(axis, size, piece_ref, out_ref, landing, send, recv):
    mesh_type = pl.DeviceIdType.MESH
    me = lax.axis_index(axis)
    other = lax.axis_index("tp" if axis == "seq" else "seq")

    def peer(u):
        return (u, other) if axis == "seq" else (other, u)

    def remote(u, slot):
        return pltpu.make_async_remote_copy(
            piece_ref, landing.at[slot], send.at[u], recv.at[slot],
            device_id=peer(u), device_id_type=mesh_type,
        )

    barrier = pltpu.get_barrier_semaphore()
    for u in range(size):
        @pl.when(me != u)
        def _():
            pl.semaphore_signal(barrier, inc=1, device_id=peer(u), device_id_type=mesh_type)
    pl.semaphore_wait(barrier, size - 1)

    for u in range(size):
        @pl.when(me == u)
        def _():
            pltpu.make_async_copy(piece_ref, landing.at[u], recv.at[u]).start()

        @pl.when(me != u)
        def _():
            remote(u, me).start()

    for u in range(size):
        @pl.when(me == u)
        def _():
            pltpu.make_async_copy(piece_ref, landing.at[u], recv.at[u]).wait()

        @pl.when(me != u)
        def _():
            remote(u, me).wait_send()
            remote(u, u).wait_recv()

    out_ref[...] = landing[...]


def gather_axis(piece, axis, size, key):
    return pl.pallas_call(
        functools.partial(gather_kernel, axis, size),
        out_shape=jax.ShapeDtypeStruct((size,) + piece.shape, piece.dtype),
        in_specs=[pl.BlockSpec(memory_space=pltpu.VMEM)],
        out_specs=pl.BlockSpec(memory_space=pltpu.VMEM),
        scratch_shapes=[
            pltpu.VMEM((size,) + piece.shape, piece.dtype),
            pltpu.SemaphoreType.DMA((size,)),
            pltpu.SemaphoreType.DMA((size,)),
        ],
        compiler_params=pltpu.CompilerParams(collective_id=key, has_side_effects=True),
    )(piece)


def combine_rows(part, seq_size, tp_size, slices):
    rows, width = part.shape
    chunk = width // slices
    return pl.pallas_call(
        functools.partial(combine_kernel, seq_size, tp_size, slices),
        out_shape=jax.ShapeDtypeStruct((tp_size, rows, chunk), jnp.bfloat16),
        in_specs=[pl.BlockSpec(memory_space=pltpu.VMEM)],
        out_specs=pl.BlockSpec(memory_space=pltpu.VMEM),
        scratch_shapes=[
            pltpu.VMEM((slices, rows, chunk), jnp.float32),
            pltpu.VMEM((rows, chunk), jnp.bfloat16),
            pltpu.VMEM((rows, chunk), jnp.bfloat16),
            pltpu.VMEM((tp_size, rows, chunk), jnp.bfloat16),
            pltpu.SemaphoreType.DMA((slices,)),
            pltpu.SemaphoreType.DMA((slices,)),
            pltpu.SemaphoreType.DMA((1,)),
            pltpu.SemaphoreType.DMA((1,)),
            pltpu.SemaphoreType.DMA((tp_size,)),
            pltpu.SemaphoreType.DMA((tp_size,)),
        ],
        compiler_params=pltpu.CompilerParams(collective_id=2, has_side_effects=True),
    )(part)


def body(
    hidden_in,
    new_query,
    new_key,
    new_value,
    key_cache,
    value_cache,
    lengths,
    out_weight,
    norm_gain,
    router_weight,
    expert_ids,
    gate_weight,
    up_weight,
    down_weight,
):
    req_dev, steps, width = hidden_in.shape
    block = key_cache.shape[1]
    head_size = width // HEADS
    scale = head_size ** (-0.5)
    seq_index = lax.axis_index("seq")
    tp_index = lax.axis_index("tp")
    seq_size = lax.axis_size("seq")
    tp_size = lax.axis_size("tp")
    rows = steps * HEADS

    head_mask = (jnp.arange(width) // head_size)[None, :] == jnp.arange(HEADS)[:, None]
    q_wide = jnp.where(head_mask[None, None], new_query[:, :, None, :], 0).reshape(
        req_dev, rows, width
    )
    with jax.named_scope("cache_scores"):
        scores = (
            jnp.einsum("rqd,rpd->rqp", q_wide, key_cache, preferred_element_type=jnp.float32)
            * scale
        )
    positions = seq_index * block + jnp.arange(block, dtype=jnp.int32)
    usable = (positions[None, :] < lengths[:, None])[:, None, :]
    scores = jnp.where(usable, scores, masked_score)
    fresh_scores = (
        jnp.einsum("rqd,rsd->rqs", q_wide, new_key, preferred_element_type=jnp.float32) * scale
    )
    causal = (
        (jnp.arange(rows)[:, None] // HEADS) >= jnp.arange(steps)[None, :]
    ) & (seq_index == 0)
    fresh_scores = jnp.where(causal, fresh_scores, masked_score)
    local_max = jnp.maximum(jnp.max(scores, axis=2), jnp.max(fresh_scores, axis=2))
    weights = jnp.where(usable, jnp.exp(scores - local_max[..., None]), 0.0)
    fresh_weights = jnp.where(causal, jnp.exp(fresh_scores - local_max[..., None]), 0.0)
    totals = jnp.sum(weights, axis=2) + jnp.sum(fresh_weights, axis=2)
    with jax.named_scope("cache_values"):
        wide_values = jnp.einsum(
            "rqp,rpd->rqd",
            weights.astype(jnp.bfloat16),
            value_cache,
            preferred_element_type=jnp.float32,
        )
    wide_values = wide_values + jnp.einsum(
        "rqs,rsd->rqd",
        fresh_weights.astype(jnp.bfloat16),
        new_value,
        preferred_element_type=jnp.float32,
    )
    partial = jnp.sum(
        jnp.where(head_mask[None, None], wide_values.reshape(req_dev, steps, HEADS, width), 0.0),
        axis=2,
    )
    stats = jnp.concatenate(
        [
            partial,
            local_max.reshape(req_dev, steps, HEADS),
            totals.reshape(req_dev, steps, HEADS),
        ],
        axis=2,
    )
    every = gather_axis(stats.reshape(req_dev * steps, -1), "seq", seq_size, 0).reshape(
        (seq_size,) + stats.shape
    )
    block_sums = every[..., :width]
    block_max = every[..., width : width + HEADS]
    block_totals = every[..., width + HEADS :]
    overall = jnp.max(block_max, axis=0)
    factors = jnp.exp(block_max - overall[None])
    numer = jnp.sum(jnp.repeat(factors, head_size, axis=-1) * block_sums, axis=0)
    denom = jnp.sum(factors * block_totals, axis=0)
    context = (numer / jnp.repeat(denom, head_size, axis=-1)).astype(jnp.bfloat16)
    attention = jnp.einsum("rtd,de->rte", context, out_weight, preferred_element_type=jnp.float32)
    feature_block = width // seq_size
    attn_out = lax.dynamic_slice_in_dim(
        attention, seq_index * feature_block, feature_block, 2
    ).astype(jnp.bfloat16)
    residual = hidden_in.astype(jnp.float32) + attention
    normed = (
        residual
        * lax.rsqrt(jnp.mean(residual * residual, axis=-1, keepdims=True) + norm_epsilon)
        * norm_gain
    ).astype(jnp.bfloat16)
    experts = router_weight.shape[1]
    topk = expert_ids.shape[2]
    requests = req_dev * tp_size
    capacity = (5 * requests * topk + 4 * experts - 1) // (4 * experts)
    expert_range = jnp.arange(experts, dtype=jnp.int32)
    packed = jnp.concatenate([normed, expert_ids.astype(jnp.bfloat16)], axis=2)
    all_packed = gather_axis(packed.reshape(req_dev * steps, -1), "tp", tp_size, 1).reshape(
        requests, steps, -1
    )
    all_normed = all_packed[:, :, :width]
    all_ids = all_packed[:, :, width:].astype(jnp.int32)
    onehot = all_ids[..., None] == expert_range
    hits = jnp.sum(onehot.astype(jnp.int32), axis=2)
    earlier = jnp.cumsum(hits, axis=0) - hits
    all_slots = jnp.sum(jnp.where(onehot, earlier[:, :, None, :], 0), axis=3)
    logits = jnp.einsum(
        "rtd,de->rte", all_normed, router_weight, preferred_element_type=jnp.float32
    )
    chosen = jnp.sum(jnp.where(onehot, logits[:, :, None, :], 0.0), axis=3)
    share = 1.0 / (1.0 + jnp.exp(chosen[:, :, ::-1] - chosen))
    slices = seq_size * tp_size // experts
    mine = (seq_index * tp_size + tp_index) // slices
    match = all_ids == mine
    slot_mine = jnp.sum(jnp.where(match, all_slots, 0), axis=2)
    share_mine = jnp.sum(jnp.where(match, share, 0.0), axis=2)
    kept = jnp.any(match, axis=2) & (slot_mine < capacity)
    select = kept[None] & (slot_mine[None] == jnp.arange(capacity, dtype=jnp.int32)[:, None, None])
    buffer = (
        jnp.einsum(
            "crt,rtd->tcd",
            select.astype(jnp.bfloat16),
            all_normed,
            preferred_element_type=jnp.float32,
        )
        .astype(jnp.bfloat16)
        .reshape(steps * capacity, width)
    )
    contract = (((1,), (1,)), ((), ()))
    gate = lax.dot_general(buffer, gate_weight, contract, preferred_element_type=jnp.float32)
    upward = lax.dot_general(buffer, up_weight, contract, preferred_element_type=jnp.float32)
    inner = (jax.nn.gelu(gate) * upward).astype(jnp.bfloat16)
    produced = jnp.dot(inner, down_weight, preferred_element_type=jnp.float32)
    groups = tp_size // slices
    padded = 8 * ((steps * capacity + 7) // 8)
    part = jnp.pad(produced, ((0, padded - steps * capacity), (0, 0)))
    gathered = combine_rows(part, seq_size, tp_size, slices)
    halves = slices // seq_size
    gathered = gathered.astype(jnp.float32).reshape(groups, tp_size // (groups * halves), halves, padded, width // slices)
    own_slots = lax.dynamic_slice_in_dim(all_slots, tp_index * req_dev, req_dev, 0)
    own_share = lax.dynamic_slice_in_dim(share, tp_index * req_dev, req_dev, 0)
    weight = jnp.where(own_slots < capacity, own_share, 0.0)
    row_of = jnp.arange(steps, dtype=jnp.int32)[None, :, None] * capacity + own_slots
    hit = (
        (expert_ids[..., None, None, None] % groups == jnp.arange(groups)[:, None, None])
        & (expert_ids[..., None, None, None] // groups == jnp.arange(tp_size // (groups * halves))[None, :, None])
        & (row_of[..., None, None, None] == jnp.arange(padded)[None, None, :])
    )
    pick = jnp.sum(jnp.where(hit, weight[..., None, None, None], 0.0), axis=2)
    mixture = jnp.einsum(
        "rtzyp,zyhpf->rthf", pick, gathered, precision=lax.Precision.HIGHEST
    ).reshape(req_dev, steps, feature_block)
    own_residual = lax.dynamic_slice_in_dim(residual, seq_index * feature_block, feature_block, 2)
    layer_out = (own_residual + mixture).astype(jnp.bfloat16)
    return (attn_out, layer_out)


def solution(mesh):
    return jax.shard_map(
        body,
        mesh=mesh,
        in_specs=(
            P("tp", None, None),
            P("tp", None, None),
            P("tp", None, None),
            P("tp", None, None),
            P("tp", "seq", None),
            P("tp", "seq", None),
            P("tp"),
            P(),
            P(),
            P(),
            P("tp", None, None),
            P(("seq", "tp"), None),
            P(("seq", "tp"), None),
            P(("seq", "tp"), None),
        ),
        out_specs=(P("tp", None, "seq"), P("tp", None, "seq")),
        check_vma=False,
    )
```

```python
import functools

import jax
import jax.numpy as jnp
from jax import lax
from jax.experimental import pallas as pl
from jax.experimental.pallas import tpu as pltpu
from jax.sharding import PartitionSpec as P

HEADS = 16


masked_score = -1e30
norm_epsilon = 1e-06


def combine_kernel(seq_size, tp_size, slices, part_ref, select_ref, out_ref, recv, summed, middle,
                   outgoing, landing, send1, recv1, send2, recv2, send3, recv3):
    mesh_type = pl.DeviceIdType.MESH
    s = lax.axis_index("seq")
    t = lax.axis_index("tp")
    g = t // slices
    j = t % slices
    chunk = recv.shape[2]
    halves = slices // seq_size
    dest_seq = j // halves
    half = j % halves
    dest_t = g * slices + s * halves + half
    to_self = dest_seq == s

    barrier = pltpu.get_barrier_semaphore()
    for u in range(tp_size):
        @pl.when(t != u)
        def _():
            pl.semaphore_signal(barrier, inc=1, device_id=(s, u), device_id_type=mesh_type)

    @pl.when(to_self)
    def _():
        pl.semaphore_wait(barrier, tp_size - 1)

    @pl.when(jnp.logical_not(to_self))
    def _():
        pl.semaphore_signal(
            barrier, inc=1, device_id=(dest_seq, dest_t), device_id_type=mesh_type
        )
        pl.semaphore_wait(barrier, tp_size)

    def stage1(i):
        return pltpu.make_async_remote_copy(
            part_ref.at[:, pl.ds(i * chunk, chunk)],
            recv.at[j],
            send1.at[i],
            recv1.at[j],
            device_id=(s, g * slices + i),
            device_id_type=mesh_type,
        )

    def stage1_local(i):
        return pltpu.make_async_copy(part_ref.at[:, pl.ds(i * chunk, chunk)], recv.at[i], recv1.at[i])

    for i in range(slices):
        @pl.when(j == i)
        def _():
            stage1_local(i).start()

        @pl.when(j != i)
        def _():
            stage1(i).start()

    for i in range(slices):
        @pl.when(j == i)
        def _():
            stage1_local(i).wait()

        @pl.when(j != i)
        def _():
            stage1(i).wait_send()
            pltpu.make_async_remote_copy(
                part_ref.at[:, pl.ds(0, chunk)],
                recv.at[i],
                send1.at[i],
                recv1.at[i],
                device_id=(s, g * slices + i),
                device_id_type=mesh_type,
            ).wait_recv()

    total = recv[0]
    for i in range(1, slices):
        total = total + recv[i]
    summed[...] = total.astype(summed.dtype)


    @pl.when(to_self)
    def _():
        pltpu.make_async_copy(summed, middle, recv2.at[0]).start()
        pltpu.make_async_copy(summed, middle, recv2.at[0]).wait()

    @pl.when(jnp.logical_not(to_self))
    def _():
        copy = pltpu.make_async_remote_copy(
            summed, middle, send2.at[0], recv2.at[0],
            device_id=(dest_seq, dest_t), device_id_type=mesh_type,
        )
        copy.start()
        copy.wait_send()

    src_seq = (t % slices) // halves
    src_t = g * slices + s * halves + t % halves
    from_self = src_seq == s

    @pl.when(jnp.logical_not(from_self))
    def _():
        pltpu.make_async_remote_copy(
            summed, middle, send2.at[0], recv2.at[0],
            device_id=(src_seq, src_t), device_id_type=mesh_type,
        ).wait_recv()

    picked = jnp.dot(
        select_ref[...].reshape(-1, select_ref.shape[2]),
        middle[...].astype(jnp.float32),
        precision=lax.Precision.HIGHEST,
        preferred_element_type=jnp.float32,
    )
    outgoing[...] = picked.reshape(outgoing.shape).astype(outgoing.dtype)

    def stage3(u):
        return pltpu.make_async_remote_copy(
            outgoing.at[u], landing.at[t], send3.at[u], recv3.at[t],
            device_id=(s, u), device_id_type=mesh_type,
        )

    for u in range(tp_size):
        @pl.when(t == u)
        def _():
            pltpu.make_async_copy(outgoing.at[u], landing.at[u], recv3.at[u]).start()

        @pl.when(t != u)
        def _():
            stage3(u).start()

    for u in range(tp_size):
        @pl.when(t == u)
        def _():
            pltpu.make_async_copy(outgoing.at[u], landing.at[u], recv3.at[u]).wait()

        @pl.when(t != u)
        def _():
            stage3(u).wait_send()
            pltpu.make_async_remote_copy(
                outgoing.at[u], landing.at[u], send3.at[u], recv3.at[u],
                device_id=(s, u), device_id_type=mesh_type,
            ).wait_recv()

    out_ref[...] = landing[...]


def gather_kernel(axis, size, piece_ref, out_ref, landing, send, recv):
    mesh_type = pl.DeviceIdType.MESH
    me = lax.axis_index(axis)
    other = lax.axis_index("tp" if axis == "seq" else "seq")

    def peer(u):
        return (u, other) if axis == "seq" else (other, u)

    def remote(u, slot):
        return pltpu.make_async_remote_copy(
            piece_ref, landing.at[slot], send.at[u], recv.at[slot],
            device_id=peer(u), device_id_type=mesh_type,
        )

    barrier = pltpu.get_barrier_semaphore()
    for u in range(size):
        @pl.when(me != u)
        def _():
            pl.semaphore_signal(barrier, inc=1, device_id=peer(u), device_id_type=mesh_type)
    pl.semaphore_wait(barrier, size - 1)

    for u in range(size):
        @pl.when(me == u)
        def _():
            pltpu.make_async_copy(piece_ref, landing.at[u], recv.at[u]).start()

        @pl.when(me != u)
        def _():
            remote(u, me).start()

    for u in range(size):
        @pl.when(me == u)
        def _():
            pltpu.make_async_copy(piece_ref, landing.at[u], recv.at[u]).wait()

        @pl.when(me != u)
        def _():
            remote(u, me).wait_send()
            remote(u, u).wait_recv()

    out_ref[...] = landing[...]


def gather_axis(piece, axis, size, key):
    return pl.pallas_call(
        functools.partial(gather_kernel, axis, size),
        out_shape=jax.ShapeDtypeStruct((size,) + piece.shape, piece.dtype),
        in_specs=[pl.BlockSpec(memory_space=pltpu.VMEM)],
        out_specs=pl.BlockSpec(memory_space=pltpu.VMEM),
        scratch_shapes=[
            pltpu.VMEM((size,) + piece.shape, piece.dtype),
            pltpu.SemaphoreType.DMA((size,)),
            pltpu.SemaphoreType.DMA((size,)),
        ],
        compiler_params=pltpu.CompilerParams(collective_id=key, has_side_effects=True),
    )(piece)


def combine_rows(part, select, seq_size, tp_size, slices):
    rows, width = part.shape
    chunk = width // slices
    tokens = select.shape[1]
    return pl.pallas_call(
        functools.partial(combine_kernel, seq_size, tp_size, slices),
        out_shape=jax.ShapeDtypeStruct((tp_size, tokens, chunk), jnp.bfloat16),
        in_specs=[pl.BlockSpec(memory_space=pltpu.VMEM)] * 2,
        out_specs=pl.BlockSpec(memory_space=pltpu.VMEM),
        scratch_shapes=[
            pltpu.VMEM((slices, rows, chunk), jnp.float32),
            pltpu.VMEM((rows, chunk), jnp.bfloat16),
            pltpu.VMEM((rows, chunk), jnp.bfloat16),
            pltpu.VMEM((tp_size, tokens, chunk), jnp.bfloat16),
            pltpu.VMEM((tp_size, tokens, chunk), jnp.bfloat16),
            pltpu.SemaphoreType.DMA((slices,)),
            pltpu.SemaphoreType.DMA((slices,)),
            pltpu.SemaphoreType.DMA((1,)),
            pltpu.SemaphoreType.DMA((1,)),
            pltpu.SemaphoreType.DMA((tp_size,)),
            pltpu.SemaphoreType.DMA((tp_size,)),
        ],
        compiler_params=pltpu.CompilerParams(collective_id=2, has_side_effects=True),
    )(part, select)


def body(
    hidden_in,
    new_query,
    new_key,
    new_value,
    key_cache,
    value_cache,
    lengths,
    out_weight,
    norm_gain,
    router_weight,
    expert_ids,
    gate_weight,
    up_weight,
    down_weight,
):
    req_dev, steps, width = hidden_in.shape
    block = key_cache.shape[1]
    head_size = width // HEADS
    scale = head_size ** (-0.5)
    seq_index = lax.axis_index("seq")
    tp_index = lax.axis_index("tp")
    seq_size = lax.axis_size("seq")
    tp_size = lax.axis_size("tp")
    rows = steps * HEADS

    head_mask = (jnp.arange(width) // head_size)[None, :] == jnp.arange(HEADS)[:, None]
    q_wide = jnp.where(head_mask[None, None], new_query[:, :, None, :], 0).reshape(
        req_dev, rows, width
    )
    with jax.named_scope("cache_scores"):
        scores = (
            jnp.einsum("rqd,rpd->rqp", q_wide, key_cache, preferred_element_type=jnp.float32)
            * scale
        )
    positions = seq_index * block + jnp.arange(block, dtype=jnp.int32)
    usable = (positions[None, :] < lengths[:, None])[:, None, :]
    scores = jnp.where(usable, scores, masked_score)
    fresh_scores = (
        jnp.einsum("rqd,rsd->rqs", q_wide, new_key, preferred_element_type=jnp.float32) * scale
    )
    causal = (
        (jnp.arange(rows)[:, None] // HEADS) >= jnp.arange(steps)[None, :]
    ) & (seq_index == 0)
    fresh_scores = jnp.where(causal, fresh_scores, masked_score)
    local_max = jnp.maximum(jnp.max(scores, axis=2), jnp.max(fresh_scores, axis=2))
    weights = jnp.where(usable, jnp.exp(scores - local_max[..., None]), 0.0)
    fresh_weights = jnp.where(causal, jnp.exp(fresh_scores - local_max[..., None]), 0.0)
    totals = jnp.sum(weights, axis=2) + jnp.sum(fresh_weights, axis=2)
    with jax.named_scope("cache_values"):
        wide_values = jnp.einsum(
            "rqp,rpd->rqd",
            weights.astype(jnp.bfloat16),
            value_cache,
            preferred_element_type=jnp.float32,
        )
    wide_values = wide_values + jnp.einsum(
        "rqs,rsd->rqd",
        fresh_weights.astype(jnp.bfloat16),
        new_value,
        preferred_element_type=jnp.float32,
    )
    partial = jnp.sum(
        jnp.where(head_mask[None, None], wide_values.reshape(req_dev, steps, HEADS, width), 0.0),
        axis=2,
    )
    stats = jnp.concatenate(
        [
            partial,
            local_max.reshape(req_dev, steps, HEADS),
            totals.reshape(req_dev, steps, HEADS),
        ],
        axis=2,
    )
    every = gather_axis(stats.reshape(req_dev * steps, -1), "seq", seq_size, 0).reshape(
        (seq_size,) + stats.shape
    )
    block_sums = every[..., :width]
    block_max = every[..., width : width + HEADS]
    block_totals = every[..., width + HEADS :]
    overall = jnp.max(block_max, axis=0)
    factors = jnp.exp(block_max - overall[None])
    numer = jnp.sum(jnp.repeat(factors, head_size, axis=-1) * block_sums, axis=0)
    denom = jnp.sum(factors * block_totals, axis=0)
    context = (numer / jnp.repeat(denom, head_size, axis=-1)).astype(jnp.bfloat16)
    attention = jnp.einsum("rtd,de->rte", context, out_weight, preferred_element_type=jnp.float32)
    feature_block = width // seq_size
    attn_out = lax.dynamic_slice_in_dim(
        attention, seq_index * feature_block, feature_block, 2
    ).astype(jnp.bfloat16)
    residual = hidden_in.astype(jnp.float32) + attention
    normed = (
        residual
        * lax.rsqrt(jnp.mean(residual * residual, axis=-1, keepdims=True) + norm_epsilon)
        * norm_gain
    ).astype(jnp.bfloat16)
    experts = router_weight.shape[1]
    topk = expert_ids.shape[2]
    requests = req_dev * tp_size
    capacity = (5 * requests * topk + 4 * experts - 1) // (4 * experts)
    expert_range = jnp.arange(experts, dtype=jnp.int32)
    packed = jnp.concatenate([normed, expert_ids.astype(jnp.bfloat16)], axis=2)
    all_packed = gather_axis(packed.reshape(req_dev * steps, -1), "tp", tp_size, 1).reshape(
        requests, steps, -1
    )
    all_normed = all_packed[:, :, :width]
    all_ids = all_packed[:, :, width:].astype(jnp.int32)
    onehot = all_ids[..., None] == expert_range
    hits = jnp.sum(onehot.astype(jnp.int32), axis=2)
    earlier = jnp.cumsum(hits, axis=0) - hits
    all_slots = jnp.sum(jnp.where(onehot, earlier[:, :, None, :], 0), axis=3)
    logits = jnp.einsum(
        "rtd,de->rte", all_normed, router_weight, preferred_element_type=jnp.float32
    )
    chosen = jnp.sum(jnp.where(onehot, logits[:, :, None, :], 0.0), axis=3)
    share = 1.0 / (1.0 + jnp.exp(chosen[:, :, ::-1] - chosen))
    slices = seq_size * tp_size // experts
    mine = (seq_index * tp_size + tp_index) // slices
    match = all_ids == mine
    slot_mine = jnp.sum(jnp.where(match, all_slots, 0), axis=2)
    share_mine = jnp.sum(jnp.where(match, share, 0.0), axis=2)
    kept = jnp.any(match, axis=2) & (slot_mine < capacity)
    select = kept[None] & (slot_mine[None] == jnp.arange(capacity, dtype=jnp.int32)[:, None, None])
    buffer = (
        jnp.einsum(
            "crt,rtd->tcd",
            select.astype(jnp.bfloat16),
            all_normed,
            preferred_element_type=jnp.float32,
        )
        .astype(jnp.bfloat16)
        .reshape(steps * capacity, width)
    )
    contract = (((1,), (1,)), ((), ()))
    gate = lax.dot_general(buffer, gate_weight, contract, preferred_element_type=jnp.float32)
    upward = lax.dot_general(buffer, up_weight, contract, preferred_element_type=jnp.float32)
    inner = (jax.nn.gelu(gate) * upward).astype(jnp.bfloat16)
    produced = jnp.dot(inner, down_weight, preferred_element_type=jnp.float32)
    groups = tp_size // slices
    padded = 8 * ((steps * capacity + 7) // 8)
    part = jnp.pad(produced, ((0, padded - steps * capacity), (0, 0)))
    halves = slices // seq_size
    held = ((tp_index % slices) // halves) * groups + tp_index // slices
    held_match = (all_ids == held) & (all_slots < capacity)
    held_row = jnp.arange(steps, dtype=jnp.int32)[None, :, None] * capacity + all_slots
    select_rows = jnp.sum(
        jnp.where(
            held_match[..., None] & (held_row[..., None] == jnp.arange(padded)),
            share[..., None],
            0.0,
        ),
        axis=2,
    ).reshape(tp_size, req_dev * steps, padded)
    tokens = 16 * ((req_dev * steps + 15) // 16)
    select_rows = jnp.pad(select_rows, ((0, 0), (0, tokens - req_dev * steps), (0, 0)))
    landed = combine_rows(part, select_rows, seq_size, tp_size, slices)
    landed = landed.astype(jnp.float32).reshape(tp_size // halves, halves, tokens, width // slices)
    mixture = (
        jnp.sum(landed, axis=0)[:, : req_dev * steps]
        .transpose(1, 0, 2)
        .reshape(req_dev, steps, feature_block)
    )
    own_residual = lax.dynamic_slice_in_dim(residual, seq_index * feature_block, feature_block, 2)
    layer_out = (own_residual + mixture).astype(jnp.bfloat16)
    return (attn_out, layer_out)


def solution(mesh):
    return jax.shard_map(
        body,
        mesh=mesh,
        in_specs=(
            P("tp", None, None),
            P("tp", None, None),
            P("tp", None, None),
            P("tp", None, None),
            P("tp", "seq", None),
            P("tp", "seq", None),
            P("tp"),
            P(),
            P(),
            P(),
            P("tp", None, None),
            P(("seq", "tp"), None),
            P(("seq", "tp"), None),
            P(("seq", "tp"), None),
        ),
        out_specs=(P("tp", None, "seq"), P("tp", None, "seq")),
        check_vma=False,
    )
```

```python
import functools

import jax
import jax.numpy as jnp
from jax import lax
from jax.experimental import pallas as pl
from jax.experimental.pallas import tpu as pltpu
from jax.sharding import PartitionSpec as P

HEADS = 16


masked_score = -1e30
norm_epsilon = 1e-06


def combine_kernel(seq_size, tp_size, slices, part_ref, select_ref, out_ref, recv, middle,
                   outgoing, landing, send1, recv1, send3, recv3):
    mesh_type = pl.DeviceIdType.MESH
    s = lax.axis_index("seq")
    t = lax.axis_index("tp")
    g = t // slices
    j = t % slices
    chunk = recv.shape[2]
    halves = slices // seq_size
    src_seq = j // halves

    def dest(i):
        return (i // halves, g * slices + s * halves + i % halves)

    def is_self(i):
        return (i // halves == s) & (g * slices + s * halves + i % halves == t)

    barrier = pltpu.get_barrier_semaphore()
    for u in range(tp_size):
        @pl.when(t != u)
        def _():
            pl.semaphore_signal(barrier, inc=1, device_id=(s, u), device_id_type=mesh_type)
    for i in range(slices):
        @pl.when(i // halves != s)
        def _():
            pl.semaphore_signal(barrier, inc=1, device_id=dest(i), device_id_type=mesh_type)
    for k in range(slices):
        @pl.when((src_seq != s) & (k // halves != s))
        def _():
            pl.semaphore_signal(
                barrier, inc=1, device_id=(src_seq, g * slices + k), device_id_type=mesh_type
            )
    far = (seq_size - 1) * halves
    near = tp_size - 1 + far

    @pl.when(src_seq == s)
    def _():
        pl.semaphore_wait(barrier, near)

    @pl.when(src_seq != s)
    def _():
        pl.semaphore_wait(barrier, near + slices - halves)

    def stage1(i):
        return pltpu.make_async_remote_copy(
            part_ref.at[:, pl.ds(i * chunk, chunk)],
            recv.at[j],
            send1.at[i],
            recv1.at[j],
            device_id=dest(i),
            device_id_type=mesh_type,
        )

    for i in range(slices):
        @pl.when(is_self(i))
        def _():
            pltpu.make_async_copy(
                part_ref.at[:, pl.ds(i * chunk, chunk)], recv.at[j], recv1.at[j]
            ).start()

        @pl.when(jnp.logical_not(is_self(i)))
        def _():
            stage1(i).start()

    for i in range(slices):
        @pl.when(jnp.logical_not(is_self(i)))
        def _():
            stage1(i).wait_send()

    for k in range(slices):
        from_self = (src_seq == s) & (k == j)

        @pl.when(from_self)
        def _():
            pltpu.make_async_copy(
                part_ref.at[:, pl.ds(0, chunk)], recv.at[k], recv1.at[k]
            ).wait()

        @pl.when(jnp.logical_not(from_self))
        def _():
            pltpu.make_async_remote_copy(
                part_ref.at[:, pl.ds(0, chunk)],
                recv.at[k],
                send1.at[0],
                recv1.at[k],
                device_id=(src_seq, g * slices + k),
                device_id_type=mesh_type,
            ).wait_recv()

    total = recv[0]
    for k in range(1, slices):
        total = total + recv[k]
    middle[...] = total.astype(middle.dtype)

    picked = jnp.dot(
        select_ref[...].reshape(-1, select_ref.shape[2]),
        middle[...],
        precision=lax.Precision.HIGHEST,
        preferred_element_type=jnp.float32,
    )
    outgoing[...] = picked.reshape(outgoing.shape).astype(outgoing.dtype)

    def stage3(u):
        return pltpu.make_async_remote_copy(
            outgoing.at[u], landing.at[t], send3.at[u], recv3.at[t],
            device_id=(s, u), device_id_type=mesh_type,
        )

    for u in range(tp_size):
        @pl.when(t == u)
        def _():
            pltpu.make_async_copy(outgoing.at[u], landing.at[u], recv3.at[u]).start()

        @pl.when(t != u)
        def _():
            stage3(u).start()

    for u in range(tp_size):
        @pl.when(t == u)
        def _():
            pltpu.make_async_copy(outgoing.at[u], landing.at[u], recv3.at[u]).wait()

        @pl.when(t != u)
        def _():
            stage3(u).wait_send()
            pltpu.make_async_remote_copy(
                outgoing.at[u], landing.at[u], send3.at[u], recv3.at[u],
                device_id=(s, u), device_id_type=mesh_type,
            ).wait_recv()

    out_ref[...] = landing[...]


def gather_kernel(axis, size, piece_ref, out_ref, landing, send, recv):
    mesh_type = pl.DeviceIdType.MESH
    me = lax.axis_index(axis)
    other = lax.axis_index("tp" if axis == "seq" else "seq")

    def peer(u):
        return (u, other) if axis == "seq" else (other, u)

    def remote(u, slot):
        return pltpu.make_async_remote_copy(
            piece_ref, landing.at[slot], send.at[u], recv.at[slot],
            device_id=peer(u), device_id_type=mesh_type,
        )

    barrier = pltpu.get_barrier_semaphore()
    for u in range(size):
        @pl.when(me != u)
        def _():
            pl.semaphore_signal(barrier, inc=1, device_id=peer(u), device_id_type=mesh_type)
    pl.semaphore_wait(barrier, size - 1)

    for u in range(size):
        @pl.when(me == u)
        def _():
            pltpu.make_async_copy(piece_ref, landing.at[u], recv.at[u]).start()

        @pl.when(me != u)
        def _():
            remote(u, me).start()

    for u in range(size):
        @pl.when(me == u)
        def _():
            pltpu.make_async_copy(piece_ref, landing.at[u], recv.at[u]).wait()

        @pl.when(me != u)
        def _():
            remote(u, me).wait_send()
            remote(u, u).wait_recv()

    out_ref[...] = landing[...]


def gather_axis(piece, axis, size, key):
    return pl.pallas_call(
        functools.partial(gather_kernel, axis, size),
        out_shape=jax.ShapeDtypeStruct((size,) + piece.shape, piece.dtype),
        in_specs=[pl.BlockSpec(memory_space=pltpu.VMEM)],
        out_specs=pl.BlockSpec(memory_space=pltpu.VMEM),
        scratch_shapes=[
            pltpu.VMEM((size,) + piece.shape, piece.dtype),
            pltpu.SemaphoreType.DMA((size,)),
            pltpu.SemaphoreType.DMA((size,)),
        ],
        compiler_params=pltpu.CompilerParams(collective_id=key, has_side_effects=True),
    )(piece)


def combine_rows(part, select, seq_size, tp_size, slices):
    rows, width = part.shape
    chunk = width // slices
    tokens = select.shape[1]
    return pl.pallas_call(
        functools.partial(combine_kernel, seq_size, tp_size, slices),
        out_shape=jax.ShapeDtypeStruct((tp_size, tokens, chunk), jnp.bfloat16),
        in_specs=[pl.BlockSpec(memory_space=pltpu.VMEM)] * 2,
        out_specs=pl.BlockSpec(memory_space=pltpu.VMEM),
        scratch_shapes=[
            pltpu.VMEM((slices, rows, chunk), jnp.float32),
            pltpu.VMEM((rows, chunk), jnp.float32),
            pltpu.VMEM((tp_size, tokens, chunk), jnp.bfloat16),
            pltpu.VMEM((tp_size, tokens, chunk), jnp.bfloat16),
            pltpu.SemaphoreType.DMA((slices,)),
            pltpu.SemaphoreType.DMA((slices,)),
            pltpu.SemaphoreType.DMA((tp_size,)),
            pltpu.SemaphoreType.DMA((tp_size,)),
        ],
        compiler_params=pltpu.CompilerParams(collective_id=2, has_side_effects=True),
    )(part, select)


def body(
    hidden_in,
    new_query,
    new_key,
    new_value,
    key_cache,
    value_cache,
    lengths,
    out_weight,
    norm_gain,
    router_weight,
    expert_ids,
    gate_weight,
    up_weight,
    down_weight,
):
    req_dev, steps, width = hidden_in.shape
    block = key_cache.shape[1]
    head_size = width // HEADS
    scale = head_size ** (-0.5)
    seq_index = lax.axis_index("seq")
    tp_index = lax.axis_index("tp")
    seq_size = lax.axis_size("seq")
    tp_size = lax.axis_size("tp")
    rows = steps * HEADS

    head_mask = (jnp.arange(width) // head_size)[None, :] == jnp.arange(HEADS)[:, None]
    q_wide = jnp.where(head_mask[None, None], new_query[:, :, None, :], 0).reshape(
        req_dev, rows, width
    )
    with jax.named_scope("cache_scores"):
        scores = (
            jnp.einsum("rqd,rpd->rqp", q_wide, key_cache, preferred_element_type=jnp.float32)
            * scale
        )
    positions = seq_index * block + jnp.arange(block, dtype=jnp.int32)
    usable = (positions[None, :] < lengths[:, None])[:, None, :]
    scores = jnp.where(usable, scores, masked_score)
    fresh_scores = (
        jnp.einsum("rqd,rsd->rqs", q_wide, new_key, preferred_element_type=jnp.float32) * scale
    )
    causal = (
        (jnp.arange(rows)[:, None] // HEADS) >= jnp.arange(steps)[None, :]
    ) & (seq_index == 0)
    fresh_scores = jnp.where(causal, fresh_scores, masked_score)
    local_max = jnp.maximum(jnp.max(scores, axis=2), jnp.max(fresh_scores, axis=2))
    weights = jnp.where(usable, jnp.exp(scores - local_max[..., None]), 0.0)
    fresh_weights = jnp.where(causal, jnp.exp(fresh_scores - local_max[..., None]), 0.0)
    totals = jnp.sum(weights, axis=2) + jnp.sum(fresh_weights, axis=2)
    with jax.named_scope("cache_values"):
        wide_values = jnp.einsum(
            "rqp,rpd->rqd",
            weights.astype(jnp.bfloat16),
            value_cache,
            preferred_element_type=jnp.float32,
        )
    wide_values = wide_values + jnp.einsum(
        "rqs,rsd->rqd",
        fresh_weights.astype(jnp.bfloat16),
        new_value,
        preferred_element_type=jnp.float32,
    )
    partial = jnp.sum(
        jnp.where(head_mask[None, None], wide_values.reshape(req_dev, steps, HEADS, width), 0.0),
        axis=2,
    )
    stats = jnp.concatenate(
        [
            partial,
            local_max.reshape(req_dev, steps, HEADS),
            totals.reshape(req_dev, steps, HEADS),
        ],
        axis=2,
    )
    every = gather_axis(stats.reshape(req_dev * steps, -1), "seq", seq_size, 0).reshape(
        (seq_size,) + stats.shape
    )
    block_sums = every[..., :width]
    block_max = every[..., width : width + HEADS]
    block_totals = every[..., width + HEADS :]
    overall = jnp.max(block_max, axis=0)
    factors = jnp.exp(block_max - overall[None])
    numer = jnp.sum(jnp.repeat(factors, head_size, axis=-1) * block_sums, axis=0)
    denom = jnp.sum(factors * block_totals, axis=0)
    context = (numer / jnp.repeat(denom, head_size, axis=-1)).astype(jnp.bfloat16)
    attention = jnp.einsum("rtd,de->rte", context, out_weight, preferred_element_type=jnp.float32)
    feature_block = width // seq_size
    attn_out = lax.dynamic_slice_in_dim(
        attention, seq_index * feature_block, feature_block, 2
    ).astype(jnp.bfloat16)
    residual = hidden_in.astype(jnp.float32) + attention
    normed = (
        residual
        * lax.rsqrt(jnp.mean(residual * residual, axis=-1, keepdims=True) + norm_epsilon)
        * norm_gain
    ).astype(jnp.bfloat16)
    experts = router_weight.shape[1]
    topk = expert_ids.shape[2]
    requests = req_dev * tp_size
    capacity = (5 * requests * topk + 4 * experts - 1) // (4 * experts)
    expert_range = jnp.arange(experts, dtype=jnp.int32)
    packed = jnp.concatenate([normed, expert_ids.astype(jnp.bfloat16)], axis=2)
    all_packed = gather_axis(packed.reshape(req_dev * steps, -1), "tp", tp_size, 1).reshape(
        requests, steps, -1
    )
    all_normed = all_packed[:, :, :width]
    all_ids = all_packed[:, :, width:].astype(jnp.int32)
    onehot = all_ids[..., None] == expert_range
    hits = jnp.sum(onehot.astype(jnp.int32), axis=2)
    earlier = jnp.cumsum(hits, axis=0) - hits
    all_slots = jnp.sum(jnp.where(onehot, earlier[:, :, None, :], 0), axis=3)
    logits = jnp.einsum(
        "rtd,de->rte", all_normed, router_weight, preferred_element_type=jnp.float32
    )
    chosen = jnp.sum(jnp.where(onehot, logits[:, :, None, :], 0.0), axis=3)
    share = 1.0 / (1.0 + jnp.exp(chosen[:, :, ::-1] - chosen))
    slices = seq_size * tp_size // experts
    mine = (seq_index * tp_size + tp_index) // slices
    match = all_ids == mine
    slot_mine = jnp.sum(jnp.where(match, all_slots, 0), axis=2)
    share_mine = jnp.sum(jnp.where(match, share, 0.0), axis=2)
    kept = jnp.any(match, axis=2) & (slot_mine < capacity)
    select = kept[None] & (slot_mine[None] == jnp.arange(capacity, dtype=jnp.int32)[:, None, None])
    buffer = (
        jnp.einsum(
            "crt,rtd->tcd",
            select.astype(jnp.bfloat16),
            all_normed,
            preferred_element_type=jnp.float32,
        )
        .astype(jnp.bfloat16)
        .reshape(steps * capacity, width)
    )
    contract = (((1,), (1,)), ((), ()))
    gate = lax.dot_general(buffer, gate_weight, contract, preferred_element_type=jnp.float32)
    upward = lax.dot_general(buffer, up_weight, contract, preferred_element_type=jnp.float32)
    inner = (jax.nn.gelu(gate) * upward).astype(jnp.bfloat16)
    produced = jnp.dot(inner, down_weight, preferred_element_type=jnp.float32)
    groups = tp_size // slices
    padded = 8 * ((steps * capacity + 7) // 8)
    part = jnp.pad(produced, ((0, padded - steps * capacity), (0, 0)))
    halves = slices // seq_size
    held = ((tp_index % slices) // halves) * groups + tp_index // slices
    held_match = (all_ids == held) & (all_slots < capacity)
    held_row = jnp.arange(steps, dtype=jnp.int32)[None, :, None] * capacity + all_slots
    select_rows = jnp.sum(
        jnp.where(
            held_match[..., None] & (held_row[..., None] == jnp.arange(padded)),
            share[..., None],
            0.0,
        ),
        axis=2,
    ).reshape(tp_size, req_dev * steps, padded)
    tokens = 16 * ((req_dev * steps + 15) // 16)
    select_rows = jnp.pad(select_rows, ((0, 0), (0, tokens - req_dev * steps), (0, 0)))
    landed = combine_rows(part, select_rows, seq_size, tp_size, slices)
    landed = landed.astype(jnp.float32).reshape(tp_size // halves, halves, tokens, width // slices)
    mixture = (
        jnp.sum(landed, axis=0)[:, : req_dev * steps]
        .transpose(1, 0, 2)
        .reshape(req_dev, steps, feature_block)
    )
    own_residual = lax.dynamic_slice_in_dim(residual, seq_index * feature_block, feature_block, 2)
    layer_out = (own_residual + mixture).astype(jnp.bfloat16)
    return (attn_out, layer_out)


def solution(mesh):
    return jax.shard_map(
        body,
        mesh=mesh,
        in_specs=(
            P("tp", None, None),
            P("tp", None, None),
            P("tp", None, None),
            P("tp", None, None),
            P("tp", "seq", None),
            P("tp", "seq", None),
            P("tp"),
            P(),
            P(),
            P(),
            P("tp", None, None),
            P(("seq", "tp"), None),
            P(("seq", "tp"), None),
            P(("seq", "tp"), None),
        ),
        out_specs=(P("tp", None, "seq"), P("tp", None, "seq")),
        check_vma=False,
    )
```

```python
import functools

import jax
import jax.numpy as jnp
from jax import lax
from jax.experimental import pallas as pl
from jax.experimental.pallas import tpu as pltpu
from jax.sharding import PartitionSpec as P

HEADS = 16


masked_score = -1e30
norm_epsilon = 1e-06


def exchange_kernel(seq_size, tp_size, stats_ref, ids_ref, stats_out, ids_out, stats_land,
                    ids_land, send_a, recv_a, send_b, recv_b):
    mesh_type = pl.DeviceIdType.MESH
    s = lax.axis_index("seq")
    t = lax.axis_index("tp")

    barrier = pltpu.get_barrier_semaphore()
    for u in range(seq_size):
        @pl.when(s != u)
        def _():
            pl.semaphore_signal(barrier, inc=1, device_id=(u, t), device_id_type=mesh_type)
    for u in range(tp_size):
        @pl.when(t != u)
        def _():
            pl.semaphore_signal(barrier, inc=1, device_id=(s, u), device_id_type=mesh_type)
    pl.semaphore_wait(barrier, seq_size - 1 + tp_size - 1)

    def along_seq(u, slot):
        return pltpu.make_async_remote_copy(
            stats_ref, stats_land.at[slot], send_a.at[u], recv_a.at[slot],
            device_id=(u, t), device_id_type=mesh_type,
        )

    def along_tp(u, slot):
        return pltpu.make_async_remote_copy(
            ids_ref, ids_land.at[slot], send_b.at[u], recv_b.at[slot],
            device_id=(s, u), device_id_type=mesh_type,
        )

    for u in range(seq_size):
        @pl.when(s == u)
        def _():
            pltpu.make_async_copy(stats_ref, stats_land.at[u], recv_a.at[u]).start()

        @pl.when(s != u)
        def _():
            along_seq(u, s).start()
    for u in range(tp_size):
        @pl.when(t == u)
        def _():
            pltpu.make_async_copy(ids_ref, ids_land.at[u], recv_b.at[u]).start()

        @pl.when(t != u)
        def _():
            along_tp(u, t).start()

    for u in range(seq_size):
        @pl.when(s == u)
        def _():
            pltpu.make_async_copy(stats_ref, stats_land.at[u], recv_a.at[u]).wait()

        @pl.when(s != u)
        def _():
            along_seq(u, s).wait_send()
            along_seq(u, u).wait_recv()
    for u in range(tp_size):
        @pl.when(t == u)
        def _():
            pltpu.make_async_copy(ids_ref, ids_land.at[u], recv_b.at[u]).wait()

        @pl.when(t != u)
        def _():
            along_tp(u, t).wait_send()
            along_tp(u, u).wait_recv()

    stats_out[...] = stats_land[...]
    ids_out[...] = ids_land[...]


def exchange(stats, ids, seq_size, tp_size):
    return pl.pallas_call(
        functools.partial(exchange_kernel, seq_size, tp_size),
        out_shape=(
            jax.ShapeDtypeStruct((seq_size,) + stats.shape, stats.dtype),
            jax.ShapeDtypeStruct((tp_size,) + ids.shape, ids.dtype),
        ),
        in_specs=[pl.BlockSpec(memory_space=pltpu.VMEM)] * 2,
        out_specs=(pl.BlockSpec(memory_space=pltpu.VMEM), pl.BlockSpec(memory_space=pltpu.VMEM)),
        scratch_shapes=[
            pltpu.VMEM((seq_size,) + stats.shape, stats.dtype),
            pltpu.VMEM((tp_size,) + ids.shape, ids.dtype),
            pltpu.SemaphoreType.DMA((seq_size,)),
            pltpu.SemaphoreType.DMA((seq_size,)),
            pltpu.SemaphoreType.DMA((tp_size,)),
            pltpu.SemaphoreType.DMA((tp_size,)),
        ],
        compiler_params=pltpu.CompilerParams(collective_id=0, has_side_effects=True),
    )(stats, ids)


def expert_kernel(seq_size, tp_size, slices, piece_ref, pick_in_ref, gate_ref, up_ref,
                  down_ref, pick_out_ref, out_ref, everyone, part, recv, middle, outgoing,
                  landing, send0, recv0, send1, recv1, send3, recv3):
    mesh_type = pl.DeviceIdType.MESH
    s = lax.axis_index("seq")
    t = lax.axis_index("tp")
    g = t // slices
    j = t % slices
    chunk = recv.shape[2]
    halves = slices // seq_size
    src_seq = j // halves

    def dest(i):
        return (i // halves, g * slices + s * halves + i % halves)

    def is_self(i):
        return (i // halves == s) & (g * slices + s * halves + i % halves == t)

    barrier = pltpu.get_barrier_semaphore()
    for u in range(tp_size):
        @pl.when(t != u)
        def _():
            pl.semaphore_signal(barrier, inc=1, device_id=(s, u), device_id_type=mesh_type)
    for i in range(slices):
        @pl.when(i // halves != s)
        def _():
            pl.semaphore_signal(barrier, inc=1, device_id=dest(i), device_id_type=mesh_type)
    for k in range(slices):
        @pl.when((src_seq != s) & (k // halves != s))
        def _():
            pl.semaphore_signal(
                barrier, inc=1, device_id=(src_seq, g * slices + k), device_id_type=mesh_type
            )
    far = (seq_size - 1) * halves
    near = tp_size - 1 + far

    @pl.when(src_seq == s)
    def _():
        pl.semaphore_wait(barrier, near)

    @pl.when(src_seq != s)
    def _():
        pl.semaphore_wait(barrier, near + slices - halves)

    def gather(u, slot):
        return pltpu.make_async_remote_copy(
            piece_ref, everyone.at[slot], send0.at[u], recv0.at[slot],
            device_id=(s, u), device_id_type=mesh_type,
        )

    for u in range(tp_size):
        @pl.when(t == u)
        def _():
            pltpu.make_async_copy(piece_ref, everyone.at[u], recv0.at[u]).start()

        @pl.when(t != u)
        def _():
            gather(u, t).start()

    for u in range(tp_size):
        @pl.when(t == u)
        def _():
            pltpu.make_async_copy(piece_ref, everyone.at[u], recv0.at[u]).wait()

        @pl.when(t != u)
        def _():
            gather(u, t).wait_send()
            gather(u, u).wait_recv()

    rows_in = everyone[...].reshape(-1, everyone.shape[2])
    buffer = jnp.dot(pick_in_ref[...], rows_in, preferred_element_type=jnp.float32).astype(
        jnp.bfloat16
    )
    contract = (((1,), (1,)), ((), ()))
    gate = lax.dot_general(buffer, gate_ref[...], contract, preferred_element_type=jnp.float32)
    upward = lax.dot_general(buffer, up_ref[...], contract, preferred_element_type=jnp.float32)
    inner = (jax.nn.gelu(gate) * upward).astype(jnp.bfloat16)
    part[...] = jnp.dot(inner, down_ref[...], preferred_element_type=jnp.float32)

    def stage1(i):
        return pltpu.make_async_remote_copy(
            part.at[:, pl.ds(i * chunk, chunk)],
            recv.at[j],
            send1.at[i],
            recv1.at[j],
            device_id=dest(i),
            device_id_type=mesh_type,
        )

    for i in range(slices):
        @pl.when(is_self(i))
        def _():
            pltpu.make_async_copy(part.at[:, pl.ds(i * chunk, chunk)], recv.at[j], recv1.at[j]).start()

        @pl.when(jnp.logical_not(is_self(i)))
        def _():
            stage1(i).start()

    for i in range(slices):
        @pl.when(jnp.logical_not(is_self(i)))
        def _():
            stage1(i).wait_send()

    for k in range(slices):
        from_self = (src_seq == s) & (k == j)

        @pl.when(from_self)
        def _():
            pltpu.make_async_copy(part.at[:, pl.ds(0, chunk)], recv.at[k], recv1.at[k]).wait()

        @pl.when(jnp.logical_not(from_self))
        def _():
            pltpu.make_async_remote_copy(
                part.at[:, pl.ds(0, chunk)],
                recv.at[k],
                send1.at[0],
                recv1.at[k],
                device_id=(src_seq, g * slices + k),
                device_id_type=mesh_type,
            ).wait_recv()

    total = recv[0]
    for k in range(1, slices):
        total = total + recv[k]
    middle[...] = total.astype(middle.dtype)

    picked = jnp.dot(
        pick_out_ref[...].reshape(-1, pick_out_ref.shape[2]),
        middle[...],
        preferred_element_type=jnp.float32,
    )
    outgoing[...] = picked.reshape(outgoing.shape).astype(outgoing.dtype)

    def stage3(u):
        return pltpu.make_async_remote_copy(
            outgoing.at[u], landing.at[t], send3.at[u], recv3.at[t],
            device_id=(s, u), device_id_type=mesh_type,
        )

    for u in range(tp_size):
        @pl.when(t == u)
        def _():
            pltpu.make_async_copy(outgoing.at[u], landing.at[u], recv3.at[u]).start()

        @pl.when(t != u)
        def _():
            stage3(u).start()

    for u in range(tp_size):
        @pl.when(t == u)
        def _():
            pltpu.make_async_copy(outgoing.at[u], landing.at[u], recv3.at[u]).wait()

        @pl.when(t != u)
        def _():
            stage3(u).wait_send()
            pltpu.make_async_remote_copy(
                outgoing.at[u], landing.at[u], send3.at[u], recv3.at[u],
                device_id=(s, u), device_id_type=mesh_type,
            ).wait_recv()

    out_ref[...] = landing[...]


def run_experts(piece, pick_in, gate_weight, up_weight, down_weight, pick_out, seq_size,
                tp_size, slices):
    tokens, width = piece.shape
    rows = pick_in.shape[0]
    chunk = width // slices
    return pl.pallas_call(
        functools.partial(expert_kernel, seq_size, tp_size, slices),
        out_shape=jax.ShapeDtypeStruct((tp_size, tokens, chunk), jnp.bfloat16),
        in_specs=[pl.BlockSpec(memory_space=pltpu.VMEM)] * 6,
        out_specs=pl.BlockSpec(memory_space=pltpu.VMEM),
        scratch_shapes=[
            pltpu.VMEM((tp_size, tokens, width), jnp.bfloat16),
            pltpu.VMEM((rows, width), jnp.float32),
            pltpu.VMEM((slices, rows, chunk), jnp.float32),
            pltpu.VMEM((rows, chunk), jnp.bfloat16),
            pltpu.VMEM((tp_size, tokens, chunk), jnp.bfloat16),
            pltpu.VMEM((tp_size, tokens, chunk), jnp.bfloat16),
            pltpu.SemaphoreType.DMA((tp_size,)),
            pltpu.SemaphoreType.DMA((tp_size,)),
            pltpu.SemaphoreType.DMA((slices,)),
            pltpu.SemaphoreType.DMA((slices,)),
            pltpu.SemaphoreType.DMA((tp_size,)),
            pltpu.SemaphoreType.DMA((tp_size,)),
        ],
        compiler_params=pltpu.CompilerParams(collective_id=1, has_side_effects=True),
    )(piece, pick_in, gate_weight, up_weight, down_weight, pick_out)


def body(
    hidden_in,
    new_query,
    new_key,
    new_value,
    key_cache,
    value_cache,
    lengths,
    out_weight,
    norm_gain,
    router_weight,
    expert_ids,
    gate_weight,
    up_weight,
    down_weight,
):
    req_dev, steps, width = hidden_in.shape
    block = key_cache.shape[1]
    head_size = width // HEADS
    scale = head_size ** (-0.5)
    seq_index = lax.axis_index("seq")
    tp_index = lax.axis_index("tp")
    seq_size = lax.axis_size("seq")
    tp_size = lax.axis_size("tp")
    rows = steps * HEADS
    own = req_dev * steps

    head_mask = (jnp.arange(width) // head_size)[None, :] == jnp.arange(HEADS)[:, None]
    q_wide = jnp.where(head_mask[None, None], new_query[:, :, None, :], 0).reshape(
        req_dev, rows, width
    )
    with jax.named_scope("cache_scores"):
        scores = (
            jnp.einsum("rqd,rpd->rqp", q_wide, key_cache, preferred_element_type=jnp.float32)
            * scale
        )
    positions = seq_index * block + jnp.arange(block, dtype=jnp.int32)
    usable = (positions[None, :] < lengths[:, None])[:, None, :]
    scores = jnp.where(usable, scores, masked_score)
    fresh_scores = (
        jnp.einsum("rqd,rsd->rqs", q_wide, new_key, preferred_element_type=jnp.float32) * scale
    )
    causal = (
        (jnp.arange(rows)[:, None] // HEADS) >= jnp.arange(steps)[None, :]
    ) & (seq_index == 0)
    fresh_scores = jnp.where(causal, fresh_scores, masked_score)
    local_max = jnp.maximum(jnp.max(scores, axis=2), jnp.max(fresh_scores, axis=2))
    weights = jnp.where(usable, jnp.exp(scores - local_max[..., None]), 0.0)
    fresh_weights = jnp.where(causal, jnp.exp(fresh_scores - local_max[..., None]), 0.0)
    totals = jnp.sum(weights, axis=2) + jnp.sum(fresh_weights, axis=2)
    with jax.named_scope("cache_values"):
        wide_values = jnp.einsum(
            "rqp,rpd->rqd",
            weights.astype(jnp.bfloat16),
            value_cache,
            preferred_element_type=jnp.float32,
        )
    wide_values = wide_values + jnp.einsum(
        "rqs,rsd->rqd",
        fresh_weights.astype(jnp.bfloat16),
        new_value,
        preferred_element_type=jnp.float32,
    )
    partial = jnp.sum(
        jnp.where(head_mask[None, None], wide_values.reshape(req_dev, steps, HEADS, width), 0.0),
        axis=2,
    )
    stats = jnp.concatenate(
        [
            partial,
            local_max.reshape(req_dev, steps, HEADS),
            totals.reshape(req_dev, steps, HEADS),
        ],
        axis=2,
    ).reshape(own, -1)
    id_count = expert_ids.size
    id_rows = 8
    id_piece = jnp.pad(expert_ids.reshape(1, id_count), ((0, id_rows - 1), (0, 128 - id_count)))
    every, all_id_pieces = exchange(stats, id_piece, seq_size, tp_size)
    every = every.reshape((seq_size, req_dev, steps, -1))
    all_ids = all_id_pieces[:, 0, :id_count].reshape(tp_size * req_dev, steps, -1)
    block_sums = every[..., :width]
    block_max = every[..., width : width + HEADS]
    block_totals = every[..., width + HEADS :]
    overall = jnp.max(block_max, axis=0)
    factors = jnp.exp(block_max - overall[None])
    numer = jnp.sum(jnp.repeat(factors, head_size, axis=-1) * block_sums, axis=0)
    denom = jnp.sum(factors * block_totals, axis=0)
    context = (numer / jnp.repeat(denom, head_size, axis=-1)).astype(jnp.bfloat16)
    attention = jnp.einsum("rtd,de->rte", context, out_weight, preferred_element_type=jnp.float32)
    feature_block = width // seq_size
    attn_out = lax.dynamic_slice_in_dim(
        attention, seq_index * feature_block, feature_block, 2
    ).astype(jnp.bfloat16)
    residual = hidden_in.astype(jnp.float32) + attention
    normed = (
        residual
        * lax.rsqrt(jnp.mean(residual * residual, axis=-1, keepdims=True) + norm_epsilon)
        * norm_gain
    ).astype(jnp.bfloat16)

    experts = router_weight.shape[1]
    topk = expert_ids.shape[2]
    requests = req_dev * tp_size
    capacity = (5 * requests * topk + 4 * experts - 1) // (4 * experts)
    expert_range = jnp.arange(experts, dtype=jnp.int32)
    slices = seq_size * tp_size // experts
    groups = tp_size // slices
    halves = slices // seq_size
    padded = 8 * ((steps * capacity + 7) // 8)
    tokens = 16 * ((own + 15) // 16)

    onehot = all_ids[..., None] == expert_range
    hits = jnp.sum(onehot.astype(jnp.int32), axis=2)
    earlier = jnp.cumsum(hits, axis=0) - hits
    all_slots = jnp.sum(jnp.where(onehot, earlier[:, :, None, :], 0), axis=3)
    row_of = jnp.arange(steps, dtype=jnp.int32)[None, :, None] * capacity + all_slots

    def rows_for(expert):
        hit = (all_ids == expert) & (all_slots < capacity)
        chosen_rows = jnp.any(
            hit[..., None] & (row_of[..., None] == jnp.arange(padded)), axis=2
        ).reshape(tp_size, own, padded)
        return jnp.pad(chosen_rows, ((0, 0), (0, tokens - own), (0, 0))).astype(jnp.bfloat16)

    mine = (seq_index * tp_size + tp_index) // slices
    pick_in = rows_for(mine).reshape(tp_size * tokens, padded).T
    held = ((tp_index % slices) // halves) * groups + tp_index // slices
    pick_out = rows_for(held)
    piece = jnp.pad(normed.reshape(own, width), ((0, tokens - own), (0, 0)))
    landed = run_experts(
        piece, pick_in, gate_weight, up_weight, down_weight, pick_out, seq_size, tp_size, slices
    )

    logits = jnp.einsum("rtd,de->rte", normed, router_weight, preferred_element_type=jnp.float32)
    own_hot = expert_ids[..., None] == expert_range
    chosen = jnp.sum(jnp.where(own_hot, logits[:, :, None, :], 0.0), axis=3)
    share = 1.0 / (1.0 + jnp.exp(chosen[:, :, ::-1] - chosen))
    own_slots = lax.dynamic_slice_in_dim(all_slots, tp_index * req_dev, req_dev, 0)
    weight = jnp.where(own_slots < capacity, share, 0.0)
    slot_expert = (jnp.arange(tp_size // halves) % (tp_size // (groups * halves))) * groups + (
        jnp.arange(tp_size // halves) // (tp_size // (groups * halves))
    )
    per_slot = jnp.sum(
        jnp.where(expert_ids[..., None] == slot_expert, weight[..., None], 0.0), axis=2
    ).reshape(own, tp_size // halves)
    landed = landed.astype(jnp.float32).reshape(tp_size // halves, halves, tokens, feature_block // halves)
    mixture = jnp.einsum(
        "ia,ahif->ihf", per_slot, landed[:, :, :own], precision=lax.Precision.HIGHEST
    ).reshape(req_dev, steps, feature_block)
    own_residual = lax.dynamic_slice_in_dim(residual, seq_index * feature_block, feature_block, 2)
    layer_out = (own_residual + mixture).astype(jnp.bfloat16)
    return (attn_out, layer_out)


def solution(mesh):

    return jax.shard_map(
        body,
        mesh=mesh,
        in_specs=(
            P("tp", None, None),
            P("tp", None, None),
            P("tp", None, None),
            P("tp", None, None),
            P("tp", "seq", None),
            P("tp", "seq", None),
            P("tp"),
            P(),
            P(),
            P(),
            P("tp", None, None),
            P(("seq", "tp"), None),
            P(("seq", "tp"), None),
            P(("seq", "tp"), None),
        ),
        out_specs=(P("tp", None, "seq"), P("tp", None, "seq")),
        check_vma=False,
    )
```

```python
import functools

import jax
import jax.numpy as jnp
from jax import lax
from jax.experimental import pallas as pl
from jax.experimental.pallas import tpu as pltpu
from jax.sharding import PartitionSpec as P

HEADS = 16


masked_score = -1e30
norm_epsilon = 1e-06


def exchange_kernel(seq_size, tp_size, scale, query_ref, key_hbm, value_hbm, usable_ref,
                    fresh_ref, fresh_ok_ref, fresh_value_ref, ids_ref, sums_out, stats_out,
                    ids_out, keys, values, sums, stats, sums_land, stats_land, ids_land,
                    load_sem, send_a, recv_a, send_c, recv_c, send_b, recv_b):
    mesh_type = pl.DeviceIdType.MESH
    s = lax.axis_index("seq")
    t = lax.axis_index("tp")
    req_dev, rows, width = query_ref.shape
    heads = HEADS

    barrier = pltpu.get_barrier_semaphore()
    for u in range(seq_size):
        @pl.when(s != u)
        def _():
            pl.semaphore_signal(barrier, inc=1, device_id=(u, t), device_id_type=mesh_type)
    for u in range(tp_size):
        @pl.when(t != u)
        def _():
            pl.semaphore_signal(barrier, inc=1, device_id=(s, u), device_id_type=mesh_type)

    loads = []
    for r in range(req_dev):
        loads.append(pltpu.make_async_copy(key_hbm.at[r], keys.at[r], load_sem.at[0, r]))
        loads.append(pltpu.make_async_copy(value_hbm.at[r], values.at[r], load_sem.at[1, r]))
    for copy in loads:
        copy.start()

    head_of = lax.broadcasted_iota(jnp.int32, (rows, width), 1) // (width // heads)
    row_head = lax.broadcasted_iota(jnp.int32, (rows, width), 0) % heads
    own_head = head_of == row_head
    lane = lax.broadcasted_iota(jnp.int32, (rows, 128), 1)
    contract = (((1,), (1,)), ((), ()))
    for r in range(req_dev):
        loads[2 * r].wait()
        scores = lax.dot_general(
            query_ref[r], keys[r], contract, preferred_element_type=jnp.float32
        ) * scale
        usable = usable_ref[r, 0:1, :] > 0.5
        scores = jnp.where(usable, scores, masked_score)
        fresh = fresh_ref[r]
        fresh_ok = fresh_ok_ref[r] > 0.5
        top = jnp.maximum(
            jnp.max(scores, axis=1, keepdims=True), jnp.max(fresh, axis=1, keepdims=True)
        )
        weights = jnp.where(usable, jnp.exp(scores - top), 0.0)
        fresh_weights = jnp.where(fresh_ok, jnp.exp(fresh - top), 0.0)
        total = jnp.sum(weights, axis=1, keepdims=True) + jnp.sum(
            fresh_weights, axis=1, keepdims=True
        )
        loads[2 * r + 1].wait()
        wide = jnp.dot(
            weights.astype(jnp.bfloat16), values[r], preferred_element_type=jnp.float32
        ) + jnp.dot(
            fresh_weights.astype(jnp.bfloat16), fresh_value_ref[r],
            preferred_element_type=jnp.float32,
        )
        wide = jnp.where(own_head, wide, 0.0)
        sums[r] = jnp.sum(wide.reshape(rows // heads, heads, width), axis=1)
        stats[r] = jnp.where(lane < 64, top, total)

    pl.semaphore_wait(barrier, seq_size - 1 + tp_size - 1)

    def sums_copy(u, slot):
        return pltpu.make_async_remote_copy(
            sums, sums_land.at[slot], send_a.at[u], recv_a.at[slot],
            device_id=(u, t), device_id_type=mesh_type,
        )

    def stats_copy(u, slot):
        return pltpu.make_async_remote_copy(
            stats, stats_land.at[slot], send_c.at[u], recv_c.at[slot],
            device_id=(u, t), device_id_type=mesh_type,
        )

    def along_tp(u, slot):
        return pltpu.make_async_remote_copy(
            ids_ref, ids_land.at[slot], send_b.at[u], recv_b.at[slot],
            device_id=(s, u), device_id_type=mesh_type,
        )

    for u in range(seq_size):
        @pl.when(s == u)
        def _():
            pltpu.make_async_copy(sums, sums_land.at[u], recv_a.at[u]).start()
            pltpu.make_async_copy(stats, stats_land.at[u], recv_c.at[u]).start()

        @pl.when(s != u)
        def _():
            sums_copy(u, s).start()
            stats_copy(u, s).start()
    for u in range(tp_size):
        @pl.when(t == u)
        def _():
            pltpu.make_async_copy(ids_ref, ids_land.at[u], recv_b.at[u]).start()

        @pl.when(t != u)
        def _():
            along_tp(u, t).start()

    for u in range(seq_size):
        @pl.when(s == u)
        def _():
            pltpu.make_async_copy(sums, sums_land.at[u], recv_a.at[u]).wait()
            pltpu.make_async_copy(stats, stats_land.at[u], recv_c.at[u]).wait()

        @pl.when(s != u)
        def _():
            sums_copy(u, s).wait_send()
            sums_copy(u, u).wait_recv()
            stats_copy(u, s).wait_send()
            stats_copy(u, u).wait_recv()
    for u in range(tp_size):
        @pl.when(t == u)
        def _():
            pltpu.make_async_copy(ids_ref, ids_land.at[u], recv_b.at[u]).wait()

        @pl.when(t != u)
        def _():
            along_tp(u, t).wait_send()
            along_tp(u, u).wait_recv()

    sums_out[...] = sums_land[...]
    stats_out[...] = stats_land[...]
    ids_out[...] = ids_land[...]


def exchange(query, key_cache, value_cache, usable, fresh, fresh_ok, fresh_value, ids,
             seq_size, tp_size, scale):
    req_dev, rows, width = query.shape
    steps = rows // HEADS
    vmem = pl.BlockSpec(memory_space=pltpu.VMEM)
    return pl.pallas_call(
        functools.partial(exchange_kernel, seq_size, tp_size, scale),
        out_shape=(
            jax.ShapeDtypeStruct((seq_size, req_dev, steps, width), jnp.float32),
            jax.ShapeDtypeStruct((seq_size, req_dev, rows, 128), jnp.float32),
            jax.ShapeDtypeStruct((tp_size,) + ids.shape, ids.dtype),
        ),
        in_specs=[vmem, pl.BlockSpec(memory_space=pl.ANY), pl.BlockSpec(memory_space=pl.ANY)]
        + [vmem] * 5,
        out_specs=(vmem, vmem, vmem),
        scratch_shapes=[
            pltpu.VMEM(key_cache.shape, key_cache.dtype),
            pltpu.VMEM(value_cache.shape, value_cache.dtype),
            pltpu.VMEM((req_dev, steps, width), jnp.float32),
            pltpu.VMEM((req_dev, rows, 128), jnp.float32),
            pltpu.VMEM((seq_size, req_dev, steps, width), jnp.float32),
            pltpu.VMEM((seq_size, req_dev, rows, 128), jnp.float32),
            pltpu.VMEM((tp_size,) + ids.shape, ids.dtype),
            pltpu.SemaphoreType.DMA((2, req_dev)),
            pltpu.SemaphoreType.DMA((seq_size,)),
            pltpu.SemaphoreType.DMA((seq_size,)),
            pltpu.SemaphoreType.DMA((seq_size,)),
            pltpu.SemaphoreType.DMA((seq_size,)),
            pltpu.SemaphoreType.DMA((tp_size,)),
            pltpu.SemaphoreType.DMA((tp_size,)),
        ],
        compiler_params=pltpu.CompilerParams(
            collective_id=0, has_side_effects=True, vmem_limit_bytes=48 * 1024 * 1024
        ),
    )(query, key_cache, value_cache, usable, fresh, fresh_ok, fresh_value, ids)


def expert_kernel(seq_size, tp_size, slices, piece_ref, pick_in_ref, gate_ref, up_ref,
                  down_ref, pick_out_ref, out_ref, everyone, part, recv, middle, outgoing,
                  landing, send0, recv0, send1, recv1, send3, recv3):
    mesh_type = pl.DeviceIdType.MESH
    s = lax.axis_index("seq")
    t = lax.axis_index("tp")
    g = t // slices
    j = t % slices
    chunk = recv.shape[2]
    halves = slices // seq_size
    src_seq = j // halves

    def dest(i):
        return (i // halves, g * slices + s * halves + i % halves)

    def is_self(i):
        return (i // halves == s) & (g * slices + s * halves + i % halves == t)

    barrier = pltpu.get_barrier_semaphore()
    for u in range(tp_size):
        @pl.when(t != u)
        def _():
            pl.semaphore_signal(barrier, inc=1, device_id=(s, u), device_id_type=mesh_type)
    for i in range(slices):
        @pl.when(i // halves != s)
        def _():
            pl.semaphore_signal(barrier, inc=1, device_id=dest(i), device_id_type=mesh_type)
    for k in range(slices):
        @pl.when((src_seq != s) & (k // halves != s))
        def _():
            pl.semaphore_signal(
                barrier, inc=1, device_id=(src_seq, g * slices + k), device_id_type=mesh_type
            )
    far = (seq_size - 1) * halves
    near = tp_size - 1 + far

    @pl.when(src_seq == s)
    def _():
        pl.semaphore_wait(barrier, near)

    @pl.when(src_seq != s)
    def _():
        pl.semaphore_wait(barrier, near + slices - halves)

    def gather(u, slot):
        return pltpu.make_async_remote_copy(
            piece_ref, everyone.at[slot], send0.at[u], recv0.at[slot],
            device_id=(s, u), device_id_type=mesh_type,
        )

    for u in range(tp_size):
        @pl.when(t == u)
        def _():
            pltpu.make_async_copy(piece_ref, everyone.at[u], recv0.at[u]).start()

        @pl.when(t != u)
        def _():
            gather(u, t).start()

    for u in range(tp_size):
        @pl.when(t == u)
        def _():
            pltpu.make_async_copy(piece_ref, everyone.at[u], recv0.at[u]).wait()

        @pl.when(t != u)
        def _():
            gather(u, t).wait_send()
            gather(u, u).wait_recv()

    rows_in = everyone[...].reshape(-1, everyone.shape[2])
    buffer = jnp.dot(pick_in_ref[...], rows_in, preferred_element_type=jnp.float32).astype(
        jnp.bfloat16
    )
    contract = (((1,), (1,)), ((), ()))
    gate = lax.dot_general(buffer, gate_ref[...], contract, preferred_element_type=jnp.float32)
    upward = lax.dot_general(buffer, up_ref[...], contract, preferred_element_type=jnp.float32)
    inner = (jax.nn.gelu(gate) * upward).astype(jnp.bfloat16)
    part[...] = jnp.dot(inner, down_ref[...], preferred_element_type=jnp.float32)

    def stage1(i):
        return pltpu.make_async_remote_copy(
            part.at[:, pl.ds(i * chunk, chunk)],
            recv.at[j],
            send1.at[i],
            recv1.at[j],
            device_id=dest(i),
            device_id_type=mesh_type,
        )

    for i in range(slices):
        @pl.when(is_self(i))
        def _():
            pltpu.make_async_copy(part.at[:, pl.ds(i * chunk, chunk)], recv.at[j], recv1.at[j]).start()

        @pl.when(jnp.logical_not(is_self(i)))
        def _():
            stage1(i).start()

    for i in range(slices):
        @pl.when(jnp.logical_not(is_self(i)))
        def _():
            stage1(i).wait_send()

    for k in range(slices):
        from_self = (src_seq == s) & (k == j)

        @pl.when(from_self)
        def _():
            pltpu.make_async_copy(part.at[:, pl.ds(0, chunk)], recv.at[k], recv1.at[k]).wait()

        @pl.when(jnp.logical_not(from_self))
        def _():
            pltpu.make_async_remote_copy(
                part.at[:, pl.ds(0, chunk)],
                recv.at[k],
                send1.at[0],
                recv1.at[k],
                device_id=(src_seq, g * slices + k),
                device_id_type=mesh_type,
            ).wait_recv()

    total = recv[0]
    for k in range(1, slices):
        total = total + recv[k]
    middle[...] = total.astype(middle.dtype)

    picked = jnp.dot(
        pick_out_ref[...].reshape(-1, pick_out_ref.shape[2]),
        middle[...],
        preferred_element_type=jnp.float32,
    )
    outgoing[...] = picked.reshape(outgoing.shape).astype(outgoing.dtype)

    def stage3(u):
        return pltpu.make_async_remote_copy(
            outgoing.at[u], landing.at[t], send3.at[u], recv3.at[t],
            device_id=(s, u), device_id_type=mesh_type,
        )

    for u in range(tp_size):
        @pl.when(t == u)
        def _():
            pltpu.make_async_copy(outgoing.at[u], landing.at[u], recv3.at[u]).start()

        @pl.when(t != u)
        def _():
            stage3(u).start()

    for u in range(tp_size):
        @pl.when(t == u)
        def _():
            pltpu.make_async_copy(outgoing.at[u], landing.at[u], recv3.at[u]).wait()

        @pl.when(t != u)
        def _():
            stage3(u).wait_send()
            pltpu.make_async_remote_copy(
                outgoing.at[u], landing.at[u], send3.at[u], recv3.at[u],
                device_id=(s, u), device_id_type=mesh_type,
            ).wait_recv()

    out_ref[...] = landing[...]


def run_experts(piece, pick_in, gate_weight, up_weight, down_weight, pick_out, seq_size,
                tp_size, slices):
    tokens, width = piece.shape
    rows = pick_in.shape[0]
    chunk = width // slices
    return pl.pallas_call(
        functools.partial(expert_kernel, seq_size, tp_size, slices),
        out_shape=jax.ShapeDtypeStruct((tp_size, tokens, chunk), jnp.bfloat16),
        in_specs=[pl.BlockSpec(memory_space=pltpu.VMEM)] * 6,
        out_specs=pl.BlockSpec(memory_space=pltpu.VMEM),
        scratch_shapes=[
            pltpu.VMEM((tp_size, tokens, width), jnp.bfloat16),
            pltpu.VMEM((rows, width), jnp.float32),
            pltpu.VMEM((slices, rows, chunk), jnp.float32),
            pltpu.VMEM((rows, chunk), jnp.bfloat16),
            pltpu.VMEM((tp_size, tokens, chunk), jnp.bfloat16),
            pltpu.VMEM((tp_size, tokens, chunk), jnp.bfloat16),
            pltpu.SemaphoreType.DMA((tp_size,)),
            pltpu.SemaphoreType.DMA((tp_size,)),
            pltpu.SemaphoreType.DMA((slices,)),
            pltpu.SemaphoreType.DMA((slices,)),
            pltpu.SemaphoreType.DMA((tp_size,)),
            pltpu.SemaphoreType.DMA((tp_size,)),
        ],
        compiler_params=pltpu.CompilerParams(collective_id=1, has_side_effects=True),
    )(piece, pick_in, gate_weight, up_weight, down_weight, pick_out)


def body(
    hidden_in,
    new_query,
    new_key,
    new_value,
    key_cache,
    value_cache,
    lengths,
    out_weight,
    norm_gain,
    router_weight,
    expert_ids,
    gate_weight,
    up_weight,
    down_weight,
):
    req_dev, steps, width = hidden_in.shape
    block = key_cache.shape[1]
    head_size = width // HEADS
    scale = head_size ** (-0.5)
    seq_index = lax.axis_index("seq")
    tp_index = lax.axis_index("tp")
    seq_size = lax.axis_size("seq")
    tp_size = lax.axis_size("tp")
    rows = steps * HEADS
    own = req_dev * steps

    head_mask = (jnp.arange(width) // head_size)[None, :] == jnp.arange(HEADS)[:, None]
    q_wide = jnp.where(head_mask[None, None], new_query[:, :, None, :], 0).reshape(
        req_dev, rows, width
    )
    positions = seq_index * block + jnp.arange(block, dtype=jnp.int32)
    usable = (positions[None, :] < lengths[:, None]).astype(jnp.float32)
    usable = jnp.broadcast_to(usable[:, None, :], (req_dev, 8, block))
    fresh_scores = (
        jnp.einsum("rqd,rsd->rqs", q_wide, new_key, preferred_element_type=jnp.float32) * scale
    )
    causal = (
        (jnp.arange(rows)[:, None] // HEADS) >= jnp.arange(steps)[None, :]
    ) & (seq_index == 0)
    fresh_scores = jnp.where(causal, fresh_scores, masked_score)
    fresh_scores = jnp.pad(
        fresh_scores, ((0, 0), (0, 0), (0, 128 - steps)), constant_values=masked_score
    )
    fresh_ok = jnp.pad(
        jnp.broadcast_to(causal, (req_dev, rows, steps)).astype(jnp.float32),
        ((0, 0), (0, 0), (0, 128 - steps)),
    )
    fresh_value = jnp.pad(new_value, ((0, 0), (0, 128 - steps), (0, 0)))
    id_count = expert_ids.size
    id_rows = 8
    id_piece = jnp.pad(expert_ids.reshape(1, id_count), ((0, id_rows - 1), (0, 128 - id_count)))
    block_sums, every_stats, all_id_pieces = exchange(
        q_wide, key_cache, value_cache, usable, fresh_scores, fresh_ok, fresh_value, id_piece,
        seq_size, tp_size, scale,
    )
    all_ids = all_id_pieces[:, 0, :id_count].reshape(tp_size * req_dev, steps, -1)
    block_max = every_stats[..., 0].reshape(seq_size, req_dev, steps, HEADS)
    block_totals = every_stats[..., 64].reshape(seq_size, req_dev, steps, HEADS)
    overall = jnp.max(block_max, axis=0)
    factors = jnp.exp(block_max - overall[None])
    numer = jnp.sum(jnp.repeat(factors, head_size, axis=-1) * block_sums, axis=0)
    denom = jnp.sum(factors * block_totals, axis=0)
    context = (numer / jnp.repeat(denom, head_size, axis=-1)).astype(jnp.bfloat16)
    attention = jnp.einsum("rtd,de->rte", context, out_weight, preferred_element_type=jnp.float32)
    feature_block = width // seq_size
    attn_out = lax.dynamic_slice_in_dim(
        attention, seq_index * feature_block, feature_block, 2
    ).astype(jnp.bfloat16)
    residual = hidden_in.astype(jnp.float32) + attention
    normed = (
        residual
        * lax.rsqrt(jnp.mean(residual * residual, axis=-1, keepdims=True) + norm_epsilon)
        * norm_gain
    ).astype(jnp.bfloat16)

    experts = router_weight.shape[1]
    topk = expert_ids.shape[2]
    requests = req_dev * tp_size
    capacity = (5 * requests * topk + 4 * experts - 1) // (4 * experts)
    expert_range = jnp.arange(experts, dtype=jnp.int32)
    slices = seq_size * tp_size // experts
    groups = tp_size // slices
    halves = slices // seq_size
    padded = 8 * ((steps * capacity + 7) // 8)
    tokens = 16 * ((own + 15) // 16)

    onehot = all_ids[..., None] == expert_range
    hits = jnp.sum(onehot.astype(jnp.int32), axis=2)
    earlier = jnp.cumsum(hits, axis=0) - hits
    all_slots = jnp.sum(jnp.where(onehot, earlier[:, :, None, :], 0), axis=3)
    row_of = jnp.arange(steps, dtype=jnp.int32)[None, :, None] * capacity + all_slots

    def rows_for(expert):
        hit = (all_ids == expert) & (all_slots < capacity)
        chosen_rows = jnp.any(
            hit[..., None] & (row_of[..., None] == jnp.arange(padded)), axis=2
        ).reshape(tp_size, own, padded)
        return jnp.pad(chosen_rows, ((0, 0), (0, tokens - own), (0, 0))).astype(jnp.bfloat16)

    mine = (seq_index * tp_size + tp_index) // slices
    pick_in = rows_for(mine).reshape(tp_size * tokens, padded).T
    held = ((tp_index % slices) // halves) * groups + tp_index // slices
    pick_out = rows_for(held)
    piece = jnp.pad(normed.reshape(own, width), ((0, tokens - own), (0, 0)))
    landed = run_experts(
        piece, pick_in, gate_weight, up_weight, down_weight, pick_out, seq_size, tp_size, slices
    )

    logits = jnp.einsum("rtd,de->rte", normed, router_weight, preferred_element_type=jnp.float32)
    own_hot = expert_ids[..., None] == expert_range
    chosen = jnp.sum(jnp.where(own_hot, logits[:, :, None, :], 0.0), axis=3)
    share = 1.0 / (1.0 + jnp.exp(chosen[:, :, ::-1] - chosen))
    own_slots = lax.dynamic_slice_in_dim(all_slots, tp_index * req_dev, req_dev, 0)
    weight = jnp.where(own_slots < capacity, share, 0.0)
    slot_expert = (jnp.arange(tp_size // halves) % (tp_size // (groups * halves))) * groups + (
        jnp.arange(tp_size // halves) // (tp_size // (groups * halves))
    )
    per_slot = jnp.sum(
        jnp.where(expert_ids[..., None] == slot_expert, weight[..., None], 0.0), axis=2
    ).reshape(own, tp_size // halves)
    landed = landed.astype(jnp.float32).reshape(tp_size // halves, halves, tokens, feature_block // halves)
    mixture = jnp.einsum(
        "ia,ahif->ihf", per_slot, landed[:, :, :own], precision=lax.Precision.HIGHEST
    ).reshape(req_dev, steps, feature_block)
    own_residual = lax.dynamic_slice_in_dim(residual, seq_index * feature_block, feature_block, 2)
    layer_out = (own_residual + mixture).astype(jnp.bfloat16)
    return (attn_out, layer_out)


def solution(mesh):

    return jax.shard_map(
        body,
        mesh=mesh,
        in_specs=(
            P("tp", None, None),
            P("tp", None, None),
            P("tp", None, None),
            P("tp", None, None),
            P("tp", "seq", None),
            P("tp", "seq", None),
            P("tp"),
            P(),
            P(),
            P(),
            P("tp", None, None),
            P(("seq", "tp"), None),
            P(("seq", "tp"), None),
            P(("seq", "tp"), None),
        ),
        out_specs=(P("tp", None, "seq"), P("tp", None, "seq")),
        check_vma=False,
    )
```

```python
import functools

import jax
import jax.numpy as jnp
from jax import lax
from jax.experimental import pallas as pl
from jax.experimental.pallas import tpu as pltpu
from jax.sharding import PartitionSpec as P

HEADS = 16


masked_score = -1e30
norm_epsilon = 1e-06


def exchange_kernel(seq_size, tp_size, scale, query_ref, key_hbm, value_hbm, usable_ref,
                    fresh_ref, fresh_ok_ref, fresh_value_ref, ids_ref, sums_out,
                    ids_out, keys, values, sums, sums_land, ids_land,
                    load_sem, send_a, recv_a, send_b, recv_b):
    mesh_type = pl.DeviceIdType.MESH
    s = lax.axis_index("seq")
    t = lax.axis_index("tp")
    req_dev, rows, width = query_ref.shape
    heads = HEADS

    barrier = pltpu.get_barrier_semaphore()
    for u in range(seq_size):
        @pl.when(s != u)
        def _():
            pl.semaphore_signal(barrier, inc=1, device_id=(u, t), device_id_type=mesh_type)
    for u in range(tp_size):
        @pl.when(t != u)
        def _():
            pl.semaphore_signal(barrier, inc=1, device_id=(s, u), device_id_type=mesh_type)

    loads = []
    for r in range(req_dev):
        loads.append(pltpu.make_async_copy(key_hbm.at[r], keys.at[r], load_sem.at[0, r]))
        loads.append(pltpu.make_async_copy(value_hbm.at[r], values.at[r], load_sem.at[1, r]))
    for copy in loads:
        copy.start()

    head_of = lax.broadcasted_iota(jnp.int32, (rows, width), 1) // (width // heads)
    row_head = lax.broadcasted_iota(jnp.int32, (rows, width), 0) % heads
    own_head = head_of == row_head
    spread = (
        lax.broadcasted_iota(jnp.int32, (rows // heads, rows), 1) // heads
        == lax.broadcasted_iota(jnp.int32, (rows // heads, rows), 0)
    ).astype(jnp.float32)
    contract = (((1,), (1,)), ((), ()))
    for r in range(req_dev):
        loads[2 * r].wait()
        scores = lax.dot_general(
            query_ref[r], keys[r], contract, preferred_element_type=jnp.float32
        ) * scale
        usable = usable_ref[r, 0:1, :] > 0.5
        scores = jnp.where(usable, scores, masked_score)
        fresh = fresh_ref[r]
        fresh_ok = fresh_ok_ref[r] > 0.5
        top = jnp.maximum(
            jnp.max(scores, axis=1, keepdims=True), jnp.max(fresh, axis=1, keepdims=True)
        )
        weights = jnp.where(usable, jnp.exp(scores - top), 0.0)
        fresh_weights = jnp.where(fresh_ok, jnp.exp(fresh - top), 0.0)
        total = jnp.sum(weights, axis=1, keepdims=True) + jnp.sum(
            fresh_weights, axis=1, keepdims=True
        )
        loads[2 * r + 1].wait()
        wide = jnp.dot(
            weights.astype(jnp.bfloat16), values[r], preferred_element_type=jnp.float32
        ) + jnp.dot(
            fresh_weights.astype(jnp.bfloat16), fresh_value_ref[r],
            preferred_element_type=jnp.float32,
        )
        wide = jnp.where(own_head, wide, 0.0)
        steps = rows // heads
        sums[r, 0:steps, :] = jnp.sum(wide.reshape(steps, heads, width), axis=1)
        sums[r, steps : 2 * steps, :] = jnp.dot(
            spread, jnp.where(own_head, top, 0.0),
            precision=lax.Precision.HIGHEST, preferred_element_type=jnp.float32,
        )
        sums[r, 2 * steps : 3 * steps, :] = jnp.dot(
            spread, jnp.where(own_head, total, 0.0),
            precision=lax.Precision.HIGHEST, preferred_element_type=jnp.float32,
        )
        sums[r, 3 * steps :, :] = jnp.zeros((sums.shape[1] - 3 * steps, width), jnp.float32)

    pl.semaphore_wait(barrier, seq_size - 1 + tp_size - 1)

    def sums_copy(u, slot):
        return pltpu.make_async_remote_copy(
            sums, sums_land.at[slot], send_a.at[u], recv_a.at[slot],
            device_id=(u, t), device_id_type=mesh_type,
        )

    def along_tp(u, slot):
        return pltpu.make_async_remote_copy(
            ids_ref, ids_land.at[slot], send_b.at[u], recv_b.at[slot],
            device_id=(s, u), device_id_type=mesh_type,
        )

    for u in range(seq_size):
        @pl.when(s == u)
        def _():
            pltpu.make_async_copy(sums, sums_land.at[u], recv_a.at[u]).start()

        @pl.when(s != u)
        def _():
            sums_copy(u, s).start()
    for u in range(tp_size):
        @pl.when(t == u)
        def _():
            pltpu.make_async_copy(ids_ref, ids_land.at[u], recv_b.at[u]).start()

        @pl.when(t != u)
        def _():
            along_tp(u, t).start()

    for u in range(seq_size):
        @pl.when(s == u)
        def _():
            pltpu.make_async_copy(sums, sums_land.at[u], recv_a.at[u]).wait()

        @pl.when(s != u)
        def _():
            sums_copy(u, s).wait_send()
            sums_copy(u, u).wait_recv()
    for u in range(tp_size):
        @pl.when(t == u)
        def _():
            pltpu.make_async_copy(ids_ref, ids_land.at[u], recv_b.at[u]).wait()

        @pl.when(t != u)
        def _():
            along_tp(u, t).wait_send()
            along_tp(u, u).wait_recv()

    sums_out[...] = sums_land[...]
    ids_out[...] = ids_land[...]


def exchange(query, key_cache, value_cache, usable, fresh, fresh_ok, fresh_value, ids,
             seq_size, tp_size, scale):
    req_dev, rows, width = query.shape
    steps = rows // HEADS
    vmem = pl.BlockSpec(memory_space=pltpu.VMEM)
    return pl.pallas_call(
        functools.partial(exchange_kernel, seq_size, tp_size, scale),
        out_shape=(
            jax.ShapeDtypeStruct((seq_size, req_dev, 4 * steps, width), jnp.float32),
            jax.ShapeDtypeStruct((tp_size,) + ids.shape, ids.dtype),
        ),
        in_specs=[vmem, pl.BlockSpec(memory_space=pl.ANY), pl.BlockSpec(memory_space=pl.ANY)]
        + [vmem] * 5,
        out_specs=(vmem, vmem),
        scratch_shapes=[
            pltpu.VMEM(key_cache.shape, key_cache.dtype),
            pltpu.VMEM(value_cache.shape, value_cache.dtype),
            pltpu.VMEM((req_dev, 4 * steps, width), jnp.float32),
            pltpu.VMEM((seq_size, req_dev, 4 * steps, width), jnp.float32),
            pltpu.VMEM((tp_size,) + ids.shape, ids.dtype),
            pltpu.SemaphoreType.DMA((2, req_dev)),
            pltpu.SemaphoreType.DMA((seq_size,)),
            pltpu.SemaphoreType.DMA((seq_size,)),
            pltpu.SemaphoreType.DMA((tp_size,)),
            pltpu.SemaphoreType.DMA((tp_size,)),
        ],
        compiler_params=pltpu.CompilerParams(
            collective_id=0, has_side_effects=True, vmem_limit_bytes=48 * 1024 * 1024
        ),
    )(query, key_cache, value_cache, usable, fresh, fresh_ok, fresh_value, ids)


def expert_kernel(seq_size, tp_size, slices, sums_ref, hidden_ref, out_weight_ref, gain_ref,
                  pick_in_ref, gate_ref, up_ref, down_ref, pick_out_ref, out_ref, attn_ref,
                  normed_ref, piece_ref, context, everyone, part, recv, middle, outgoing,
                  landing, send0, recv0, send1, recv1, send3, recv3):
    mesh_type = pl.DeviceIdType.MESH
    s = lax.axis_index("seq")
    t = lax.axis_index("tp")
    g = t // slices
    j = t % slices
    chunk = recv.shape[2]
    halves = slices // seq_size
    src_seq = j // halves

    def dest(i):
        return (i // halves, g * slices + s * halves + i % halves)

    def is_self(i):
        return (i // halves == s) & (g * slices + s * halves + i % halves == t)

    barrier = pltpu.get_barrier_semaphore()
    for u in range(tp_size):
        @pl.when(t != u)
        def _():
            pl.semaphore_signal(barrier, inc=1, device_id=(s, u), device_id_type=mesh_type)
    for i in range(slices):
        @pl.when(i // halves != s)
        def _():
            pl.semaphore_signal(barrier, inc=1, device_id=dest(i), device_id_type=mesh_type)
    for k in range(slices):
        @pl.when((src_seq != s) & (k // halves != s))
        def _():
            pl.semaphore_signal(
                barrier, inc=1, device_id=(src_seq, g * slices + k), device_id_type=mesh_type
            )
    req_dev = sums_ref.shape[1]
    steps = sums_ref.shape[2] // 4
    context[...] = jnp.zeros_like(context)
    for r in range(req_dev):
        block_sums = [sums_ref[b, r, 0:steps, :] for b in range(seq_size)]
        block_max = [sums_ref[b, r, steps : 2 * steps, :] for b in range(seq_size)]
        block_totals = [sums_ref[b, r, 2 * steps : 3 * steps, :] for b in range(seq_size)]
        overall = block_max[0]
        for b in range(1, seq_size):
            overall = jnp.maximum(overall, block_max[b])
        numer = jnp.zeros_like(overall)
        denom = jnp.zeros_like(overall)
        for b in range(seq_size):
            factor = jnp.exp(block_max[b] - overall)
            numer = numer + factor * block_sums[b]
            denom = denom + factor * block_totals[b]
        context[r * steps : (r + 1) * steps, :] = numer / denom
    attention = jnp.dot(
        context[...].astype(jnp.bfloat16), out_weight_ref[...], preferred_element_type=jnp.float32
    )
    attn_ref[...] = attention
    residual = hidden_ref[...] + attention
    mean_square = jnp.mean(residual * residual, axis=1, keepdims=True)
    normed = (residual * lax.rsqrt(mean_square + norm_epsilon) * gain_ref[...]).astype(
        jnp.bfloat16
    )
    piece_ref[...] = normed
    normed_ref[...] = normed

    far = (seq_size - 1) * halves
    near = tp_size - 1 + far

    @pl.when(src_seq == s)
    def _():
        pl.semaphore_wait(barrier, near)

    @pl.when(src_seq != s)
    def _():
        pl.semaphore_wait(barrier, near + slices - halves)

    def gather(u, slot):
        return pltpu.make_async_remote_copy(
            piece_ref, everyone.at[slot], send0.at[u], recv0.at[slot],
            device_id=(s, u), device_id_type=mesh_type,
        )

    for u in range(tp_size):
        @pl.when(t == u)
        def _():
            pltpu.make_async_copy(piece_ref, everyone.at[u], recv0.at[u]).start()

        @pl.when(t != u)
        def _():
            gather(u, t).start()

    for u in range(tp_size):
        @pl.when(t == u)
        def _():
            pltpu.make_async_copy(piece_ref, everyone.at[u], recv0.at[u]).wait()

        @pl.when(t != u)
        def _():
            gather(u, t).wait_send()
            gather(u, u).wait_recv()

    rows_in = everyone[...].reshape(-1, everyone.shape[2])
    buffer = jnp.dot(pick_in_ref[...], rows_in, preferred_element_type=jnp.float32).astype(
        jnp.bfloat16
    )
    contract = (((1,), (1,)), ((), ()))
    gate = lax.dot_general(buffer, gate_ref[...], contract, preferred_element_type=jnp.float32)
    upward = lax.dot_general(buffer, up_ref[...], contract, preferred_element_type=jnp.float32)
    inner = (jax.nn.gelu(gate) * upward).astype(jnp.bfloat16)
    part[...] = jnp.dot(inner, down_ref[...], preferred_element_type=jnp.float32)

    def stage1(i):
        return pltpu.make_async_remote_copy(
            part.at[:, pl.ds(i * chunk, chunk)],
            recv.at[j],
            send1.at[i],
            recv1.at[j],
            device_id=dest(i),
            device_id_type=mesh_type,
        )

    for i in range(slices):
        @pl.when(is_self(i))
        def _():
            pltpu.make_async_copy(part.at[:, pl.ds(i * chunk, chunk)], recv.at[j], recv1.at[j]).start()

        @pl.when(jnp.logical_not(is_self(i)))
        def _():
            stage1(i).start()

    for i in range(slices):
        @pl.when(jnp.logical_not(is_self(i)))
        def _():
            stage1(i).wait_send()

    for k in range(slices):
        from_self = (src_seq == s) & (k == j)

        @pl.when(from_self)
        def _():
            pltpu.make_async_copy(part.at[:, pl.ds(0, chunk)], recv.at[k], recv1.at[k]).wait()

        @pl.when(jnp.logical_not(from_self))
        def _():
            pltpu.make_async_remote_copy(
                part.at[:, pl.ds(0, chunk)],
                recv.at[k],
                send1.at[0],
                recv1.at[k],
                device_id=(src_seq, g * slices + k),
                device_id_type=mesh_type,
            ).wait_recv()

    total = recv[0]
    for k in range(1, slices):
        total = total + recv[k]
    middle[...] = total.astype(middle.dtype)

    picked = jnp.dot(
        pick_out_ref[...].reshape(-1, pick_out_ref.shape[2]),
        middle[...],
        preferred_element_type=jnp.float32,
    )
    outgoing[...] = picked.reshape(outgoing.shape).astype(outgoing.dtype)

    def stage3(u):
        return pltpu.make_async_remote_copy(
            outgoing.at[u], landing.at[t], send3.at[u], recv3.at[t],
            device_id=(s, u), device_id_type=mesh_type,
        )

    for u in range(tp_size):
        @pl.when(t == u)
        def _():
            pltpu.make_async_copy(outgoing.at[u], landing.at[u], recv3.at[u]).start()

        @pl.when(t != u)
        def _():
            stage3(u).start()

    for u in range(tp_size):
        @pl.when(t == u)
        def _():
            pltpu.make_async_copy(outgoing.at[u], landing.at[u], recv3.at[u]).wait()

        @pl.when(t != u)
        def _():
            stage3(u).wait_send()
            pltpu.make_async_remote_copy(
                outgoing.at[u], landing.at[u], send3.at[u], recv3.at[u],
                device_id=(s, u), device_id_type=mesh_type,
            ).wait_recv()

    out_ref[...] = landing[...]


def run_experts(sums, hidden, out_weight, gain, pick_in, gate_weight, up_weight, down_weight,
                pick_out, seq_size, tp_size, slices):
    tokens, width = hidden.shape
    rows = pick_in.shape[0]
    chunk = width // slices
    vmem = pl.BlockSpec(memory_space=pltpu.VMEM)
    return pl.pallas_call(
        functools.partial(expert_kernel, seq_size, tp_size, slices),
        out_shape=(
            jax.ShapeDtypeStruct((tp_size, tokens, chunk), jnp.bfloat16),
            jax.ShapeDtypeStruct((tokens, width), jnp.float32),
            jax.ShapeDtypeStruct((tokens, width), jnp.bfloat16),
        ),
        in_specs=[vmem] * 9,
        out_specs=(vmem, vmem, vmem),
        scratch_shapes=[
            pltpu.VMEM((tokens, width), jnp.bfloat16),
            pltpu.VMEM((tokens, width), jnp.float32),
            pltpu.VMEM((tp_size, tokens, width), jnp.bfloat16),
            pltpu.VMEM((rows, width), jnp.float32),
            pltpu.VMEM((slices, rows, chunk), jnp.float32),
            pltpu.VMEM((rows, chunk), jnp.bfloat16),
            pltpu.VMEM((tp_size, tokens, chunk), jnp.bfloat16),
            pltpu.VMEM((tp_size, tokens, chunk), jnp.bfloat16),
            pltpu.SemaphoreType.DMA((tp_size,)),
            pltpu.SemaphoreType.DMA((tp_size,)),
            pltpu.SemaphoreType.DMA((slices,)),
            pltpu.SemaphoreType.DMA((slices,)),
            pltpu.SemaphoreType.DMA((tp_size,)),
            pltpu.SemaphoreType.DMA((tp_size,)),
        ],
        compiler_params=pltpu.CompilerParams(
            collective_id=1, has_side_effects=True, vmem_limit_bytes=48 * 1024 * 1024
        ),
    )(sums, hidden, out_weight, gain, pick_in, gate_weight, up_weight, down_weight, pick_out)


def body(
    hidden_in,
    new_query,
    new_key,
    new_value,
    key_cache,
    value_cache,
    lengths,
    out_weight,
    norm_gain,
    router_weight,
    expert_ids,
    gate_weight,
    up_weight,
    down_weight,
):
    req_dev, steps, width = hidden_in.shape
    block = key_cache.shape[1]
    head_size = width // HEADS
    scale = head_size ** (-0.5)
    seq_index = lax.axis_index("seq")
    tp_index = lax.axis_index("tp")
    seq_size = lax.axis_size("seq")
    tp_size = lax.axis_size("tp")
    rows = steps * HEADS
    own = req_dev * steps

    head_mask = (jnp.arange(width) // head_size)[None, :] == jnp.arange(HEADS)[:, None]
    q_wide = jnp.where(head_mask[None, None], new_query[:, :, None, :], 0).reshape(
        req_dev, rows, width
    )
    positions = seq_index * block + jnp.arange(block, dtype=jnp.int32)
    usable = (positions[None, :] < lengths[:, None]).astype(jnp.float32)
    usable = jnp.broadcast_to(usable[:, None, :], (req_dev, 8, block))
    fresh_scores = (
        jnp.einsum("rqd,rsd->rqs", q_wide, new_key, preferred_element_type=jnp.float32) * scale
    )
    causal = (
        (jnp.arange(rows)[:, None] // HEADS) >= jnp.arange(steps)[None, :]
    ) & (seq_index == 0)
    fresh_scores = jnp.where(causal, fresh_scores, masked_score)
    fresh_scores = jnp.pad(
        fresh_scores, ((0, 0), (0, 0), (0, 128 - steps)), constant_values=masked_score
    )
    fresh_ok = jnp.pad(
        jnp.broadcast_to(causal, (req_dev, rows, steps)).astype(jnp.float32),
        ((0, 0), (0, 0), (0, 128 - steps)),
    )
    fresh_value = jnp.pad(new_value, ((0, 0), (0, 128 - steps), (0, 0)))
    id_count = expert_ids.size
    id_rows = 8
    id_piece = jnp.pad(expert_ids.reshape(1, id_count), ((0, id_rows - 1), (0, 128 - id_count)))
    block_sums, all_id_pieces = exchange(
        q_wide, key_cache, value_cache, usable, fresh_scores, fresh_ok, fresh_value, id_piece,
        seq_size, tp_size, scale,
    )
    all_ids = all_id_pieces[:, 0, :id_count].reshape(tp_size * req_dev, steps, -1)
    feature_block = width // seq_size
    experts = router_weight.shape[1]
    topk = expert_ids.shape[2]
    requests = req_dev * tp_size
    capacity = (5 * requests * topk + 4 * experts - 1) // (4 * experts)
    expert_range = jnp.arange(experts, dtype=jnp.int32)
    slices = seq_size * tp_size // experts
    groups = tp_size // slices
    halves = slices // seq_size
    padded = 8 * ((steps * capacity + 7) // 8)
    tokens = 16 * ((own + 15) // 16)

    onehot = all_ids[..., None] == expert_range
    hits = jnp.sum(onehot.astype(jnp.int32), axis=2)
    earlier = jnp.cumsum(hits, axis=0) - hits
    all_slots = jnp.sum(jnp.where(onehot, earlier[:, :, None, :], 0), axis=3)
    row_of = jnp.arange(steps, dtype=jnp.int32)[None, :, None] * capacity + all_slots

    def rows_for(expert):
        hit = (all_ids == expert) & (all_slots < capacity)
        chosen_rows = jnp.any(
            hit[..., None] & (row_of[..., None] == jnp.arange(padded)), axis=2
        ).reshape(tp_size, own, padded)
        return jnp.pad(chosen_rows, ((0, 0), (0, tokens - own), (0, 0))).astype(jnp.bfloat16)

    mine = (seq_index * tp_size + tp_index) // slices
    pick_in = rows_for(mine).reshape(tp_size * tokens, padded).T
    held = ((tp_index % slices) // halves) * groups + tp_index // slices
    pick_out = rows_for(held)
    hidden = jnp.pad(
        hidden_in.astype(jnp.float32).reshape(own, width), ((0, tokens - own), (0, 0))
    )
    landed, attention, normed = run_experts(
        block_sums, hidden, out_weight, norm_gain.reshape(1, width), pick_in, gate_weight,
        up_weight, down_weight, pick_out, seq_size, tp_size, slices,
    )
    attention = attention[:own].reshape(req_dev, steps, width)
    normed = normed[:own].reshape(req_dev, steps, width)
    attn_out = lax.dynamic_slice_in_dim(
        attention, seq_index * feature_block, feature_block, 2
    ).astype(jnp.bfloat16)
    residual = hidden_in.astype(jnp.float32) + attention

    logits = jnp.einsum("rtd,de->rte", normed, router_weight, preferred_element_type=jnp.float32)
    own_hot = expert_ids[..., None] == expert_range
    chosen = jnp.sum(jnp.where(own_hot, logits[:, :, None, :], 0.0), axis=3)
    share = 1.0 / (1.0 + jnp.exp(chosen[:, :, ::-1] - chosen))
    own_slots = lax.dynamic_slice_in_dim(all_slots, tp_index * req_dev, req_dev, 0)
    weight = jnp.where(own_slots < capacity, share, 0.0)
    slot_expert = (jnp.arange(tp_size // halves) % (tp_size // (groups * halves))) * groups + (
        jnp.arange(tp_size // halves) // (tp_size // (groups * halves))
    )
    per_slot = jnp.sum(
        jnp.where(expert_ids[..., None] == slot_expert, weight[..., None], 0.0), axis=2
    ).reshape(own, tp_size // halves)
    landed = landed.astype(jnp.float32).reshape(tp_size // halves, halves, tokens, feature_block // halves)
    mixture = jnp.einsum(
        "ia,ahif->ihf", per_slot, landed[:, :, :own], precision=lax.Precision.HIGHEST
    ).reshape(req_dev, steps, feature_block)
    own_residual = lax.dynamic_slice_in_dim(residual, seq_index * feature_block, feature_block, 2)
    layer_out = (own_residual + mixture).astype(jnp.bfloat16)
    return (attn_out, layer_out)


def solution(mesh):

    return jax.shard_map(
        body,
        mesh=mesh,
        in_specs=(
            P("tp", None, None),
            P("tp", None, None),
            P("tp", None, None),
            P("tp", None, None),
            P("tp", "seq", None),
            P("tp", "seq", None),
            P("tp"),
            P(),
            P(),
            P(),
            P("tp", None, None),
            P(("seq", "tp"), None),
            P(("seq", "tp"), None),
            P(("seq", "tp"), None),
        ),
        out_specs=(P("tp", None, "seq"), P("tp", None, "seq")),
        check_vma=False,
    )
```

```python
import functools

import jax
import jax.numpy as jnp
from jax import lax
from jax.experimental import pallas as pl
from jax.experimental.pallas import tpu as pltpu
from jax.sharding import PartitionSpec as P

HEADS = 16


masked_score = -1e30
norm_epsilon = 1e-06


def exchange_kernel(seq_size, tp_size, scale, query_ref, key_hbm, value_hbm, usable_ref,
                    fresh_ref, fresh_ok_ref, fresh_value_ref, ids_ref, sums_out,
                    ids_out, keys, values, sums, sums_land, ids_land,
                    load_sem, send_a, recv_a, send_b, recv_b):
    mesh_type = pl.DeviceIdType.MESH
    s = lax.axis_index("seq")
    t = lax.axis_index("tp")
    req_dev, rows, width = query_ref.shape
    heads = HEADS

    barrier = pltpu.get_barrier_semaphore()
    for u in range(seq_size):
        @pl.when(s != u)
        def _():
            pl.semaphore_signal(barrier, inc=1, device_id=(u, t), device_id_type=mesh_type)
    for u in range(tp_size):
        @pl.when(t != u)
        def _():
            pl.semaphore_signal(barrier, inc=1, device_id=(s, u), device_id_type=mesh_type)

    loads = []
    for r in range(req_dev):
        loads.append(pltpu.make_async_copy(key_hbm.at[r], keys.at[r], load_sem.at[0, r]))
        loads.append(pltpu.make_async_copy(value_hbm.at[r], values.at[r], load_sem.at[1, r]))
    for copy in loads:
        copy.start()

    head_of = lax.broadcasted_iota(jnp.int32, (rows, width), 1) // (width // heads)
    row_head = lax.broadcasted_iota(jnp.int32, (rows, width), 0) % heads
    own_head = head_of == row_head
    spread = (
        lax.broadcasted_iota(jnp.int32, (rows // heads, rows), 1) // heads
        == lax.broadcasted_iota(jnp.int32, (rows // heads, rows), 0)
    ).astype(jnp.float32)
    contract = (((1,), (1,)), ((), ()))
    for r in range(req_dev):
        loads[2 * r].wait()
        scores = lax.dot_general(
            query_ref[r], keys[r], contract, preferred_element_type=jnp.float32
        ) * scale
        usable = usable_ref[r, 0:1, :] > 0.5
        scores = jnp.where(usable, scores, masked_score)
        fresh = fresh_ref[r]
        fresh_ok = fresh_ok_ref[r] > 0.5
        top = jnp.maximum(
            jnp.max(scores, axis=1, keepdims=True), jnp.max(fresh, axis=1, keepdims=True)
        )
        weights = jnp.where(usable, jnp.exp(scores - top), 0.0)
        fresh_weights = jnp.where(fresh_ok, jnp.exp(fresh - top), 0.0)
        total = jnp.sum(weights, axis=1, keepdims=True) + jnp.sum(
            fresh_weights, axis=1, keepdims=True
        )
        loads[2 * r + 1].wait()
        wide = jnp.dot(
            weights.astype(jnp.bfloat16), values[r], preferred_element_type=jnp.float32
        ) + jnp.dot(
            fresh_weights.astype(jnp.bfloat16), fresh_value_ref[r],
            preferred_element_type=jnp.float32,
        )
        wide = jnp.where(own_head, wide, 0.0)
        steps = rows // heads
        sums[r, 0:steps, :] = jnp.sum(wide.reshape(steps, heads, width), axis=1)
        sums[r, steps : 2 * steps, :] = jnp.dot(
            spread, jnp.where(own_head, top, 0.0),
            precision=lax.Precision.HIGHEST, preferred_element_type=jnp.float32,
        )
        sums[r, 2 * steps : 3 * steps, :] = jnp.dot(
            spread, jnp.where(own_head, total, 0.0),
            precision=lax.Precision.HIGHEST, preferred_element_type=jnp.float32,
        )
        sums[r, 3 * steps :, :] = jnp.zeros((sums.shape[1] - 3 * steps, width), jnp.float32)

    pl.semaphore_wait(barrier, seq_size - 1 + tp_size - 1)

    def sums_copy(u, slot):
        return pltpu.make_async_remote_copy(
            sums, sums_land.at[slot], send_a.at[u], recv_a.at[slot],
            device_id=(u, t), device_id_type=mesh_type,
        )

    def along_tp(u, slot):
        return pltpu.make_async_remote_copy(
            ids_ref, ids_land.at[slot], send_b.at[u], recv_b.at[slot],
            device_id=(s, u), device_id_type=mesh_type,
        )

    for u in range(seq_size):
        @pl.when(s == u)
        def _():
            pltpu.make_async_copy(sums, sums_land.at[u], recv_a.at[u]).start()

        @pl.when(s != u)
        def _():
            sums_copy(u, s).start()
    for u in range(tp_size):
        @pl.when(t == u)
        def _():
            pltpu.make_async_copy(ids_ref, ids_land.at[u], recv_b.at[u]).start()

        @pl.when(t != u)
        def _():
            along_tp(u, t).start()

    for u in range(seq_size):
        @pl.when(s == u)
        def _():
            pltpu.make_async_copy(sums, sums_land.at[u], recv_a.at[u]).wait()

        @pl.when(s != u)
        def _():
            sums_copy(u, s).wait_send()
            sums_copy(u, u).wait_recv()
    for u in range(tp_size):
        @pl.when(t == u)
        def _():
            pltpu.make_async_copy(ids_ref, ids_land.at[u], recv_b.at[u]).wait()

        @pl.when(t != u)
        def _():
            along_tp(u, t).wait_send()
            along_tp(u, u).wait_recv()

    sums_out[...] = sums_land[...]
    ids_out[...] = ids_land[...]


def exchange(query, key_cache, value_cache, usable, fresh, fresh_ok, fresh_value, ids,
             seq_size, tp_size, scale):
    req_dev, rows, width = query.shape
    steps = rows // HEADS
    vmem = pl.BlockSpec(memory_space=pltpu.VMEM)
    return pl.pallas_call(
        functools.partial(exchange_kernel, seq_size, tp_size, scale),
        out_shape=(
            jax.ShapeDtypeStruct((seq_size, req_dev, 4 * steps, width), jnp.float32),
            jax.ShapeDtypeStruct((tp_size,) + ids.shape, ids.dtype),
        ),
        in_specs=[vmem, pl.BlockSpec(memory_space=pl.ANY), pl.BlockSpec(memory_space=pl.ANY)]
        + [vmem] * 5,
        out_specs=(vmem, vmem),
        scratch_shapes=[
            pltpu.VMEM(key_cache.shape, key_cache.dtype),
            pltpu.VMEM(value_cache.shape, value_cache.dtype),
            pltpu.VMEM((req_dev, 4 * steps, width), jnp.float32),
            pltpu.VMEM((seq_size, req_dev, 4 * steps, width), jnp.float32),
            pltpu.VMEM((tp_size,) + ids.shape, ids.dtype),
            pltpu.SemaphoreType.DMA((2, req_dev)),
            pltpu.SemaphoreType.DMA((seq_size,)),
            pltpu.SemaphoreType.DMA((seq_size,)),
            pltpu.SemaphoreType.DMA((tp_size,)),
            pltpu.SemaphoreType.DMA((tp_size,)),
        ],
        compiler_params=pltpu.CompilerParams(
            collective_id=0, has_side_effects=True
        ),
    )(query, key_cache, value_cache, usable, fresh, fresh_ok, fresh_value, ids)


def expert_kernel(seq_size, tp_size, slices, sums_ref, hidden_ref, out_weight_hbm, gain_ref,
                  pick_in_ref, gate_hbm, up_hbm, down_hbm, pick_out_ref, out_ref, attn_ref,
                  normed_ref, out_weight_ref, gate_ref, up_ref, down_ref, load_sem, piece_ref,
                  context, everyone, part, recv, middle, outgoing, landing, send0, recv0,
                  send1, recv1, send3, recv3):
    mesh_type = pl.DeviceIdType.MESH
    s = lax.axis_index("seq")
    t = lax.axis_index("tp")
    g = t // slices
    j = t % slices
    chunk = recv.shape[2]
    halves = slices // seq_size
    src_seq = j // halves

    def dest(i):
        return (i // halves, g * slices + s * halves + i % halves)

    def is_self(i):
        return (i // halves == s) & (g * slices + s * halves + i % halves == t)

    barrier = pltpu.get_barrier_semaphore()
    for u in range(tp_size):
        @pl.when(t != u)
        def _():
            pl.semaphore_signal(barrier, inc=1, device_id=(s, u), device_id_type=mesh_type)
    for i in range(slices):
        @pl.when(i // halves != s)
        def _():
            pl.semaphore_signal(barrier, inc=1, device_id=dest(i), device_id_type=mesh_type)
    for k in range(slices):
        @pl.when((src_seq != s) & (k // halves != s))
        def _():
            pl.semaphore_signal(
                barrier, inc=1, device_id=(src_seq, g * slices + k), device_id_type=mesh_type
            )
    loads = [
        pltpu.make_async_copy(src_hbm, dst, load_sem.at[n])
        for n, (src_hbm, dst) in enumerate(
            [(out_weight_hbm, out_weight_ref), (gate_hbm, gate_ref), (up_hbm, up_ref),
             (down_hbm, down_ref)]
        )
    ]
    for copy in loads:
        copy.start()

    req_dev = sums_ref.shape[1]
    steps = sums_ref.shape[2] // 4
    context[...] = jnp.zeros_like(context)
    for r in range(req_dev):
        block_sums = [sums_ref[b, r, 0:steps, :] for b in range(seq_size)]
        block_max = [sums_ref[b, r, steps : 2 * steps, :] for b in range(seq_size)]
        block_totals = [sums_ref[b, r, 2 * steps : 3 * steps, :] for b in range(seq_size)]
        overall = block_max[0]
        for b in range(1, seq_size):
            overall = jnp.maximum(overall, block_max[b])
        numer = jnp.zeros_like(overall)
        denom = jnp.zeros_like(overall)
        for b in range(seq_size):
            factor = jnp.exp(block_max[b] - overall)
            numer = numer + factor * block_sums[b]
            denom = denom + factor * block_totals[b]
        context[r * steps : (r + 1) * steps, :] = numer / denom
    loads[0].wait()
    attention = jnp.dot(
        context[...].astype(jnp.bfloat16), out_weight_ref[...], preferred_element_type=jnp.float32
    )
    attn_ref[...] = attention
    residual = hidden_ref[...] + attention
    mean_square = jnp.mean(residual * residual, axis=1, keepdims=True)
    normed = (residual * lax.rsqrt(mean_square + norm_epsilon) * gain_ref[...]).astype(
        jnp.bfloat16
    )
    piece_ref[...] = normed
    normed_ref[...] = normed

    far = (seq_size - 1) * halves
    near = tp_size - 1 + far

    @pl.when(src_seq == s)
    def _():
        pl.semaphore_wait(barrier, near)

    @pl.when(src_seq != s)
    def _():
        pl.semaphore_wait(barrier, near + slices - halves)

    def gather(u, slot):
        return pltpu.make_async_remote_copy(
            piece_ref, everyone.at[slot], send0.at[u], recv0.at[slot],
            device_id=(s, u), device_id_type=mesh_type,
        )

    for u in range(tp_size):
        @pl.when(t == u)
        def _():
            pltpu.make_async_copy(piece_ref, everyone.at[u], recv0.at[u]).start()

        @pl.when(t != u)
        def _():
            gather(u, t).start()

    for u in range(tp_size):
        @pl.when(t == u)
        def _():
            pltpu.make_async_copy(piece_ref, everyone.at[u], recv0.at[u]).wait()

        @pl.when(t != u)
        def _():
            gather(u, t).wait_send()
            gather(u, u).wait_recv()

    for copy in loads[1:]:
        copy.wait()
    rows_in = everyone[...].reshape(-1, everyone.shape[2])
    buffer = jnp.dot(pick_in_ref[...], rows_in, preferred_element_type=jnp.float32).astype(
        jnp.bfloat16
    )
    contract = (((1,), (1,)), ((), ()))
    gate = lax.dot_general(buffer, gate_ref[...], contract, preferred_element_type=jnp.float32)
    upward = lax.dot_general(buffer, up_ref[...], contract, preferred_element_type=jnp.float32)
    inner = (jax.nn.gelu(gate) * upward).astype(jnp.bfloat16)
    part[...] = jnp.dot(inner, down_ref[...], preferred_element_type=jnp.float32)

    def stage1(i):
        return pltpu.make_async_remote_copy(
            part.at[:, pl.ds(i * chunk, chunk)],
            recv.at[j],
            send1.at[i],
            recv1.at[j],
            device_id=dest(i),
            device_id_type=mesh_type,
        )

    for i in range(slices):
        @pl.when(is_self(i))
        def _():
            pltpu.make_async_copy(part.at[:, pl.ds(i * chunk, chunk)], recv.at[j], recv1.at[j]).start()

        @pl.when(jnp.logical_not(is_self(i)))
        def _():
            stage1(i).start()

    for i in range(slices):
        @pl.when(jnp.logical_not(is_self(i)))
        def _():
            stage1(i).wait_send()

    for k in range(slices):
        from_self = (src_seq == s) & (k == j)

        @pl.when(from_self)
        def _():
            pltpu.make_async_copy(part.at[:, pl.ds(0, chunk)], recv.at[k], recv1.at[k]).wait()

        @pl.when(jnp.logical_not(from_self))
        def _():
            pltpu.make_async_remote_copy(
                part.at[:, pl.ds(0, chunk)],
                recv.at[k],
                send1.at[0],
                recv1.at[k],
                device_id=(src_seq, g * slices + k),
                device_id_type=mesh_type,
            ).wait_recv()

    total = recv[0]
    for k in range(1, slices):
        total = total + recv[k]
    middle[...] = total.astype(middle.dtype)

    picked = jnp.dot(
        pick_out_ref[...].reshape(-1, pick_out_ref.shape[2]),
        middle[...],
        preferred_element_type=jnp.float32,
    )
    outgoing[...] = picked.reshape(outgoing.shape).astype(outgoing.dtype)

    def stage3(u):
        return pltpu.make_async_remote_copy(
            outgoing.at[u], landing.at[t], send3.at[u], recv3.at[t],
            device_id=(s, u), device_id_type=mesh_type,
        )

    for u in range(tp_size):
        @pl.when(t == u)
        def _():
            pltpu.make_async_copy(outgoing.at[u], landing.at[u], recv3.at[u]).start()

        @pl.when(t != u)
        def _():
            stage3(u).start()

    for u in range(tp_size):
        @pl.when(t == u)
        def _():
            pltpu.make_async_copy(outgoing.at[u], landing.at[u], recv3.at[u]).wait()

        @pl.when(t != u)
        def _():
            stage3(u).wait_send()
            pltpu.make_async_remote_copy(
                outgoing.at[u], landing.at[u], send3.at[u], recv3.at[u],
                device_id=(s, u), device_id_type=mesh_type,
            ).wait_recv()

    out_ref[...] = landing[...]


def run_experts(sums, hidden, out_weight, gain, pick_in, gate_weight, up_weight, down_weight,
                pick_out, seq_size, tp_size, slices):
    tokens, width = hidden.shape
    rows = pick_in.shape[0]
    chunk = width // slices
    vmem = pl.BlockSpec(memory_space=pltpu.VMEM)
    hbm = pl.BlockSpec(memory_space=pl.ANY)
    return pl.pallas_call(
        functools.partial(expert_kernel, seq_size, tp_size, slices),
        out_shape=(
            jax.ShapeDtypeStruct((tp_size, tokens, chunk), jnp.bfloat16),
            jax.ShapeDtypeStruct((tokens, width), jnp.float32),
            jax.ShapeDtypeStruct((tokens, width), jnp.bfloat16),
        ),
        in_specs=[vmem, vmem, hbm, vmem, vmem, hbm, hbm, hbm, vmem],
        out_specs=(vmem, vmem, vmem),
        scratch_shapes=[
            pltpu.VMEM(out_weight.shape, out_weight.dtype),
            pltpu.VMEM(gate_weight.shape, gate_weight.dtype),
            pltpu.VMEM(up_weight.shape, up_weight.dtype),
            pltpu.VMEM(down_weight.shape, down_weight.dtype),
            pltpu.SemaphoreType.DMA((4,)),
            pltpu.VMEM((tokens, width), jnp.bfloat16),
            pltpu.VMEM((tokens, width), jnp.float32),
            pltpu.VMEM((tp_size, tokens, width), jnp.bfloat16),
            pltpu.VMEM((rows, width), jnp.float32),
            pltpu.VMEM((slices, rows, chunk), jnp.float32),
            pltpu.VMEM((rows, chunk), jnp.bfloat16),
            pltpu.VMEM((tp_size, tokens, chunk), jnp.bfloat16),
            pltpu.VMEM((tp_size, tokens, chunk), jnp.bfloat16),
            pltpu.SemaphoreType.DMA((tp_size,)),
            pltpu.SemaphoreType.DMA((tp_size,)),
            pltpu.SemaphoreType.DMA((slices,)),
            pltpu.SemaphoreType.DMA((slices,)),
            pltpu.SemaphoreType.DMA((tp_size,)),
            pltpu.SemaphoreType.DMA((tp_size,)),
        ],
        compiler_params=pltpu.CompilerParams(
            collective_id=1, has_side_effects=True
        ),
    )(sums, hidden, out_weight, gain, pick_in, gate_weight, up_weight, down_weight, pick_out)


def body(
    hidden_in,
    new_query,
    new_key,
    new_value,
    key_cache,
    value_cache,
    lengths,
    out_weight,
    norm_gain,
    router_weight,
    expert_ids,
    gate_weight,
    up_weight,
    down_weight,
):
    req_dev, steps, width = hidden_in.shape
    block = key_cache.shape[1]
    head_size = width // HEADS
    scale = head_size ** (-0.5)
    seq_index = lax.axis_index("seq")
    tp_index = lax.axis_index("tp")
    seq_size = lax.axis_size("seq")
    tp_size = lax.axis_size("tp")
    rows = steps * HEADS
    own = req_dev * steps

    head_mask = (jnp.arange(width) // head_size)[None, :] == jnp.arange(HEADS)[:, None]
    q_wide = jnp.where(head_mask[None, None], new_query[:, :, None, :], 0).reshape(
        req_dev, rows, width
    )
    positions = seq_index * block + jnp.arange(block, dtype=jnp.int32)
    usable = (positions[None, :] < lengths[:, None]).astype(jnp.float32)
    usable = jnp.broadcast_to(usable[:, None, :], (req_dev, 8, block))
    fresh_scores = (
        jnp.einsum("rqd,rsd->rqs", q_wide, new_key, preferred_element_type=jnp.float32) * scale
    )
    causal = (
        (jnp.arange(rows)[:, None] // HEADS) >= jnp.arange(steps)[None, :]
    ) & (seq_index == 0)
    fresh_scores = jnp.where(causal, fresh_scores, masked_score)
    fresh_scores = jnp.pad(
        fresh_scores, ((0, 0), (0, 0), (0, 128 - steps)), constant_values=masked_score
    )
    fresh_ok = jnp.pad(
        jnp.broadcast_to(causal, (req_dev, rows, steps)).astype(jnp.float32),
        ((0, 0), (0, 0), (0, 128 - steps)),
    )
    fresh_value = jnp.pad(new_value, ((0, 0), (0, 128 - steps), (0, 0)))
    id_count = expert_ids.size
    id_rows = 8
    id_piece = jnp.pad(expert_ids.reshape(1, id_count), ((0, id_rows - 1), (0, 128 - id_count)))
    block_sums, all_id_pieces = exchange(
        q_wide, key_cache, value_cache, usable, fresh_scores, fresh_ok, fresh_value, id_piece,
        seq_size, tp_size, scale,
    )
    all_ids = all_id_pieces[:, 0, :id_count].reshape(tp_size * req_dev, steps, -1)
    feature_block = width // seq_size
    experts = router_weight.shape[1]
    topk = expert_ids.shape[2]
    requests = req_dev * tp_size
    capacity = (5 * requests * topk + 4 * experts - 1) // (4 * experts)
    expert_range = jnp.arange(experts, dtype=jnp.int32)
    slices = seq_size * tp_size // experts
    groups = tp_size // slices
    halves = slices // seq_size
    padded = 8 * ((steps * capacity + 7) // 8)
    tokens = 16 * ((own + 15) // 16)

    onehot = all_ids[..., None] == expert_range
    hits = jnp.sum(onehot.astype(jnp.int32), axis=2)
    earlier = jnp.cumsum(hits, axis=0) - hits
    all_slots = jnp.sum(jnp.where(onehot, earlier[:, :, None, :], 0), axis=3)
    row_of = jnp.arange(steps, dtype=jnp.int32)[None, :, None] * capacity + all_slots

    def rows_for(expert):
        hit = (all_ids == expert) & (all_slots < capacity)
        chosen_rows = jnp.any(
            hit[..., None] & (row_of[..., None] == jnp.arange(padded)), axis=2
        ).reshape(tp_size, own, padded)
        return jnp.pad(chosen_rows, ((0, 0), (0, tokens - own), (0, 0))).astype(jnp.bfloat16)

    mine = (seq_index * tp_size + tp_index) // slices
    pick_in = rows_for(mine).reshape(tp_size * tokens, padded).T
    held = ((tp_index % slices) // halves) * groups + tp_index // slices
    pick_out = rows_for(held)
    hidden = jnp.pad(
        hidden_in.astype(jnp.float32).reshape(own, width), ((0, tokens - own), (0, 0))
    )
    landed, attention, normed = run_experts(
        block_sums, hidden, out_weight, norm_gain.reshape(1, width), pick_in, gate_weight,
        up_weight, down_weight, pick_out, seq_size, tp_size, slices,
    )
    attention = attention[:own].reshape(req_dev, steps, width)
    normed = normed[:own].reshape(req_dev, steps, width)
    attn_out = lax.dynamic_slice_in_dim(
        attention, seq_index * feature_block, feature_block, 2
    ).astype(jnp.bfloat16)
    residual = hidden_in.astype(jnp.float32) + attention

    logits = jnp.einsum("rtd,de->rte", normed, router_weight, preferred_element_type=jnp.float32)
    own_hot = expert_ids[..., None] == expert_range
    chosen = jnp.sum(jnp.where(own_hot, logits[:, :, None, :], 0.0), axis=3)
    share = 1.0 / (1.0 + jnp.exp(chosen[:, :, ::-1] - chosen))
    own_slots = lax.dynamic_slice_in_dim(all_slots, tp_index * req_dev, req_dev, 0)
    weight = jnp.where(own_slots < capacity, share, 0.0)
    slot_expert = (jnp.arange(tp_size // halves) % (tp_size // (groups * halves))) * groups + (
        jnp.arange(tp_size // halves) // (tp_size // (groups * halves))
    )
    per_slot = jnp.sum(
        jnp.where(expert_ids[..., None] == slot_expert, weight[..., None], 0.0), axis=2
    ).reshape(own, tp_size // halves)
    landed = landed.astype(jnp.float32).reshape(tp_size // halves, halves, tokens, feature_block // halves)
    mixture = jnp.einsum(
        "ia,ahif->ihf", per_slot, landed[:, :, :own], precision=lax.Precision.HIGHEST
    ).reshape(req_dev, steps, feature_block)
    own_residual = lax.dynamic_slice_in_dim(residual, seq_index * feature_block, feature_block, 2)
    layer_out = (own_residual + mixture).astype(jnp.bfloat16)
    return (attn_out, layer_out)


def solution(mesh):

    return jax.shard_map(
        body,
        mesh=mesh,
        in_specs=(
            P("tp", None, None),
            P("tp", None, None),
            P("tp", None, None),
            P("tp", None, None),
            P("tp", "seq", None),
            P("tp", "seq", None),
            P("tp"),
            P(),
            P(),
            P(),
            P("tp", None, None),
            P(("seq", "tp"), None),
            P(("seq", "tp"), None),
            P(("seq", "tp"), None),
        ),
        out_specs=(P("tp", None, "seq"), P("tp", None, "seq")),
        check_vma=False,
    )
```

```python
import functools

import jax
import jax.numpy as jnp
from jax import lax
from jax.experimental import pallas as pl
from jax.experimental.pallas import tpu as pltpu
from jax.sharding import PartitionSpec as P

HEADS = 16


masked_score = -1e30
norm_epsilon = 1e-06


def exchange_kernel(seq_size, tp_size, scale, query_ref, key_hbm, value_hbm, usable_ref,
                    fresh_ref, fresh_ok_ref, fresh_value_ref, ids_ref, sums_out,
                    ids_out, keys, values, sums, sums_land, ids_land,
                    load_sem, send_a, recv_a, send_b, recv_b):
    mesh_type = pl.DeviceIdType.MESH
    s = lax.axis_index("seq")
    t = lax.axis_index("tp")
    req_dev, rows, width = query_ref.shape
    heads = HEADS

    barrier = pltpu.get_barrier_semaphore()
    for u in range(seq_size):
        @pl.when(s != u)
        def _():
            pl.semaphore_signal(barrier, inc=1, device_id=(u, t), device_id_type=mesh_type)
    for u in range(tp_size):
        @pl.when(t != u)
        def _():
            pl.semaphore_signal(barrier, inc=1, device_id=(s, u), device_id_type=mesh_type)

    loads = []
    for r in range(req_dev):
        loads.append(pltpu.make_async_copy(key_hbm.at[r], keys.at[r], load_sem.at[0, r]))
        loads.append(pltpu.make_async_copy(value_hbm.at[r], values.at[r], load_sem.at[1, r]))
    for copy in loads:
        copy.start()

    head_of = lax.broadcasted_iota(jnp.int32, (rows, width), 1) // (width // heads)
    row_head = lax.broadcasted_iota(jnp.int32, (rows, width), 0) % heads
    own_head = head_of == row_head
    spread = (
        lax.broadcasted_iota(jnp.int32, (rows // heads, rows), 1) // heads
        == lax.broadcasted_iota(jnp.int32, (rows // heads, rows), 0)
    ).astype(jnp.float32)
    contract = (((1,), (1,)), ((), ()))
    for r in range(req_dev):
        loads[2 * r].wait()
        scores = lax.dot_general(
            query_ref[r], keys[r], contract, preferred_element_type=jnp.float32
        ) * scale
        usable = usable_ref[r, 0:1, :] > 0.5
        scores = jnp.where(usable, scores, masked_score)
        fresh = fresh_ref[r]
        fresh_ok = fresh_ok_ref[r] > 0.5
        top = jnp.maximum(
            jnp.max(scores, axis=1, keepdims=True), jnp.max(fresh, axis=1, keepdims=True)
        )
        weights = jnp.where(usable, jnp.exp(scores - top), 0.0)
        fresh_weights = jnp.where(fresh_ok, jnp.exp(fresh - top), 0.0)
        total = jnp.sum(weights, axis=1, keepdims=True) + jnp.sum(
            fresh_weights, axis=1, keepdims=True
        )
        loads[2 * r + 1].wait()
        wide = jnp.dot(
            weights.astype(jnp.bfloat16), values[r], preferred_element_type=jnp.float32
        ) + jnp.dot(
            fresh_weights.astype(jnp.bfloat16), fresh_value_ref[r],
            preferred_element_type=jnp.float32,
        )
        wide = jnp.where(own_head, wide, 0.0)
        steps = rows // heads
        sums[r, 0:steps, :] = jnp.sum(wide.reshape(steps, heads, width), axis=1)
        sums[r, steps : 2 * steps, :] = jnp.dot(
            spread, jnp.where(own_head, top, 0.0),
            precision=lax.Precision.HIGHEST, preferred_element_type=jnp.float32,
        )
        sums[r, 2 * steps : 3 * steps, :] = jnp.dot(
            spread, jnp.where(own_head, total, 0.0),
            precision=lax.Precision.HIGHEST, preferred_element_type=jnp.float32,
        )
        sums[r, 3 * steps :, :] = jnp.zeros((sums.shape[1] - 3 * steps, width), jnp.float32)

    pl.semaphore_wait(barrier, seq_size - 1 + tp_size - 1)

    def sums_copy(u, slot):
        return pltpu.make_async_remote_copy(
            sums, sums_land.at[slot], send_a.at[u], recv_a.at[slot],
            device_id=(u, t), device_id_type=mesh_type,
        )

    def along_tp(u, slot):
        return pltpu.make_async_remote_copy(
            ids_ref, ids_land.at[slot], send_b.at[u], recv_b.at[slot],
            device_id=(s, u), device_id_type=mesh_type,
        )

    for u in range(seq_size):
        @pl.when(s == u)
        def _():
            pltpu.make_async_copy(sums, sums_land.at[u], recv_a.at[u]).start()

        @pl.when(s != u)
        def _():
            sums_copy(u, s).start()
    for u in range(tp_size):
        @pl.when(t == u)
        def _():
            pltpu.make_async_copy(ids_ref, ids_land.at[u], recv_b.at[u]).start()

        @pl.when(t != u)
        def _():
            along_tp(u, t).start()

    for u in range(seq_size):
        @pl.when(s == u)
        def _():
            pltpu.make_async_copy(sums, sums_land.at[u], recv_a.at[u]).wait()

        @pl.when(s != u)
        def _():
            sums_copy(u, s).wait_send()
            sums_copy(u, u).wait_recv()
    for u in range(tp_size):
        @pl.when(t == u)
        def _():
            pltpu.make_async_copy(ids_ref, ids_land.at[u], recv_b.at[u]).wait()

        @pl.when(t != u)
        def _():
            along_tp(u, t).wait_send()
            along_tp(u, u).wait_recv()

    sums_out[...] = sums_land[...]
    ids_out[...] = ids_land[...]


def exchange(query, key_cache, value_cache, usable, fresh, fresh_ok, fresh_value, ids,
             seq_size, tp_size, scale):
    req_dev, rows, width = query.shape
    steps = rows // HEADS
    vmem = pl.BlockSpec(memory_space=pltpu.VMEM)
    return pl.pallas_call(
        functools.partial(exchange_kernel, seq_size, tp_size, scale),
        out_shape=(
            jax.ShapeDtypeStruct((seq_size, req_dev, 4 * steps, width), jnp.float32),
            jax.ShapeDtypeStruct((tp_size,) + ids.shape, ids.dtype),
        ),
        in_specs=[vmem, pl.BlockSpec(memory_space=pl.ANY), pl.BlockSpec(memory_space=pl.ANY)]
        + [vmem] * 5,
        out_specs=(vmem, vmem),
        scratch_shapes=[
            pltpu.VMEM(key_cache.shape, key_cache.dtype),
            pltpu.VMEM(value_cache.shape, value_cache.dtype),
            pltpu.VMEM((req_dev, 4 * steps, width), jnp.float32),
            pltpu.VMEM((seq_size, req_dev, 4 * steps, width), jnp.float32),
            pltpu.VMEM((tp_size,) + ids.shape, ids.dtype),
            pltpu.SemaphoreType.DMA((2, req_dev)),
            pltpu.SemaphoreType.DMA((seq_size,)),
            pltpu.SemaphoreType.DMA((seq_size,)),
            pltpu.SemaphoreType.DMA((tp_size,)),
            pltpu.SemaphoreType.DMA((tp_size,)),
        ],
        compiler_params=pltpu.CompilerParams(
            collective_id=0, has_side_effects=True, vmem_limit_bytes=48 * 1024 * 1024
        ),
    )(query, key_cache, value_cache, usable, fresh, fresh_ok, fresh_value, ids)


def expert_kernel(seq_size, tp_size, slices, sums_ref, hidden_ref, out_weight_hbm, gain_ref,
                  pick_in_ref, gate_hbm, up_hbm, down_hbm, pick_out_ref, out_ref, attn_ref,
                  normed_ref, out_weight_ref, gate_ref, up_ref, down_ref, load_sem, piece_ref,
                  context, everyone, part, recv, middle, outgoing, landing, send0, recv0,
                  send1, recv1, send3, recv3):
    mesh_type = pl.DeviceIdType.MESH
    s = lax.axis_index("seq")
    t = lax.axis_index("tp")
    g = t // slices
    j = t % slices
    chunk = recv.shape[2]
    halves = slices // seq_size
    src_seq = j // halves

    def dest(i):
        return (i // halves, g * slices + s * halves + i % halves)

    def is_self(i):
        return (i // halves == s) & (g * slices + s * halves + i % halves == t)

    barrier = pltpu.get_barrier_semaphore()
    for u in range(tp_size):
        @pl.when(t != u)
        def _():
            pl.semaphore_signal(barrier, inc=1, device_id=(s, u), device_id_type=mesh_type)
    for i in range(slices):
        @pl.when(i // halves != s)
        def _():
            pl.semaphore_signal(barrier, inc=1, device_id=dest(i), device_id_type=mesh_type)
    for k in range(slices):
        @pl.when((src_seq != s) & (k // halves != s))
        def _():
            pl.semaphore_signal(
                barrier, inc=1, device_id=(src_seq, g * slices + k), device_id_type=mesh_type
            )
    loads = [
        pltpu.make_async_copy(src_hbm, dst, load_sem.at[n])
        for n, (src_hbm, dst) in enumerate(
            [(out_weight_hbm, out_weight_ref), (gate_hbm, gate_ref), (up_hbm, up_ref),
             (down_hbm, down_ref)]
        )
    ]
    for copy in loads:
        copy.start()

    req_dev = sums_ref.shape[1]
    steps = sums_ref.shape[2] // 4
    context[...] = jnp.zeros_like(context)
    for r in range(req_dev):
        block_sums = [sums_ref[b, r, 0:steps, :] for b in range(seq_size)]
        block_max = [sums_ref[b, r, steps : 2 * steps, :] for b in range(seq_size)]
        block_totals = [sums_ref[b, r, 2 * steps : 3 * steps, :] for b in range(seq_size)]
        overall = block_max[0]
        for b in range(1, seq_size):
            overall = jnp.maximum(overall, block_max[b])
        numer = jnp.zeros_like(overall)
        denom = jnp.zeros_like(overall)
        for b in range(seq_size):
            factor = jnp.exp(block_max[b] - overall)
            numer = numer + factor * block_sums[b]
            denom = denom + factor * block_totals[b]
        context[r * steps : (r + 1) * steps, :] = numer / denom
    loads[0].wait()
    attention = jnp.dot(
        context[...].astype(jnp.bfloat16), out_weight_ref[...], preferred_element_type=jnp.float32
    )
    attn_ref[...] = attention
    residual = hidden_ref[...] + attention
    mean_square = jnp.mean(residual * residual, axis=1, keepdims=True)
    normed = (residual * lax.rsqrt(mean_square + norm_epsilon) * gain_ref[...]).astype(
        jnp.bfloat16
    )
    piece_ref[...] = normed
    normed_ref[...] = normed

    far = (seq_size - 1) * halves
    near = tp_size - 1 + far

    @pl.when(src_seq == s)
    def _():
        pl.semaphore_wait(barrier, near)

    @pl.when(src_seq != s)
    def _():
        pl.semaphore_wait(barrier, near + slices - halves)

    def gather(u, slot):
        return pltpu.make_async_remote_copy(
            piece_ref, everyone.at[slot], send0.at[u], recv0.at[slot],
            device_id=(s, u), device_id_type=mesh_type,
        )

    for u in range(tp_size):
        @pl.when(t == u)
        def _():
            pltpu.make_async_copy(piece_ref, everyone.at[u], recv0.at[u]).start()

        @pl.when(t != u)
        def _():
            gather(u, t).start()

    for u in range(tp_size):
        @pl.when(t == u)
        def _():
            pltpu.make_async_copy(piece_ref, everyone.at[u], recv0.at[u]).wait()

        @pl.when(t != u)
        def _():
            gather(u, t).wait_send()
            gather(u, u).wait_recv()

    for copy in loads[1:]:
        copy.wait()
    rows_in = everyone[...].reshape(-1, everyone.shape[2])
    buffer = jnp.dot(pick_in_ref[...], rows_in, preferred_element_type=jnp.float32).astype(
        jnp.bfloat16
    )
    contract = (((1,), (1,)), ((), ()))
    gate = lax.dot_general(buffer, gate_ref[...], contract, preferred_element_type=jnp.float32)
    upward = lax.dot_general(buffer, up_ref[...], contract, preferred_element_type=jnp.float32)
    inner = (jax.nn.gelu(gate) * upward).astype(jnp.bfloat16)
    part[...] = jnp.dot(inner, down_ref[...], preferred_element_type=jnp.float32)

    def stage1(i):
        return pltpu.make_async_remote_copy(
            part.at[:, pl.ds(i * chunk, chunk)],
            recv.at[j],
            send1.at[i],
            recv1.at[j],
            device_id=dest(i),
            device_id_type=mesh_type,
        )

    for i in range(slices):
        @pl.when(is_self(i))
        def _():
            pltpu.make_async_copy(part.at[:, pl.ds(i * chunk, chunk)], recv.at[j], recv1.at[j]).start()

        @pl.when(jnp.logical_not(is_self(i)))
        def _():
            stage1(i).start()

    for i in range(slices):
        @pl.when(jnp.logical_not(is_self(i)))
        def _():
            stage1(i).wait_send()

    for k in range(slices):
        from_self = (src_seq == s) & (k == j)

        @pl.when(from_self)
        def _():
            pltpu.make_async_copy(part.at[:, pl.ds(0, chunk)], recv.at[k], recv1.at[k]).wait()

        @pl.when(jnp.logical_not(from_self))
        def _():
            pltpu.make_async_remote_copy(
                part.at[:, pl.ds(0, chunk)],
                recv.at[k],
                send1.at[0],
                recv1.at[k],
                device_id=(src_seq, g * slices + k),
                device_id_type=mesh_type,
            ).wait_recv()

    total = recv[0]
    for k in range(1, slices):
        total = total + recv[k]
    middle[...] = total.astype(middle.dtype)

    picked = jnp.dot(
        pick_out_ref[...].reshape(-1, pick_out_ref.shape[2]),
        middle[...],
        preferred_element_type=jnp.float32,
    )
    outgoing[...] = picked.reshape(outgoing.shape).astype(outgoing.dtype)

    def stage3(u):
        return pltpu.make_async_remote_copy(
            outgoing.at[u], landing.at[t], send3.at[u], recv3.at[t],
            device_id=(s, u), device_id_type=mesh_type,
        )

    for u in range(tp_size):
        @pl.when(t == u)
        def _():
            pltpu.make_async_copy(outgoing.at[u], landing.at[u], recv3.at[u]).start()

        @pl.when(t != u)
        def _():
            stage3(u).start()

    for u in range(tp_size):
        @pl.when(t == u)
        def _():
            pltpu.make_async_copy(outgoing.at[u], landing.at[u], recv3.at[u]).wait()

        @pl.when(t != u)
        def _():
            stage3(u).wait_send()
            pltpu.make_async_remote_copy(
                outgoing.at[u], landing.at[u], send3.at[u], recv3.at[u],
                device_id=(s, u), device_id_type=mesh_type,
            ).wait_recv()

    out_ref[...] = landing[...]


def run_experts(sums, hidden, out_weight, gain, pick_in, gate_weight, up_weight, down_weight,
                pick_out, seq_size, tp_size, slices):
    tokens, width = hidden.shape
    rows = pick_in.shape[0]
    chunk = width // slices
    vmem = pl.BlockSpec(memory_space=pltpu.VMEM)
    hbm = pl.BlockSpec(memory_space=pl.ANY)
    return pl.pallas_call(
        functools.partial(expert_kernel, seq_size, tp_size, slices),
        out_shape=(
            jax.ShapeDtypeStruct((tp_size, tokens, chunk), jnp.bfloat16),
            jax.ShapeDtypeStruct((tokens, width), jnp.float32),
            jax.ShapeDtypeStruct((tokens, width), jnp.bfloat16),
        ),
        in_specs=[vmem, vmem, hbm, vmem, vmem, hbm, hbm, hbm, vmem],
        out_specs=(vmem, vmem, vmem),
        scratch_shapes=[
            pltpu.VMEM(out_weight.shape, out_weight.dtype),
            pltpu.VMEM(gate_weight.shape, gate_weight.dtype),
            pltpu.VMEM(up_weight.shape, up_weight.dtype),
            pltpu.VMEM(down_weight.shape, down_weight.dtype),
            pltpu.SemaphoreType.DMA((4,)),
            pltpu.VMEM((tokens, width), jnp.bfloat16),
            pltpu.VMEM((tokens, width), jnp.float32),
            pltpu.VMEM((tp_size, tokens, width), jnp.bfloat16),
            pltpu.VMEM((rows, width), jnp.float32),
            pltpu.VMEM((slices, rows, chunk), jnp.float32),
            pltpu.VMEM((rows, chunk), jnp.bfloat16),
            pltpu.VMEM((tp_size, tokens, chunk), jnp.bfloat16),
            pltpu.VMEM((tp_size, tokens, chunk), jnp.bfloat16),
            pltpu.SemaphoreType.DMA((tp_size,)),
            pltpu.SemaphoreType.DMA((tp_size,)),
            pltpu.SemaphoreType.DMA((slices,)),
            pltpu.SemaphoreType.DMA((slices,)),
            pltpu.SemaphoreType.DMA((tp_size,)),
            pltpu.SemaphoreType.DMA((tp_size,)),
        ],
        compiler_params=pltpu.CompilerParams(
            collective_id=1, has_side_effects=True
        ),
    )(sums, hidden, out_weight, gain, pick_in, gate_weight, up_weight, down_weight, pick_out)


def body(
    hidden_in,
    new_query,
    new_key,
    new_value,
    key_cache,
    value_cache,
    lengths,
    out_weight,
    norm_gain,
    router_weight,
    expert_ids,
    gate_weight,
    up_weight,
    down_weight,
):
    req_dev, steps, width = hidden_in.shape
    block = key_cache.shape[1]
    head_size = width // HEADS
    scale = head_size ** (-0.5)
    seq_index = lax.axis_index("seq")
    tp_index = lax.axis_index("tp")
    seq_size = lax.axis_size("seq")
    tp_size = lax.axis_size("tp")
    rows = steps * HEADS
    own = req_dev * steps

    head_mask = (jnp.arange(width) // head_size)[None, :] == jnp.arange(HEADS)[:, None]
    q_wide = jnp.where(head_mask[None, None], new_query[:, :, None, :], 0).reshape(
        req_dev, rows, width
    )
    positions = seq_index * block + jnp.arange(block, dtype=jnp.int32)
    usable = (positions[None, :] < lengths[:, None]).astype(jnp.float32)
    usable = jnp.broadcast_to(usable[:, None, :], (req_dev, 8, block))
    fresh_scores = (
        jnp.einsum("rqd,rsd->rqs", q_wide, new_key, preferred_element_type=jnp.float32) * scale
    )
    causal = (
        (jnp.arange(rows)[:, None] // HEADS) >= jnp.arange(steps)[None, :]
    ) & (seq_index == 0)
    fresh_scores = jnp.where(causal, fresh_scores, masked_score)
    fresh_scores = jnp.pad(
        fresh_scores, ((0, 0), (0, 0), (0, 128 - steps)), constant_values=masked_score
    )
    fresh_ok = jnp.pad(
        jnp.broadcast_to(causal, (req_dev, rows, steps)).astype(jnp.float32),
        ((0, 0), (0, 0), (0, 128 - steps)),
    )
    fresh_value = jnp.pad(new_value, ((0, 0), (0, 128 - steps), (0, 0)))
    id_count = expert_ids.size
    id_rows = 8
    id_piece = jnp.pad(expert_ids.reshape(1, id_count), ((0, id_rows - 1), (0, 128 - id_count)))
    block_sums, all_id_pieces = exchange(
        q_wide, key_cache, value_cache, usable, fresh_scores, fresh_ok, fresh_value, id_piece,
        seq_size, tp_size, scale,
    )
    all_ids = all_id_pieces[:, 0, :id_count].reshape(tp_size * req_dev, steps, -1)
    feature_block = width // seq_size
    experts = router_weight.shape[1]
    topk = expert_ids.shape[2]
    requests = req_dev * tp_size
    capacity = (5 * requests * topk + 4 * experts - 1) // (4 * experts)
    expert_range = jnp.arange(experts, dtype=jnp.int32)
    slices = seq_size * tp_size // experts
    groups = tp_size // slices
    halves = slices // seq_size
    padded = 8 * ((steps * capacity + 7) // 8)
    tokens = 16 * ((own + 15) // 16)

    onehot = all_ids[..., None] == expert_range
    hits = jnp.sum(onehot.astype(jnp.int32), axis=2)
    earlier = jnp.cumsum(hits, axis=0) - hits
    all_slots = jnp.sum(jnp.where(onehot, earlier[:, :, None, :], 0), axis=3)
    row_of = jnp.arange(steps, dtype=jnp.int32)[None, :, None] * capacity + all_slots

    def rows_for(expert):
        hit = (all_ids == expert) & (all_slots < capacity)
        chosen_rows = jnp.any(
            hit[..., None] & (row_of[..., None] == jnp.arange(padded)), axis=2
        ).reshape(tp_size, own, padded)
        return jnp.pad(chosen_rows, ((0, 0), (0, tokens - own), (0, 0))).astype(jnp.bfloat16)

    mine = (seq_index * tp_size + tp_index) // slices
    pick_in = rows_for(mine).reshape(tp_size * tokens, padded).T
    held = ((tp_index % slices) // halves) * groups + tp_index // slices
    pick_out = rows_for(held)
    hidden = jnp.pad(
        hidden_in.astype(jnp.float32).reshape(own, width), ((0, tokens - own), (0, 0))
    )
    landed, attention, normed = run_experts(
        block_sums, hidden, out_weight, norm_gain.reshape(1, width), pick_in, gate_weight,
        up_weight, down_weight, pick_out, seq_size, tp_size, slices,
    )
    attention = attention[:own].reshape(req_dev, steps, width)
    normed = normed[:own].reshape(req_dev, steps, width)
    attn_out = lax.dynamic_slice_in_dim(
        attention, seq_index * feature_block, feature_block, 2
    ).astype(jnp.bfloat16)
    residual = hidden_in.astype(jnp.float32) + attention

    logits = jnp.einsum("rtd,de->rte", normed, router_weight, preferred_element_type=jnp.float32)
    own_hot = expert_ids[..., None] == expert_range
    chosen = jnp.sum(jnp.where(own_hot, logits[:, :, None, :], 0.0), axis=3)
    share = 1.0 / (1.0 + jnp.exp(chosen[:, :, ::-1] - chosen))
    own_slots = lax.dynamic_slice_in_dim(all_slots, tp_index * req_dev, req_dev, 0)
    weight = jnp.where(own_slots < capacity, share, 0.0)
    slot_expert = (jnp.arange(tp_size // halves) % (tp_size // (groups * halves))) * groups + (
        jnp.arange(tp_size // halves) // (tp_size // (groups * halves))
    )
    per_slot = jnp.sum(
        jnp.where(expert_ids[..., None] == slot_expert, weight[..., None], 0.0), axis=2
    ).reshape(own, tp_size // halves)
    landed = landed.astype(jnp.float32).reshape(tp_size // halves, halves, tokens, feature_block // halves)
    mixture = jnp.einsum(
        "ia,ahif->ihf", per_slot, landed[:, :, :own], precision=lax.Precision.HIGHEST
    ).reshape(req_dev, steps, feature_block)
    own_residual = lax.dynamic_slice_in_dim(residual, seq_index * feature_block, feature_block, 2)
    layer_out = (own_residual + mixture).astype(jnp.bfloat16)
    return (attn_out, layer_out)


def solution(mesh):

    return jax.shard_map(
        body,
        mesh=mesh,
        in_specs=(
            P("tp", None, None),
            P("tp", None, None),
            P("tp", None, None),
            P("tp", None, None),
            P("tp", "seq", None),
            P("tp", "seq", None),
            P("tp"),
            P(),
            P(),
            P(),
            P("tp", None, None),
            P(("seq", "tp"), None),
            P(("seq", "tp"), None),
            P(("seq", "tp"), None),
        ),
        out_specs=(P("tp", None, "seq"), P("tp", None, "seq")),
        check_vma=False,
    )
```

```python
import functools

import jax
import jax.numpy as jnp
from jax import lax
from jax.experimental import pallas as pl
from jax.experimental.pallas import tpu as pltpu
from jax.sharding import PartitionSpec as P

HEADS = 16


masked_score = -1e30
norm_epsilon = 1e-06


def exchange_kernel(seq_size, tp_size, scale, query_ref, key_hbm, value_hbm, usable_ref,
                    fresh_ref, fresh_ok_ref, fresh_value_ref, ids_ref, sums_out,
                    ids_out, keys, values, sums, sums_land, ids_land,
                    load_sem, send_a, recv_a, send_b, recv_b):
    mesh_type = pl.DeviceIdType.MESH
    s = lax.axis_index("seq")
    t = lax.axis_index("tp")
    req_dev, rows, width = query_ref.shape
    heads = HEADS

    barrier = pltpu.get_barrier_semaphore()
    for u in range(seq_size):
        @pl.when(s != u)
        def _():
            pl.semaphore_signal(barrier, inc=1, device_id=(u, t), device_id_type=mesh_type)
    for u in range(tp_size):
        @pl.when(t != u)
        def _():
            pl.semaphore_signal(barrier, inc=1, device_id=(s, u), device_id_type=mesh_type)

    loads = []
    for r in range(req_dev):
        loads.append(pltpu.make_async_copy(key_hbm.at[r], keys.at[r], load_sem.at[0, r]))
        loads.append(pltpu.make_async_copy(value_hbm.at[r], values.at[r], load_sem.at[1, r]))
    for copy in loads:
        copy.start()

    head_of = lax.broadcasted_iota(jnp.int32, (rows, width), 1) // (width // heads)
    row_head = lax.broadcasted_iota(jnp.int32, (rows, width), 0) % heads
    own_head = head_of == row_head
    spread = (
        lax.broadcasted_iota(jnp.int32, (rows // heads, rows), 1) // heads
        == lax.broadcasted_iota(jnp.int32, (rows // heads, rows), 0)
    ).astype(jnp.float32)
    contract = (((1,), (1,)), ((), ()))
    for r in range(req_dev):
        loads[2 * r].wait()
        scores = lax.dot_general(
            query_ref[r], keys[r], contract, preferred_element_type=jnp.float32
        ) * scale
        usable = usable_ref[r, 0:1, :] > 0.5
        scores = jnp.where(usable, scores, masked_score)
        fresh = fresh_ref[r]
        fresh_ok = fresh_ok_ref[r] > 0.5
        top = jnp.maximum(
            jnp.max(scores, axis=1, keepdims=True), jnp.max(fresh, axis=1, keepdims=True)
        )
        weights = jnp.where(usable, jnp.exp(scores - top), 0.0)
        fresh_weights = jnp.where(fresh_ok, jnp.exp(fresh - top), 0.0)
        total = jnp.sum(weights, axis=1, keepdims=True) + jnp.sum(
            fresh_weights, axis=1, keepdims=True
        )
        loads[2 * r + 1].wait()
        wide = jnp.dot(
            weights.astype(jnp.bfloat16), values[r], preferred_element_type=jnp.float32
        ) + jnp.dot(
            fresh_weights.astype(jnp.bfloat16), fresh_value_ref[r],
            preferred_element_type=jnp.float32,
        )
        wide = jnp.where(own_head, wide, 0.0)
        steps = rows // heads
        sums[r, 0:steps, :] = jnp.sum(wide.reshape(steps, heads, width), axis=1)
        sums[r, steps : 2 * steps, :] = jnp.dot(
            spread, jnp.where(own_head, top, 0.0),
            precision=lax.Precision.HIGHEST, preferred_element_type=jnp.float32,
        )
        sums[r, 2 * steps : 3 * steps, :] = jnp.dot(
            spread, jnp.where(own_head, total, 0.0),
            precision=lax.Precision.HIGHEST, preferred_element_type=jnp.float32,
        )
        sums[r, 3 * steps :, :] = jnp.zeros((sums.shape[1] - 3 * steps, width), jnp.float32)

    pl.semaphore_wait(barrier, seq_size - 1 + tp_size - 1)

    def sums_copy(u, slot):
        return pltpu.make_async_remote_copy(
            sums, sums_land.at[slot], send_a.at[u], recv_a.at[slot],
            device_id=(u, t), device_id_type=mesh_type,
        )

    def along_tp(u, slot):
        return pltpu.make_async_remote_copy(
            ids_ref, ids_land.at[slot], send_b.at[u], recv_b.at[slot],
            device_id=(s, u), device_id_type=mesh_type,
        )

    for u in range(seq_size):
        @pl.when(s == u)
        def _():
            pltpu.make_async_copy(sums, sums_land.at[u], recv_a.at[u]).start()

        @pl.when(s != u)
        def _():
            sums_copy(u, s).start()
    for u in range(tp_size):
        @pl.when(t == u)
        def _():
            pltpu.make_async_copy(ids_ref, ids_land.at[u], recv_b.at[u]).start()

        @pl.when(t != u)
        def _():
            along_tp(u, t).start()

    for u in range(seq_size):
        @pl.when(s == u)
        def _():
            pltpu.make_async_copy(sums, sums_land.at[u], recv_a.at[u]).wait()

        @pl.when(s != u)
        def _():
            sums_copy(u, s).wait_send()
            sums_copy(u, u).wait_recv()
    for u in range(tp_size):
        @pl.when(t == u)
        def _():
            pltpu.make_async_copy(ids_ref, ids_land.at[u], recv_b.at[u]).wait()

        @pl.when(t != u)
        def _():
            along_tp(u, t).wait_send()
            along_tp(u, u).wait_recv()

    sums_out[...] = sums_land[...]
    ids_out[...] = ids_land[...]


def exchange(query, key_cache, value_cache, usable, fresh, fresh_ok, fresh_value, ids,
             seq_size, tp_size, scale):
    req_dev, rows, width = query.shape
    steps = rows // HEADS
    vmem = pl.BlockSpec(memory_space=pltpu.VMEM)
    return pl.pallas_call(
        functools.partial(exchange_kernel, seq_size, tp_size, scale),
        out_shape=(
            jax.ShapeDtypeStruct((seq_size, req_dev, 4 * steps, width), jnp.float32),
            jax.ShapeDtypeStruct((tp_size,) + ids.shape, ids.dtype),
        ),
        in_specs=[vmem, pl.BlockSpec(memory_space=pl.ANY), pl.BlockSpec(memory_space=pl.ANY)]
        + [vmem] * 5,
        out_specs=(vmem, vmem),
        scratch_shapes=[
            pltpu.VMEM(key_cache.shape, key_cache.dtype),
            pltpu.VMEM(value_cache.shape, value_cache.dtype),
            pltpu.VMEM((req_dev, 4 * steps, width), jnp.float32),
            pltpu.VMEM((seq_size, req_dev, 4 * steps, width), jnp.float32),
            pltpu.VMEM((tp_size,) + ids.shape, ids.dtype),
            pltpu.SemaphoreType.DMA((2, req_dev)),
            pltpu.SemaphoreType.DMA((seq_size,)),
            pltpu.SemaphoreType.DMA((seq_size,)),
            pltpu.SemaphoreType.DMA((tp_size,)),
            pltpu.SemaphoreType.DMA((tp_size,)),
        ],
        compiler_params=pltpu.CompilerParams(
            collective_id=0, has_side_effects=True, vmem_limit_bytes=48 * 1024 * 1024
        ),
    )(query, key_cache, value_cache, usable, fresh, fresh_ok, fresh_value, ids)


def expert_kernel(seq_size, tp_size, slices, sums_ref, hidden_ref, out_weight_hbm, gain_ref,
                  pick_in_ref, gate_hbm, up_hbm, down_hbm, pick_out_ref, out_ref, attn_ref,
                  normed_ref, out_weight_ref, gate_ref, up_ref, down_ref, load_sem, piece_ref,
                  context, everyone, part, recv, middle, outgoing, landing, send0, recv0,
                  send1, recv1, send3, recv3):
    mesh_type = pl.DeviceIdType.MESH
    s = lax.axis_index("seq")
    t = lax.axis_index("tp")
    g = t // slices
    j = t % slices
    chunk = recv.shape[2]
    halves = slices // seq_size
    src_seq = j // halves

    def dest(i):
        return (i // halves, g * slices + s * halves + i % halves)

    def is_self(i):
        return (i // halves == s) & (g * slices + s * halves + i % halves == t)

    barrier = pltpu.get_barrier_semaphore()
    for u in range(tp_size):
        @pl.when(t != u)
        def _():
            pl.semaphore_signal(barrier, inc=1, device_id=(s, u), device_id_type=mesh_type)
    for i in range(slices):
        @pl.when(i // halves != s)
        def _():
            pl.semaphore_signal(barrier, inc=1, device_id=dest(i), device_id_type=mesh_type)
    for k in range(slices):
        @pl.when((src_seq != s) & (k // halves != s))
        def _():
            pl.semaphore_signal(
                barrier, inc=1, device_id=(src_seq, g * slices + k), device_id_type=mesh_type
            )
    loads = [
        pltpu.make_async_copy(src_hbm, dst, load_sem.at[n])
        for n, (src_hbm, dst) in enumerate(
            [(out_weight_hbm, out_weight_ref), (gate_hbm, gate_ref), (up_hbm, up_ref),
             (down_hbm, down_ref)]
        )
    ]
    for copy in loads:
        copy.start()

    req_dev = sums_ref.shape[1]
    steps = sums_ref.shape[2] // 4
    context[...] = jnp.zeros_like(context)
    for r in range(req_dev):
        block_sums = [sums_ref[b, r, 0:steps, :] for b in range(seq_size)]
        block_max = [sums_ref[b, r, steps : 2 * steps, :] for b in range(seq_size)]
        block_totals = [sums_ref[b, r, 2 * steps : 3 * steps, :] for b in range(seq_size)]
        overall = block_max[0]
        for b in range(1, seq_size):
            overall = jnp.maximum(overall, block_max[b])
        numer = jnp.zeros_like(overall)
        denom = jnp.zeros_like(overall)
        for b in range(seq_size):
            factor = jnp.exp(block_max[b] - overall)
            numer = numer + factor * block_sums[b]
            denom = denom + factor * block_totals[b]
        context[r * steps : (r + 1) * steps, :] = numer / denom
    loads[0].wait()
    attention = jnp.dot(
        context[...].astype(jnp.bfloat16), out_weight_ref[...], preferred_element_type=jnp.float32
    )
    for r in range(req_dev):
        attn_ref[r] = attention[r * steps : (r + 1) * steps, :]
    residual = hidden_ref[...] + attention
    mean_square = jnp.mean(residual * residual, axis=1, keepdims=True)
    normed = (residual * lax.rsqrt(mean_square + norm_epsilon) * gain_ref[...]).astype(
        jnp.bfloat16
    )
    piece_ref[...] = normed
    for r in range(req_dev):
        normed_ref[r] = normed[r * steps : (r + 1) * steps, :]

    far = (seq_size - 1) * halves
    near = tp_size - 1 + far

    @pl.when(src_seq == s)
    def _():
        pl.semaphore_wait(barrier, near)

    @pl.when(src_seq != s)
    def _():
        pl.semaphore_wait(barrier, near + slices - halves)

    def gather(u, slot):
        return pltpu.make_async_remote_copy(
            piece_ref, everyone.at[slot], send0.at[u], recv0.at[slot],
            device_id=(s, u), device_id_type=mesh_type,
        )

    for u in range(tp_size):
        @pl.when(t == u)
        def _():
            pltpu.make_async_copy(piece_ref, everyone.at[u], recv0.at[u]).start()

        @pl.when(t != u)
        def _():
            gather(u, t).start()

    for u in range(tp_size):
        @pl.when(t == u)
        def _():
            pltpu.make_async_copy(piece_ref, everyone.at[u], recv0.at[u]).wait()

        @pl.when(t != u)
        def _():
            gather(u, t).wait_send()
            gather(u, u).wait_recv()

    for copy in loads[1:]:
        copy.wait()
    rows_in = everyone[...].reshape(-1, everyone.shape[2])
    buffer = jnp.dot(pick_in_ref[...], rows_in, preferred_element_type=jnp.float32).astype(
        jnp.bfloat16
    )
    contract = (((1,), (1,)), ((), ()))
    gate = lax.dot_general(buffer, gate_ref[...], contract, preferred_element_type=jnp.float32)
    upward = lax.dot_general(buffer, up_ref[...], contract, preferred_element_type=jnp.float32)
    inner = (jax.nn.gelu(gate) * upward).astype(jnp.bfloat16)
    part[...] = jnp.dot(inner, down_ref[...], preferred_element_type=jnp.float32)

    def stage1(i):
        return pltpu.make_async_remote_copy(
            part.at[:, pl.ds(i * chunk, chunk)],
            recv.at[j],
            send1.at[i],
            recv1.at[j],
            device_id=dest(i),
            device_id_type=mesh_type,
        )

    for i in range(slices):
        @pl.when(is_self(i))
        def _():
            pltpu.make_async_copy(part.at[:, pl.ds(i * chunk, chunk)], recv.at[j], recv1.at[j]).start()

        @pl.when(jnp.logical_not(is_self(i)))
        def _():
            stage1(i).start()

    for i in range(slices):
        @pl.when(jnp.logical_not(is_self(i)))
        def _():
            stage1(i).wait_send()

    for k in range(slices):
        from_self = (src_seq == s) & (k == j)

        @pl.when(from_self)
        def _():
            pltpu.make_async_copy(part.at[:, pl.ds(0, chunk)], recv.at[k], recv1.at[k]).wait()

        @pl.when(jnp.logical_not(from_self))
        def _():
            pltpu.make_async_remote_copy(
                part.at[:, pl.ds(0, chunk)],
                recv.at[k],
                send1.at[0],
                recv1.at[k],
                device_id=(src_seq, g * slices + k),
                device_id_type=mesh_type,
            ).wait_recv()

    total = recv[0]
    for k in range(1, slices):
        total = total + recv[k]
    middle[...] = total.astype(middle.dtype)

    picked = jnp.dot(
        pick_out_ref[...].reshape(-1, pick_out_ref.shape[2]),
        middle[...],
        preferred_element_type=jnp.float32,
    )
    outgoing[...] = picked.reshape(outgoing.shape).astype(outgoing.dtype)

    def stage3(u):
        return pltpu.make_async_remote_copy(
            outgoing.at[u], landing.at[t], send3.at[u], recv3.at[t],
            device_id=(s, u), device_id_type=mesh_type,
        )

    for u in range(tp_size):
        @pl.when(t == u)
        def _():
            pltpu.make_async_copy(outgoing.at[u], landing.at[u], recv3.at[u]).start()

        @pl.when(t != u)
        def _():
            stage3(u).start()

    for u in range(tp_size):
        @pl.when(t == u)
        def _():
            pltpu.make_async_copy(outgoing.at[u], landing.at[u], recv3.at[u]).wait()

        @pl.when(t != u)
        def _():
            stage3(u).wait_send()
            pltpu.make_async_remote_copy(
                outgoing.at[u], landing.at[u], send3.at[u], recv3.at[u],
                device_id=(s, u), device_id_type=mesh_type,
            ).wait_recv()

    out_ref[...] = landing[...]


def run_experts(sums, hidden, out_weight, gain, pick_in, gate_weight, up_weight, down_weight,
                pick_out, seq_size, tp_size, slices):
    tokens, width = hidden.shape
    rows = pick_in.shape[0]
    chunk = width // slices
    vmem = pl.BlockSpec(memory_space=pltpu.VMEM)
    hbm = pl.BlockSpec(memory_space=pl.ANY)
    return pl.pallas_call(
        functools.partial(expert_kernel, seq_size, tp_size, slices),
        out_shape=(
            jax.ShapeDtypeStruct((tp_size, tokens, chunk), jnp.bfloat16),
            jax.ShapeDtypeStruct((sums.shape[1], sums.shape[2] // 4, width), jnp.float32),
            jax.ShapeDtypeStruct((sums.shape[1], sums.shape[2] // 4, width), jnp.bfloat16),
        ),
        in_specs=[vmem, vmem, hbm, vmem, vmem, hbm, hbm, hbm, vmem],
        out_specs=(vmem, vmem, vmem),
        scratch_shapes=[
            pltpu.VMEM(out_weight.shape, out_weight.dtype),
            pltpu.VMEM(gate_weight.shape, gate_weight.dtype),
            pltpu.VMEM(up_weight.shape, up_weight.dtype),
            pltpu.VMEM(down_weight.shape, down_weight.dtype),
            pltpu.SemaphoreType.DMA((4,)),
            pltpu.VMEM((tokens, width), jnp.bfloat16),
            pltpu.VMEM((tokens, width), jnp.float32),
            pltpu.VMEM((tp_size, tokens, width), jnp.bfloat16),
            pltpu.VMEM((rows, width), jnp.float32),
            pltpu.VMEM((slices, rows, chunk), jnp.float32),
            pltpu.VMEM((rows, chunk), jnp.bfloat16),
            pltpu.VMEM((tp_size, tokens, chunk), jnp.bfloat16),
            pltpu.VMEM((tp_size, tokens, chunk), jnp.bfloat16),
            pltpu.SemaphoreType.DMA((tp_size,)),
            pltpu.SemaphoreType.DMA((tp_size,)),
            pltpu.SemaphoreType.DMA((slices,)),
            pltpu.SemaphoreType.DMA((slices,)),
            pltpu.SemaphoreType.DMA((tp_size,)),
            pltpu.SemaphoreType.DMA((tp_size,)),
        ],
        compiler_params=pltpu.CompilerParams(
            collective_id=1, has_side_effects=True
        ),
    )(sums, hidden, out_weight, gain, pick_in, gate_weight, up_weight, down_weight, pick_out)


def body(
    hidden_in,
    new_query,
    new_key,
    new_value,
    key_cache,
    value_cache,
    lengths,
    out_weight,
    norm_gain,
    router_weight,
    expert_ids,
    gate_weight,
    up_weight,
    down_weight,
):
    req_dev, steps, width = hidden_in.shape
    block = key_cache.shape[1]
    head_size = width // HEADS
    scale = head_size ** (-0.5)
    seq_index = lax.axis_index("seq")
    tp_index = lax.axis_index("tp")
    seq_size = lax.axis_size("seq")
    tp_size = lax.axis_size("tp")
    rows = steps * HEADS
    own = req_dev * steps

    head_mask = (jnp.arange(width) // head_size)[None, :] == jnp.arange(HEADS)[:, None]
    q_wide = jnp.where(head_mask[None, None], new_query[:, :, None, :], 0).reshape(
        req_dev, rows, width
    )
    positions = seq_index * block + jnp.arange(block, dtype=jnp.int32)
    usable = (positions[None, :] < lengths[:, None]).astype(jnp.float32)
    usable = jnp.broadcast_to(usable[:, None, :], (req_dev, 8, block))
    fresh_scores = (
        jnp.einsum("rqd,rsd->rqs", q_wide, new_key, preferred_element_type=jnp.float32) * scale
    )
    causal = (
        (jnp.arange(rows)[:, None] // HEADS) >= jnp.arange(steps)[None, :]
    ) & (seq_index == 0)
    fresh_scores = jnp.where(causal, fresh_scores, masked_score)
    fresh_scores = jnp.pad(
        fresh_scores, ((0, 0), (0, 0), (0, 128 - steps)), constant_values=masked_score
    )
    fresh_ok = jnp.pad(
        jnp.broadcast_to(causal, (req_dev, rows, steps)).astype(jnp.float32),
        ((0, 0), (0, 0), (0, 128 - steps)),
    )
    fresh_value = jnp.pad(new_value, ((0, 0), (0, 128 - steps), (0, 0)))
    id_count = expert_ids.size
    id_rows = 8
    id_piece = jnp.pad(expert_ids.reshape(1, id_count), ((0, id_rows - 1), (0, 128 - id_count)))
    block_sums, all_id_pieces = exchange(
        q_wide, key_cache, value_cache, usable, fresh_scores, fresh_ok, fresh_value, id_piece,
        seq_size, tp_size, scale,
    )
    all_ids = all_id_pieces[:, 0, :id_count].reshape(tp_size * req_dev, steps, -1)
    feature_block = width // seq_size
    experts = router_weight.shape[1]
    topk = expert_ids.shape[2]
    requests = req_dev * tp_size
    capacity = (5 * requests * topk + 4 * experts - 1) // (4 * experts)
    expert_range = jnp.arange(experts, dtype=jnp.int32)
    slices = seq_size * tp_size // experts
    groups = tp_size // slices
    halves = slices // seq_size
    padded = 8 * ((steps * capacity + 7) // 8)
    tokens = 16 * ((own + 15) // 16)

    onehot = all_ids[..., None] == expert_range
    hits = jnp.sum(onehot.astype(jnp.int32), axis=2)
    earlier = jnp.cumsum(hits, axis=0) - hits
    all_slots = jnp.sum(jnp.where(onehot, earlier[:, :, None, :], 0), axis=3)
    row_of = jnp.arange(steps, dtype=jnp.int32)[None, :, None] * capacity + all_slots

    def rows_for(expert):
        hit = (all_ids == expert) & (all_slots < capacity)
        chosen_rows = jnp.any(
            hit[..., None] & (row_of[..., None] == jnp.arange(padded)), axis=2
        ).reshape(tp_size, own, padded)
        return jnp.pad(chosen_rows, ((0, 0), (0, tokens - own), (0, 0))).astype(jnp.bfloat16)

    mine = (seq_index * tp_size + tp_index) // slices
    pick_in = rows_for(mine).reshape(tp_size * tokens, padded).T
    held = ((tp_index % slices) // halves) * groups + tp_index // slices
    pick_out = rows_for(held)
    hidden = jnp.pad(
        hidden_in.astype(jnp.float32).reshape(own, width), ((0, tokens - own), (0, 0))
    )
    landed, attention, normed = run_experts(
        block_sums, hidden, out_weight, norm_gain.reshape(1, width), pick_in, gate_weight,
        up_weight, down_weight, pick_out, seq_size, tp_size, slices,
    )
    attn_out = lax.dynamic_slice_in_dim(
        attention, seq_index * feature_block, feature_block, 2
    ).astype(jnp.bfloat16)
    residual = hidden_in.astype(jnp.float32) + attention

    logits = jnp.einsum("rtd,de->rte", normed, router_weight, preferred_element_type=jnp.float32)
    own_hot = expert_ids[..., None] == expert_range
    chosen = jnp.sum(jnp.where(own_hot, logits[:, :, None, :], 0.0), axis=3)
    share = 1.0 / (1.0 + jnp.exp(chosen[:, :, ::-1] - chosen))
    own_slots = lax.dynamic_slice_in_dim(all_slots, tp_index * req_dev, req_dev, 0)
    weight = jnp.where(own_slots < capacity, share, 0.0)
    slot_expert = (jnp.arange(tp_size // halves) % (tp_size // (groups * halves))) * groups + (
        jnp.arange(tp_size // halves) // (tp_size // (groups * halves))
    )
    per_slot = jnp.sum(
        jnp.where(expert_ids[..., None] == slot_expert, weight[..., None], 0.0), axis=2
    ).reshape(own, tp_size // halves)
    landed = landed.astype(jnp.float32).reshape(tp_size // halves, halves, tokens, feature_block // halves)
    mixture = jnp.einsum(
        "ia,ahif->ihf", per_slot, landed[:, :, :own], precision=lax.Precision.HIGHEST
    ).reshape(req_dev, steps, feature_block)
    own_residual = lax.dynamic_slice_in_dim(residual, seq_index * feature_block, feature_block, 2)
    layer_out = (own_residual + mixture).astype(jnp.bfloat16)
    return (attn_out, layer_out)


def solution(mesh):

    return jax.shard_map(
        body,
        mesh=mesh,
        in_specs=(
            P("tp", None, None),
            P("tp", None, None),
            P("tp", None, None),
            P("tp", None, None),
            P("tp", "seq", None),
            P("tp", "seq", None),
            P("tp"),
            P(),
            P(),
            P(),
            P("tp", None, None),
            P(("seq", "tp"), None),
            P(("seq", "tp"), None),
            P(("seq", "tp"), None),
        ),
        out_specs=(P("tp", None, "seq"), P("tp", None, "seq")),
        check_vma=False,
    )
```

```python
import functools

import jax
import jax.numpy as jnp
from jax import lax
from jax.experimental import pallas as pl
from jax.experimental.pallas import tpu as pltpu
from jax.sharding import PartitionSpec as P

HEADS = 16


masked_score = -1e30
norm_epsilon = 1e-06


def exchange_kernel(seq_size, tp_size, scale, query_ref, key_hbm, value_hbm, usable_ref,
                    fresh_ref, fresh_ok_ref, fresh_value_ref, ids_ref, sums_out,
                    ids_out, keys, values, sums, sums_land, ids_land,
                    load_sem, send_a, recv_a, send_b, recv_b):
    mesh_type = pl.DeviceIdType.MESH
    s = lax.axis_index("seq")
    t = lax.axis_index("tp")
    req_dev, rows, width = query_ref.shape
    heads = HEADS

    barrier = pltpu.get_barrier_semaphore()
    for u in range(seq_size):
        @pl.when(s != u)
        def _():
            pl.semaphore_signal(barrier, inc=1, device_id=(u, t), device_id_type=mesh_type)
    for u in range(tp_size):
        @pl.when(t != u)
        def _():
            pl.semaphore_signal(barrier, inc=1, device_id=(s, u), device_id_type=mesh_type)

    loads = []
    for r in range(req_dev):
        loads.append(pltpu.make_async_copy(key_hbm.at[r], keys.at[r], load_sem.at[0, r]))
        loads.append(pltpu.make_async_copy(value_hbm.at[r], values.at[r], load_sem.at[1, r]))
    for copy in loads:
        copy.start()

    head_of = lax.broadcasted_iota(jnp.int32, (rows, width), 1) // (width // heads)
    row_head = lax.broadcasted_iota(jnp.int32, (rows, width), 0) % heads
    own_head = head_of == row_head
    spread = (
        lax.broadcasted_iota(jnp.int32, (rows // heads, rows), 1) // heads
        == lax.broadcasted_iota(jnp.int32, (rows // heads, rows), 0)
    ).astype(jnp.float32)
    contract = (((1,), (1,)), ((), ()))
    for r in range(req_dev):
        loads[2 * r].wait()
        scores = lax.dot_general(
            query_ref[r], keys[r], contract, preferred_element_type=jnp.float32
        ) * scale
        usable = usable_ref[r, 0:1, :] > 0.5
        scores = jnp.where(usable, scores, masked_score)
        fresh = fresh_ref[r]
        fresh_ok = fresh_ok_ref[r] > 0.5
        top = jnp.maximum(
            jnp.max(scores, axis=1, keepdims=True), jnp.max(fresh, axis=1, keepdims=True)
        )
        weights = jnp.where(usable, jnp.exp(scores - top), 0.0)
        fresh_weights = jnp.where(fresh_ok, jnp.exp(fresh - top), 0.0)
        total = jnp.sum(weights, axis=1, keepdims=True) + jnp.sum(
            fresh_weights, axis=1, keepdims=True
        )
        loads[2 * r + 1].wait()
        wide = jnp.dot(
            weights.astype(jnp.bfloat16), values[r], preferred_element_type=jnp.float32
        ) + jnp.dot(
            fresh_weights.astype(jnp.bfloat16), fresh_value_ref[r],
            preferred_element_type=jnp.float32,
        )
        wide = jnp.where(own_head, wide, 0.0)
        steps = rows // heads
        sums[r, 0:steps, :] = jnp.sum(wide.reshape(steps, heads, width), axis=1)
        sums[r, steps : 2 * steps, :] = jnp.dot(
            spread, jnp.where(own_head, top, 0.0),
            precision=lax.Precision.HIGHEST, preferred_element_type=jnp.float32,
        )
        sums[r, 2 * steps : 3 * steps, :] = jnp.dot(
            spread, jnp.where(own_head, total, 0.0),
            precision=lax.Precision.HIGHEST, preferred_element_type=jnp.float32,
        )
        sums[r, 3 * steps :, :] = jnp.zeros((sums.shape[1] - 3 * steps, width), jnp.float32)

    pl.semaphore_wait(barrier, seq_size - 1 + tp_size - 1)

    def sums_copy(u, slot):
        return pltpu.make_async_remote_copy(
            sums, sums_land.at[slot], send_a.at[u], recv_a.at[slot],
            device_id=(u, t), device_id_type=mesh_type,
        )

    def along_tp(u, slot):
        return pltpu.make_async_remote_copy(
            ids_ref, ids_land.at[slot], send_b.at[u], recv_b.at[slot],
            device_id=(s, u), device_id_type=mesh_type,
        )

    for u in range(seq_size):
        @pl.when(s == u)
        def _():
            pltpu.make_async_copy(sums, sums_land.at[u], recv_a.at[u]).start()

        @pl.when(s != u)
        def _():
            sums_copy(u, s).start()
    for u in range(tp_size):
        @pl.when(t == u)
        def _():
            pltpu.make_async_copy(ids_ref, ids_land.at[u], recv_b.at[u]).start()

        @pl.when(t != u)
        def _():
            along_tp(u, t).start()

    for u in range(seq_size):
        @pl.when(s == u)
        def _():
            pltpu.make_async_copy(sums, sums_land.at[u], recv_a.at[u]).wait()

        @pl.when(s != u)
        def _():
            sums_copy(u, s).wait_send()
            sums_copy(u, u).wait_recv()
    for u in range(tp_size):
        @pl.when(t == u)
        def _():
            pltpu.make_async_copy(ids_ref, ids_land.at[u], recv_b.at[u]).wait()

        @pl.when(t != u)
        def _():
            along_tp(u, t).wait_send()
            along_tp(u, u).wait_recv()

    sums_out[...] = sums_land[...]
    ids_out[...] = ids_land[...]


def exchange(query, key_cache, value_cache, usable, fresh, fresh_ok, fresh_value, ids,
             seq_size, tp_size, scale):
    req_dev, rows, width = query.shape
    steps = rows // HEADS
    vmem = pl.BlockSpec(memory_space=pltpu.VMEM)
    return pl.pallas_call(
        functools.partial(exchange_kernel, seq_size, tp_size, scale),
        out_shape=(
            jax.ShapeDtypeStruct((seq_size, req_dev, 4 * steps, width), jnp.float32),
            jax.ShapeDtypeStruct((tp_size,) + ids.shape, ids.dtype),
        ),
        in_specs=[vmem, pl.BlockSpec(memory_space=pl.ANY), pl.BlockSpec(memory_space=pl.ANY)]
        + [vmem] * 5,
        out_specs=(vmem, vmem),
        scratch_shapes=[
            pltpu.VMEM(key_cache.shape, key_cache.dtype),
            pltpu.VMEM(value_cache.shape, value_cache.dtype),
            pltpu.VMEM((req_dev, 4 * steps, width), jnp.float32),
            pltpu.VMEM((seq_size, req_dev, 4 * steps, width), jnp.float32),
            pltpu.VMEM((tp_size,) + ids.shape, ids.dtype),
            pltpu.SemaphoreType.DMA((2, req_dev)),
            pltpu.SemaphoreType.DMA((seq_size,)),
            pltpu.SemaphoreType.DMA((seq_size,)),
            pltpu.SemaphoreType.DMA((tp_size,)),
            pltpu.SemaphoreType.DMA((tp_size,)),
        ],
        compiler_params=pltpu.CompilerParams(
            collective_id=0, has_side_effects=True, vmem_limit_bytes=48 * 1024 * 1024
        ),
    )(query, key_cache, value_cache, usable, fresh, fresh_ok, fresh_value, ids)


def expert_kernel(seq_size, tp_size, slices, sums_ref, hidden_ref, out_weight_hbm, gain_ref,
                  pick_in_ref, gate_hbm, up_hbm, down_hbm, pick_out_ref, out_ref, attn_ref,
                  normed_ref, out_weight_ref, gate_ref, up_ref, down_ref, load_sem, piece_ref,
                  context, everyone, part, recv, middle, outgoing, landing, send0, recv0,
                  send1, recv1, send3, recv3):
    mesh_type = pl.DeviceIdType.MESH
    s = lax.axis_index("seq")
    t = lax.axis_index("tp")
    g = t // slices
    j = t % slices
    chunk = recv.shape[2]
    halves = slices // seq_size
    src_seq = j // halves

    def dest(i):
        return (i // halves, g * slices + s * halves + i % halves)

    def is_self(i):
        return (i // halves == s) & (g * slices + s * halves + i % halves == t)

    barrier = pltpu.get_barrier_semaphore()
    for u in range(tp_size):
        @pl.when(t != u)
        def _():
            pl.semaphore_signal(barrier, inc=1, device_id=(s, u), device_id_type=mesh_type)
    for i in range(slices):
        @pl.when(i // halves != s)
        def _():
            pl.semaphore_signal(barrier, inc=1, device_id=dest(i), device_id_type=mesh_type)
    for k in range(slices):
        @pl.when((src_seq != s) & (k // halves != s))
        def _():
            pl.semaphore_signal(
                barrier, inc=1, device_id=(src_seq, g * slices + k), device_id_type=mesh_type
            )
    loads = [
        pltpu.make_async_copy(src_hbm, dst, load_sem.at[n])
        for n, (src_hbm, dst) in enumerate(
            [(out_weight_hbm, out_weight_ref), (gate_hbm, gate_ref), (up_hbm, up_ref),
             (down_hbm, down_ref)]
        )
    ]
    for copy in loads:
        copy.start()

    req_dev = sums_ref.shape[1]
    steps = sums_ref.shape[2] // 4
    context[...] = jnp.zeros_like(context)
    for r in range(req_dev):
        block_sums = [sums_ref[b, r, 0:steps, :] for b in range(seq_size)]
        block_max = [sums_ref[b, r, steps : 2 * steps, :] for b in range(seq_size)]
        block_totals = [sums_ref[b, r, 2 * steps : 3 * steps, :] for b in range(seq_size)]
        overall = block_max[0]
        for b in range(1, seq_size):
            overall = jnp.maximum(overall, block_max[b])
        numer = jnp.zeros_like(overall)
        denom = jnp.zeros_like(overall)
        for b in range(seq_size):
            factor = jnp.exp(block_max[b] - overall)
            numer = numer + factor * block_sums[b]
            denom = denom + factor * block_totals[b]
        context[r * steps : (r + 1) * steps, :] = numer / denom
    loads[0].wait()
    attention = jnp.dot(
        context[...].astype(jnp.bfloat16), out_weight_ref[...], preferred_element_type=jnp.float32
    )
    attn_ref[...] = attention
    residual = hidden_ref[...] + attention
    mean_square = jnp.mean(residual * residual, axis=1, keepdims=True)
    normed = (residual * lax.rsqrt(mean_square + norm_epsilon) * gain_ref[...]).astype(
        jnp.bfloat16
    )
    piece_ref[...] = normed
    normed_ref[...] = normed

    far = (seq_size - 1) * halves
    near = tp_size - 1 + far

    @pl.when(src_seq == s)
    def _():
        pl.semaphore_wait(barrier, near)

    @pl.when(src_seq != s)
    def _():
        pl.semaphore_wait(barrier, near + slices - halves)

    def gather(u, slot):
        return pltpu.make_async_remote_copy(
            piece_ref, everyone.at[slot], send0.at[u], recv0.at[slot],
            device_id=(s, u), device_id_type=mesh_type,
        )

    for u in range(tp_size):
        @pl.when(t == u)
        def _():
            pltpu.make_async_copy(piece_ref, everyone.at[u], recv0.at[u]).start()

        @pl.when(t != u)
        def _():
            gather(u, t).start()

    for u in range(tp_size):
        @pl.when(t == u)
        def _():
            pltpu.make_async_copy(piece_ref, everyone.at[u], recv0.at[u]).wait()

        @pl.when(t != u)
        def _():
            gather(u, t).wait_send()
            gather(u, u).wait_recv()

    for copy in loads[1:]:
        copy.wait()
    rows_in = everyone[...].reshape(-1, everyone.shape[2])
    buffer = jnp.dot(pick_in_ref[...], rows_in, preferred_element_type=jnp.float32).astype(
        jnp.bfloat16
    )
    contract = (((1,), (1,)), ((), ()))
    gate = lax.dot_general(buffer, gate_ref[...], contract, preferred_element_type=jnp.float32)
    upward = lax.dot_general(buffer, up_ref[...], contract, preferred_element_type=jnp.float32)
    inner = (jax.nn.gelu(gate) * upward).astype(jnp.bfloat16)
    part[...] = jnp.dot(inner, down_ref[...], preferred_element_type=jnp.float32).astype(
        part.dtype
    )

    def stage1(i):
        return pltpu.make_async_remote_copy(
            part.at[:, pl.ds(i * chunk, chunk)],
            recv.at[j],
            send1.at[i],
            recv1.at[j],
            device_id=dest(i),
            device_id_type=mesh_type,
        )

    for i in range(slices):
        @pl.when(is_self(i))
        def _():
            pltpu.make_async_copy(part.at[:, pl.ds(i * chunk, chunk)], recv.at[j], recv1.at[j]).start()

        @pl.when(jnp.logical_not(is_self(i)))
        def _():
            stage1(i).start()

    for i in range(slices):
        @pl.when(jnp.logical_not(is_self(i)))
        def _():
            stage1(i).wait_send()

    for k in range(slices):
        from_self = (src_seq == s) & (k == j)

        @pl.when(from_self)
        def _():
            pltpu.make_async_copy(part.at[:, pl.ds(0, chunk)], recv.at[k], recv1.at[k]).wait()

        @pl.when(jnp.logical_not(from_self))
        def _():
            pltpu.make_async_remote_copy(
                part.at[:, pl.ds(0, chunk)],
                recv.at[k],
                send1.at[0],
                recv1.at[k],
                device_id=(src_seq, g * slices + k),
                device_id_type=mesh_type,
            ).wait_recv()

    total = recv[0].astype(jnp.float32)
    for k in range(1, slices):
        total = total + recv[k].astype(jnp.float32)
    middle[...] = total.astype(middle.dtype)

    picked = jnp.dot(
        pick_out_ref[...].reshape(-1, pick_out_ref.shape[2]),
        middle[...],
        preferred_element_type=jnp.float32,
    )
    outgoing[...] = picked.reshape(outgoing.shape).astype(outgoing.dtype)

    def stage3(u):
        return pltpu.make_async_remote_copy(
            outgoing.at[u], landing.at[t], send3.at[u], recv3.at[t],
            device_id=(s, u), device_id_type=mesh_type,
        )

    for u in range(tp_size):
        @pl.when(t == u)
        def _():
            pltpu.make_async_copy(outgoing.at[u], landing.at[u], recv3.at[u]).start()

        @pl.when(t != u)
        def _():
            stage3(u).start()

    for u in range(tp_size):
        @pl.when(t == u)
        def _():
            pltpu.make_async_copy(outgoing.at[u], landing.at[u], recv3.at[u]).wait()

        @pl.when(t != u)
        def _():
            stage3(u).wait_send()
            pltpu.make_async_remote_copy(
                outgoing.at[u], landing.at[u], send3.at[u], recv3.at[u],
                device_id=(s, u), device_id_type=mesh_type,
            ).wait_recv()

    out_ref[...] = landing[...]


def run_experts(sums, hidden, out_weight, gain, pick_in, gate_weight, up_weight, down_weight,
                pick_out, seq_size, tp_size, slices):
    tokens, width = hidden.shape
    rows = pick_in.shape[0]
    chunk = width // slices
    vmem = pl.BlockSpec(memory_space=pltpu.VMEM)
    hbm = pl.BlockSpec(memory_space=pl.ANY)
    return pl.pallas_call(
        functools.partial(expert_kernel, seq_size, tp_size, slices),
        out_shape=(
            jax.ShapeDtypeStruct((tp_size, tokens, chunk), jnp.bfloat16),
            jax.ShapeDtypeStruct((tokens, width), jnp.float32),
            jax.ShapeDtypeStruct((tokens, width), jnp.bfloat16),
        ),
        in_specs=[vmem, vmem, hbm, vmem, vmem, hbm, hbm, hbm, vmem],
        out_specs=(vmem, vmem, vmem),
        scratch_shapes=[
            pltpu.VMEM(out_weight.shape, out_weight.dtype),
            pltpu.VMEM(gate_weight.shape, gate_weight.dtype),
            pltpu.VMEM(up_weight.shape, up_weight.dtype),
            pltpu.VMEM(down_weight.shape, down_weight.dtype),
            pltpu.SemaphoreType.DMA((4,)),
            pltpu.VMEM((tokens, width), jnp.bfloat16),
            pltpu.VMEM((tokens, width), jnp.float32),
            pltpu.VMEM((tp_size, tokens, width), jnp.bfloat16),
            pltpu.VMEM((rows, width), jnp.bfloat16),
            pltpu.VMEM((slices, rows, chunk), jnp.bfloat16),
            pltpu.VMEM((rows, chunk), jnp.bfloat16),
            pltpu.VMEM((tp_size, tokens, chunk), jnp.bfloat16),
            pltpu.VMEM((tp_size, tokens, chunk), jnp.bfloat16),
            pltpu.SemaphoreType.DMA((tp_size,)),
            pltpu.SemaphoreType.DMA((tp_size,)),
            pltpu.SemaphoreType.DMA((slices,)),
            pltpu.SemaphoreType.DMA((slices,)),
            pltpu.SemaphoreType.DMA((tp_size,)),
            pltpu.SemaphoreType.DMA((tp_size,)),
        ],
        compiler_params=pltpu.CompilerParams(
            collective_id=1, has_side_effects=True
        ),
    )(sums, hidden, out_weight, gain, pick_in, gate_weight, up_weight, down_weight, pick_out)


def body(
    hidden_in,
    new_query,
    new_key,
    new_value,
    key_cache,
    value_cache,
    lengths,
    out_weight,
    norm_gain,
    router_weight,
    expert_ids,
    gate_weight,
    up_weight,
    down_weight,
):
    req_dev, steps, width = hidden_in.shape
    block = key_cache.shape[1]
    head_size = width // HEADS
    scale = head_size ** (-0.5)
    seq_index = lax.axis_index("seq")
    tp_index = lax.axis_index("tp")
    seq_size = lax.axis_size("seq")
    tp_size = lax.axis_size("tp")
    rows = steps * HEADS
    own = req_dev * steps

    head_mask = (jnp.arange(width) // head_size)[None, :] == jnp.arange(HEADS)[:, None]
    q_wide = jnp.where(head_mask[None, None], new_query[:, :, None, :], 0).reshape(
        req_dev, rows, width
    )
    positions = seq_index * block + jnp.arange(block, dtype=jnp.int32)
    usable = (positions[None, :] < lengths[:, None]).astype(jnp.float32)
    usable = jnp.broadcast_to(usable[:, None, :], (req_dev, 8, block))
    fresh_scores = (
        jnp.einsum("rqd,rsd->rqs", q_wide, new_key, preferred_element_type=jnp.float32) * scale
    )
    causal = (
        (jnp.arange(rows)[:, None] // HEADS) >= jnp.arange(steps)[None, :]
    ) & (seq_index == 0)
    fresh_scores = jnp.where(causal, fresh_scores, masked_score)
    fresh_scores = jnp.pad(
        fresh_scores, ((0, 0), (0, 0), (0, 128 - steps)), constant_values=masked_score
    )
    fresh_ok = jnp.pad(
        jnp.broadcast_to(causal, (req_dev, rows, steps)).astype(jnp.float32),
        ((0, 0), (0, 0), (0, 128 - steps)),
    )
    fresh_value = jnp.pad(new_value, ((0, 0), (0, 128 - steps), (0, 0)))
    id_count = expert_ids.size
    id_rows = 8
    id_piece = jnp.pad(expert_ids.reshape(1, id_count), ((0, id_rows - 1), (0, 128 - id_count)))
    block_sums, all_id_pieces = exchange(
        q_wide, key_cache, value_cache, usable, fresh_scores, fresh_ok, fresh_value, id_piece,
        seq_size, tp_size, scale,
    )
    all_ids = all_id_pieces[:, 0, :id_count].reshape(tp_size * req_dev, steps, -1)
    feature_block = width // seq_size
    experts = router_weight.shape[1]
    topk = expert_ids.shape[2]
    requests = req_dev * tp_size
    capacity = (5 * requests * topk + 4 * experts - 1) // (4 * experts)
    expert_range = jnp.arange(experts, dtype=jnp.int32)
    slices = seq_size * tp_size // experts
    groups = tp_size // slices
    halves = slices // seq_size
    padded = 8 * ((steps * capacity + 7) // 8)
    tokens = 16 * ((own + 15) // 16)

    onehot = all_ids[..., None] == expert_range
    hits = jnp.sum(onehot.astype(jnp.int32), axis=2)
    earlier = jnp.cumsum(hits, axis=0) - hits
    all_slots = jnp.sum(jnp.where(onehot, earlier[:, :, None, :], 0), axis=3)
    row_of = jnp.arange(steps, dtype=jnp.int32)[None, :, None] * capacity + all_slots

    def rows_for(expert):
        hit = (all_ids == expert) & (all_slots < capacity)
        chosen_rows = jnp.any(
            hit[..., None] & (row_of[..., None] == jnp.arange(padded)), axis=2
        ).reshape(tp_size, own, padded)
        return jnp.pad(chosen_rows, ((0, 0), (0, tokens - own), (0, 0))).astype(jnp.bfloat16)

    mine = (seq_index * tp_size + tp_index) // slices
    pick_in = rows_for(mine).reshape(tp_size * tokens, padded).T
    held = ((tp_index % slices) // halves) * groups + tp_index // slices
    pick_out = rows_for(held)
    hidden = jnp.pad(
        hidden_in.astype(jnp.float32).reshape(own, width), ((0, tokens - own), (0, 0))
    )
    landed, attention, normed = run_experts(
        block_sums, hidden, out_weight, norm_gain.reshape(1, width), pick_in, gate_weight,
        up_weight, down_weight, pick_out, seq_size, tp_size, slices,
    )
    attention = attention[:own].reshape(req_dev, steps, width)
    normed = normed[:own].reshape(req_dev, steps, width)
    attn_out = lax.dynamic_slice_in_dim(
        attention, seq_index * feature_block, feature_block, 2
    ).astype(jnp.bfloat16)
    residual = hidden_in.astype(jnp.float32) + attention

    logits = jnp.einsum("rtd,de->rte", normed, router_weight, preferred_element_type=jnp.float32)
    own_hot = expert_ids[..., None] == expert_range
    chosen = jnp.sum(jnp.where(own_hot, logits[:, :, None, :], 0.0), axis=3)
    share = 1.0 / (1.0 + jnp.exp(chosen[:, :, ::-1] - chosen))
    own_slots = lax.dynamic_slice_in_dim(all_slots, tp_index * req_dev, req_dev, 0)
    weight = jnp.where(own_slots < capacity, share, 0.0)
    slot_expert = (jnp.arange(tp_size // halves) % (tp_size // (groups * halves))) * groups + (
        jnp.arange(tp_size // halves) // (tp_size // (groups * halves))
    )
    per_slot = jnp.sum(
        jnp.where(expert_ids[..., None] == slot_expert, weight[..., None], 0.0), axis=2
    ).reshape(own, tp_size // halves)
    landed = landed.astype(jnp.float32).reshape(tp_size // halves, halves, tokens, feature_block // halves)
    mixture = jnp.einsum(
        "ia,ahif->ihf", per_slot, landed[:, :, :own], precision=lax.Precision.HIGHEST
    ).reshape(req_dev, steps, feature_block)
    own_residual = lax.dynamic_slice_in_dim(residual, seq_index * feature_block, feature_block, 2)
    layer_out = (own_residual + mixture).astype(jnp.bfloat16)
    return (attn_out, layer_out)


def solution(mesh):

    return jax.shard_map(
        body,
        mesh=mesh,
        in_specs=(
            P("tp", None, None),
            P("tp", None, None),
            P("tp", None, None),
            P("tp", None, None),
            P("tp", "seq", None),
            P("tp", "seq", None),
            P("tp"),
            P(),
            P(),
            P(),
            P("tp", None, None),
            P(("seq", "tp"), None),
            P(("seq", "tp"), None),
            P(("seq", "tp"), None),
        ),
        out_specs=(P("tp", None, "seq"), P("tp", None, "seq")),
        check_vma=False,
    )
```

```python
import functools

import jax
import jax.numpy as jnp
from jax import lax
from jax.experimental import pallas as pl
from jax.experimental.pallas import tpu as pltpu
from jax.sharding import PartitionSpec as P

HEADS = 16


masked_score = -1e30
norm_epsilon = 1e-06


def exchange_kernel(seq_size, tp_size, scale, query_ref, key_hbm, value_hbm, usable_ref,
                    fresh_ref, fresh_ok_ref, fresh_value_ref, ids_ref, sums_out,
                    ids_out, keys, values, sums, sums_land, ids_land,
                    load_sem, send_a, recv_a, send_b, recv_b):
    mesh_type = pl.DeviceIdType.MESH
    s = lax.axis_index("seq")
    t = lax.axis_index("tp")
    req_dev, rows, width = query_ref.shape
    heads = HEADS

    barrier = pltpu.get_barrier_semaphore()
    for u in range(seq_size):
        @pl.when(s != u)
        def _():
            pl.semaphore_signal(barrier, inc=1, device_id=(u, t), device_id_type=mesh_type)
    for u in range(tp_size):
        @pl.when(t != u)
        def _():
            pl.semaphore_signal(barrier, inc=1, device_id=(s, u), device_id_type=mesh_type)

    loads = []
    for r in range(req_dev):
        loads.append(pltpu.make_async_copy(key_hbm.at[r], keys.at[r], load_sem.at[0, r]))
        loads.append(pltpu.make_async_copy(value_hbm.at[r], values.at[r], load_sem.at[1, r]))
    for copy in loads:
        copy.start()

    head_of = lax.broadcasted_iota(jnp.int32, (rows, width), 1) // (width // heads)
    row_head = lax.broadcasted_iota(jnp.int32, (rows, width), 0) % heads
    own_head = head_of == row_head
    spread = (
        lax.broadcasted_iota(jnp.int32, (rows // heads, rows), 1) // heads
        == lax.broadcasted_iota(jnp.int32, (rows // heads, rows), 0)
    ).astype(jnp.float32)
    contract = (((1,), (1,)), ((), ()))
    for r in range(req_dev):
        loads[2 * r].wait()
        scores = lax.dot_general(
            query_ref[r], keys[r], contract, preferred_element_type=jnp.float32
        ) * scale
        usable = usable_ref[r, 0:1, :] > 0.5
        scores = jnp.where(usable, scores, masked_score)
        fresh = fresh_ref[r]
        fresh_ok = fresh_ok_ref[r] > 0.5
        top = jnp.maximum(
            jnp.max(scores, axis=1, keepdims=True), jnp.max(fresh, axis=1, keepdims=True)
        )
        weights = jnp.where(usable, jnp.exp(scores - top), 0.0)
        fresh_weights = jnp.where(fresh_ok, jnp.exp(fresh - top), 0.0)
        total = jnp.sum(weights, axis=1, keepdims=True) + jnp.sum(
            fresh_weights, axis=1, keepdims=True
        )
        loads[2 * r + 1].wait()
        wide = jnp.dot(
            weights.astype(jnp.bfloat16), values[r], preferred_element_type=jnp.float32
        ) + jnp.dot(
            fresh_weights.astype(jnp.bfloat16), fresh_value_ref[r],
            preferred_element_type=jnp.float32,
        )
        wide = jnp.where(own_head, wide, 0.0)
        steps = rows // heads
        sums[r, 0:steps, :] = jnp.sum(wide.reshape(steps, heads, width), axis=1)
        sums[r, steps : 2 * steps, :] = jnp.dot(
            spread, jnp.where(own_head, top, 0.0),
            precision=lax.Precision.HIGHEST, preferred_element_type=jnp.float32,
        )
        sums[r, 2 * steps : 3 * steps, :] = jnp.dot(
            spread, jnp.where(own_head, total, 0.0),
            precision=lax.Precision.HIGHEST, preferred_element_type=jnp.float32,
        )
        sums[r, 3 * steps :, :] = jnp.zeros((sums.shape[1] - 3 * steps, width), jnp.float32)

    pl.semaphore_wait(barrier, seq_size - 1 + tp_size - 1)

    def sums_copy(u, slot):
        return pltpu.make_async_remote_copy(
            sums, sums_land.at[slot], send_a.at[u], recv_a.at[slot],
            device_id=(u, t), device_id_type=mesh_type,
        )

    def along_tp(u, slot):
        return pltpu.make_async_remote_copy(
            ids_ref, ids_land.at[slot], send_b.at[u], recv_b.at[slot],
            device_id=(s, u), device_id_type=mesh_type,
        )

    for u in range(seq_size):
        @pl.when(s == u)
        def _():
            pltpu.make_async_copy(sums, sums_land.at[u], recv_a.at[u]).start()

        @pl.when(s != u)
        def _():
            sums_copy(u, s).start()
    for u in range(tp_size):
        @pl.when(t == u)
        def _():
            pltpu.make_async_copy(ids_ref, ids_land.at[u], recv_b.at[u]).start()

        @pl.when(t != u)
        def _():
            along_tp(u, t).start()

    for u in range(seq_size):
        @pl.when(s == u)
        def _():
            pltpu.make_async_copy(sums, sums_land.at[u], recv_a.at[u]).wait()

        @pl.when(s != u)
        def _():
            sums_copy(u, s).wait_send()
            sums_copy(u, u).wait_recv()
    for u in range(tp_size):
        @pl.when(t == u)
        def _():
            pltpu.make_async_copy(ids_ref, ids_land.at[u], recv_b.at[u]).wait()

        @pl.when(t != u)
        def _():
            along_tp(u, t).wait_send()
            along_tp(u, u).wait_recv()

    sums_out[...] = sums_land[...]
    ids_out[...] = ids_land[...]


def exchange(query, key_cache, value_cache, usable, fresh, fresh_ok, fresh_value, ids,
             seq_size, tp_size, scale):
    req_dev, rows, width = query.shape
    steps = rows // HEADS
    vmem = pl.BlockSpec(memory_space=pltpu.VMEM)
    return pl.pallas_call(
        functools.partial(exchange_kernel, seq_size, tp_size, scale),
        out_shape=(
            jax.ShapeDtypeStruct((seq_size, req_dev, 4 * steps, width), jnp.float32),
            jax.ShapeDtypeStruct((tp_size,) + ids.shape, ids.dtype),
        ),
        in_specs=[vmem, pl.BlockSpec(memory_space=pl.ANY), pl.BlockSpec(memory_space=pl.ANY)]
        + [vmem] * 5,
        out_specs=(vmem, vmem),
        scratch_shapes=[
            pltpu.VMEM(key_cache.shape, key_cache.dtype),
            pltpu.VMEM(value_cache.shape, value_cache.dtype),
            pltpu.VMEM((req_dev, 4 * steps, width), jnp.float32),
            pltpu.VMEM((seq_size, req_dev, 4 * steps, width), jnp.float32),
            pltpu.VMEM((tp_size,) + ids.shape, ids.dtype),
            pltpu.SemaphoreType.DMA((2, req_dev)),
            pltpu.SemaphoreType.DMA((seq_size,)),
            pltpu.SemaphoreType.DMA((seq_size,)),
            pltpu.SemaphoreType.DMA((tp_size,)),
            pltpu.SemaphoreType.DMA((tp_size,)),
        ],
        compiler_params=pltpu.CompilerParams(
            collective_id=0, has_side_effects=True, vmem_limit_bytes=48 * 1024 * 1024
        ),
    )(query, key_cache, value_cache, usable, fresh, fresh_ok, fresh_value, ids)


def expert_kernel(seq_size, tp_size, slices, sums_ref, hidden_ref, out_weight_hbm, gain_ref,
                  pick_in_ref, gate_hbm, up_hbm, down_hbm, pick_out_ref, out_ref, attn_ref,
                  normed_ref, out_weight_ref, gate_ref, up_ref, down_ref, load_sem, piece_ref,
                  context, everyone, part, recv, middle, outgoing, landing, send0, recv0,
                  send1, recv1, send3, recv3):
    mesh_type = pl.DeviceIdType.MESH
    s = lax.axis_index("seq")
    t = lax.axis_index("tp")
    g = t // slices
    j = t % slices
    chunk = recv.shape[2]
    halves = slices // seq_size
    src_seq = j // halves

    def dest(i):
        return (i // halves, g * slices + s * halves + i % halves)

    def is_self(i):
        return (i // halves == s) & (g * slices + s * halves + i % halves == t)

    barrier = pltpu.get_barrier_semaphore()
    for u in range(tp_size):
        @pl.when(t != u)
        def _():
            pl.semaphore_signal(barrier, inc=1, device_id=(s, u), device_id_type=mesh_type)
    for i in range(slices):
        @pl.when(i // halves != s)
        def _():
            pl.semaphore_signal(barrier, inc=1, device_id=dest(i), device_id_type=mesh_type)
    for k in range(slices):
        @pl.when((src_seq != s) & (k // halves != s))
        def _():
            pl.semaphore_signal(
                barrier, inc=1, device_id=(src_seq, g * slices + k), device_id_type=mesh_type
            )
    loads = [
        pltpu.make_async_copy(src_hbm, dst, load_sem.at[n])
        for n, (src_hbm, dst) in enumerate(
            [(out_weight_hbm, out_weight_ref), (gate_hbm, gate_ref), (up_hbm, up_ref),
             (down_hbm, down_ref)]
        )
    ]
    for copy in loads:
        copy.start()

    req_dev = sums_ref.shape[1]
    steps = sums_ref.shape[2] // 4
    context[...] = jnp.zeros_like(context)
    for r in range(req_dev):
        block_sums = [sums_ref[b, r, 0:steps, :] for b in range(seq_size)]
        block_max = [sums_ref[b, r, steps : 2 * steps, :] for b in range(seq_size)]
        block_totals = [sums_ref[b, r, 2 * steps : 3 * steps, :] for b in range(seq_size)]
        overall = block_max[0]
        for b in range(1, seq_size):
            overall = jnp.maximum(overall, block_max[b])
        numer = jnp.zeros_like(overall)
        denom = jnp.zeros_like(overall)
        for b in range(seq_size):
            factor = jnp.exp(block_max[b] - overall)
            numer = numer + factor * block_sums[b]
            denom = denom + factor * block_totals[b]
        context[r * steps : (r + 1) * steps, :] = numer / denom
    loads[0].wait()
    attention = jnp.dot(
        context[...].astype(jnp.bfloat16), out_weight_ref[...], preferred_element_type=jnp.float32
    )
    attn_ref[...] = attention
    residual = hidden_ref[...] + attention
    mean_square = jnp.mean(residual * residual, axis=1, keepdims=True)
    normed = (residual * lax.rsqrt(mean_square + norm_epsilon) * gain_ref[...]).astype(
        jnp.bfloat16
    )
    piece_ref[...] = normed
    normed_ref[...] = normed

    far = (seq_size - 1) * halves
    near = tp_size - 1 + far

    @pl.when(src_seq == s)
    def _():
        pl.semaphore_wait(barrier, near)

    @pl.when(src_seq != s)
    def _():
        pl.semaphore_wait(barrier, near + slices - halves)

    def gather(u, slot):
        return pltpu.make_async_remote_copy(
            piece_ref, everyone.at[slot], send0.at[u], recv0.at[slot],
            device_id=(s, u), device_id_type=mesh_type,
        )

    pltpu.make_async_copy(piece_ref, everyone.at[t], recv0.at[t]).start()
    for k in range(1, tp_size):
        gather((t + k) % tp_size, t).start()

    pltpu.make_async_copy(piece_ref, everyone.at[t], recv0.at[t]).wait()
    for k in range(1, tp_size):
        u = (t + k) % tp_size
        gather(u, t).wait_send()
        gather(u, u).wait_recv()

    for copy in loads[1:]:
        copy.wait()
    rows_in = everyone[...].reshape(-1, everyone.shape[2])
    buffer = jnp.dot(pick_in_ref[...], rows_in, preferred_element_type=jnp.float32).astype(
        jnp.bfloat16
    )
    contract = (((1,), (1,)), ((), ()))
    gate = lax.dot_general(buffer, gate_ref[...], contract, preferred_element_type=jnp.float32)
    upward = lax.dot_general(buffer, up_ref[...], contract, preferred_element_type=jnp.float32)
    inner = (jax.nn.gelu(gate) * upward).astype(jnp.bfloat16)
    part[...] = jnp.dot(inner, down_ref[...], preferred_element_type=jnp.float32).astype(
        part.dtype
    )

    def stage1(i):
        return pltpu.make_async_remote_copy(
            part.at[:, pl.ds(i * chunk, chunk)],
            recv.at[j],
            send1.at[i],
            recv1.at[j],
            device_id=dest(i),
            device_id_type=mesh_type,
        )

    for i in range(slices):
        @pl.when(is_self(i))
        def _():
            pltpu.make_async_copy(part.at[:, pl.ds(i * chunk, chunk)], recv.at[j], recv1.at[j]).start()

        @pl.when(jnp.logical_not(is_self(i)))
        def _():
            stage1(i).start()

    for i in range(slices):
        @pl.when(jnp.logical_not(is_self(i)))
        def _():
            stage1(i).wait_send()

    for k in range(slices):
        from_self = (src_seq == s) & (k == j)

        @pl.when(from_self)
        def _():
            pltpu.make_async_copy(part.at[:, pl.ds(0, chunk)], recv.at[k], recv1.at[k]).wait()

        @pl.when(jnp.logical_not(from_self))
        def _():
            pltpu.make_async_remote_copy(
                part.at[:, pl.ds(0, chunk)],
                recv.at[k],
                send1.at[0],
                recv1.at[k],
                device_id=(src_seq, g * slices + k),
                device_id_type=mesh_type,
            ).wait_recv()

    total = recv[0].astype(jnp.float32)
    for k in range(1, slices):
        total = total + recv[k].astype(jnp.float32)
    middle[...] = total.astype(middle.dtype)

    picked = jnp.dot(
        pick_out_ref[...].reshape(-1, pick_out_ref.shape[2]),
        middle[...],
        preferred_element_type=jnp.float32,
    )
    outgoing[...] = picked.reshape(outgoing.shape).astype(outgoing.dtype)

    def stage3(u):
        return pltpu.make_async_remote_copy(
            outgoing.at[u], landing.at[t], send3.at[u], recv3.at[t],
            device_id=(s, u), device_id_type=mesh_type,
        )

    pltpu.make_async_copy(outgoing.at[t], landing.at[t], recv3.at[t]).start()
    for k in range(1, tp_size):
        stage3((t + k) % tp_size).start()

    pltpu.make_async_copy(outgoing.at[t], landing.at[t], recv3.at[t]).wait()
    for k in range(1, tp_size):
        u = (t + k) % tp_size
        stage3(u).wait_send()
        pltpu.make_async_remote_copy(
            outgoing.at[u], landing.at[u], send3.at[u], recv3.at[u],
            device_id=(s, u), device_id_type=mesh_type,
        ).wait_recv()

    out_ref[...] = landing[...]


def run_experts(sums, hidden, out_weight, gain, pick_in, gate_weight, up_weight, down_weight,
                pick_out, seq_size, tp_size, slices):
    tokens, width = hidden.shape
    rows = pick_in.shape[0]
    chunk = width // slices
    vmem = pl.BlockSpec(memory_space=pltpu.VMEM)
    hbm = pl.BlockSpec(memory_space=pl.ANY)
    return pl.pallas_call(
        functools.partial(expert_kernel, seq_size, tp_size, slices),
        out_shape=(
            jax.ShapeDtypeStruct((tp_size, tokens, chunk), jnp.bfloat16),
            jax.ShapeDtypeStruct((tokens, width), jnp.float32),
            jax.ShapeDtypeStruct((tokens, width), jnp.bfloat16),
        ),
        in_specs=[vmem, vmem, hbm, vmem, vmem, hbm, hbm, hbm, vmem],
        out_specs=(vmem, vmem, vmem),
        scratch_shapes=[
            pltpu.VMEM(out_weight.shape, out_weight.dtype),
            pltpu.VMEM(gate_weight.shape, gate_weight.dtype),
            pltpu.VMEM(up_weight.shape, up_weight.dtype),
            pltpu.VMEM(down_weight.shape, down_weight.dtype),
            pltpu.SemaphoreType.DMA((4,)),
            pltpu.VMEM((tokens, width), jnp.bfloat16),
            pltpu.VMEM((tokens, width), jnp.float32),
            pltpu.VMEM((tp_size, tokens, width), jnp.bfloat16),
            pltpu.VMEM((rows, width), jnp.bfloat16),
            pltpu.VMEM((slices, rows, chunk), jnp.bfloat16),
            pltpu.VMEM((rows, chunk), jnp.bfloat16),
            pltpu.VMEM((tp_size, tokens, chunk), jnp.bfloat16),
            pltpu.VMEM((tp_size, tokens, chunk), jnp.bfloat16),
            pltpu.SemaphoreType.DMA((tp_size,)),
            pltpu.SemaphoreType.DMA((tp_size,)),
            pltpu.SemaphoreType.DMA((slices,)),
            pltpu.SemaphoreType.DMA((slices,)),
            pltpu.SemaphoreType.DMA((tp_size,)),
            pltpu.SemaphoreType.DMA((tp_size,)),
        ],
        compiler_params=pltpu.CompilerParams(
            collective_id=1, has_side_effects=True
        ),
    )(sums, hidden, out_weight, gain, pick_in, gate_weight, up_weight, down_weight, pick_out)


def body(
    hidden_in,
    new_query,
    new_key,
    new_value,
    key_cache,
    value_cache,
    lengths,
    out_weight,
    norm_gain,
    router_weight,
    expert_ids,
    gate_weight,
    up_weight,
    down_weight,
):
    req_dev, steps, width = hidden_in.shape
    block = key_cache.shape[1]
    head_size = width // HEADS
    scale = head_size ** (-0.5)
    seq_index = lax.axis_index("seq")
    tp_index = lax.axis_index("tp")
    seq_size = lax.axis_size("seq")
    tp_size = lax.axis_size("tp")
    rows = steps * HEADS
    own = req_dev * steps

    head_mask = (jnp.arange(width) // head_size)[None, :] == jnp.arange(HEADS)[:, None]
    q_wide = jnp.where(head_mask[None, None], new_query[:, :, None, :], 0).reshape(
        req_dev, rows, width
    )
    positions = seq_index * block + jnp.arange(block, dtype=jnp.int32)
    usable = (positions[None, :] < lengths[:, None]).astype(jnp.float32)
    usable = jnp.broadcast_to(usable[:, None, :], (req_dev, 8, block))
    fresh_scores = (
        jnp.einsum("rqd,rsd->rqs", q_wide, new_key, preferred_element_type=jnp.float32) * scale
    )
    causal = (
        (jnp.arange(rows)[:, None] // HEADS) >= jnp.arange(steps)[None, :]
    ) & (seq_index == 0)
    fresh_scores = jnp.where(causal, fresh_scores, masked_score)
    fresh_scores = jnp.pad(
        fresh_scores, ((0, 0), (0, 0), (0, 128 - steps)), constant_values=masked_score
    )
    fresh_ok = jnp.pad(
        jnp.broadcast_to(causal, (req_dev, rows, steps)).astype(jnp.float32),
        ((0, 0), (0, 0), (0, 128 - steps)),
    )
    fresh_value = jnp.pad(new_value, ((0, 0), (0, 128 - steps), (0, 0)))
    id_count = expert_ids.size
    id_rows = 8
    id_piece = jnp.pad(expert_ids.reshape(1, id_count), ((0, id_rows - 1), (0, 128 - id_count)))
    block_sums, all_id_pieces = exchange(
        q_wide, key_cache, value_cache, usable, fresh_scores, fresh_ok, fresh_value, id_piece,
        seq_size, tp_size, scale,
    )
    all_ids = all_id_pieces[:, 0, :id_count].reshape(tp_size * req_dev, steps, -1)
    feature_block = width // seq_size
    experts = router_weight.shape[1]
    topk = expert_ids.shape[2]
    requests = req_dev * tp_size
    capacity = (5 * requests * topk + 4 * experts - 1) // (4 * experts)
    expert_range = jnp.arange(experts, dtype=jnp.int32)
    slices = seq_size * tp_size // experts
    groups = tp_size // slices
    halves = slices // seq_size
    padded = 8 * ((steps * capacity + 7) // 8)
    tokens = 16 * ((own + 15) // 16)

    onehot = all_ids[..., None] == expert_range
    hits = jnp.sum(onehot.astype(jnp.int32), axis=2)
    earlier = jnp.cumsum(hits, axis=0) - hits
    all_slots = jnp.sum(jnp.where(onehot, earlier[:, :, None, :], 0), axis=3)
    row_of = jnp.arange(steps, dtype=jnp.int32)[None, :, None] * capacity + all_slots

    def rows_for(expert):
        hit = (all_ids == expert) & (all_slots < capacity)
        chosen_rows = jnp.any(
            hit[..., None] & (row_of[..., None] == jnp.arange(padded)), axis=2
        ).reshape(tp_size, own, padded)
        return jnp.pad(chosen_rows, ((0, 0), (0, tokens - own), (0, 0))).astype(jnp.bfloat16)

    mine = (seq_index * tp_size + tp_index) // slices
    pick_in = rows_for(mine).reshape(tp_size * tokens, padded).T
    held = ((tp_index % slices) // halves) * groups + tp_index // slices
    pick_out = rows_for(held)
    hidden = jnp.pad(
        hidden_in.astype(jnp.float32).reshape(own, width), ((0, tokens - own), (0, 0))
    )
    landed, attention, normed = run_experts(
        block_sums, hidden, out_weight, norm_gain.reshape(1, width), pick_in, gate_weight,
        up_weight, down_weight, pick_out, seq_size, tp_size, slices,
    )
    attention = attention[:own].reshape(req_dev, steps, width)
    normed = normed[:own].reshape(req_dev, steps, width)
    attn_out = lax.dynamic_slice_in_dim(
        attention, seq_index * feature_block, feature_block, 2
    ).astype(jnp.bfloat16)
    residual = hidden_in.astype(jnp.float32) + attention

    logits = jnp.einsum("rtd,de->rte", normed, router_weight, preferred_element_type=jnp.float32)
    own_hot = expert_ids[..., None] == expert_range
    chosen = jnp.sum(jnp.where(own_hot, logits[:, :, None, :], 0.0), axis=3)
    share = 1.0 / (1.0 + jnp.exp(chosen[:, :, ::-1] - chosen))
    own_slots = lax.dynamic_slice_in_dim(all_slots, tp_index * req_dev, req_dev, 0)
    weight = jnp.where(own_slots < capacity, share, 0.0)
    slot_expert = (jnp.arange(tp_size // halves) % (tp_size // (groups * halves))) * groups + (
        jnp.arange(tp_size // halves) // (tp_size // (groups * halves))
    )
    per_slot = jnp.sum(
        jnp.where(expert_ids[..., None] == slot_expert, weight[..., None], 0.0), axis=2
    ).reshape(own, tp_size // halves)
    landed = landed.astype(jnp.float32).reshape(tp_size // halves, halves, tokens, feature_block // halves)
    mixture = jnp.einsum(
        "ia,ahif->ihf", per_slot, landed[:, :, :own], precision=lax.Precision.HIGHEST
    ).reshape(req_dev, steps, feature_block)
    own_residual = lax.dynamic_slice_in_dim(residual, seq_index * feature_block, feature_block, 2)
    layer_out = (own_residual + mixture).astype(jnp.bfloat16)
    return (attn_out, layer_out)


def solution(mesh):

    return jax.shard_map(
        body,
        mesh=mesh,
        in_specs=(
            P("tp", None, None),
            P("tp", None, None),
            P("tp", None, None),
            P("tp", None, None),
            P("tp", "seq", None),
            P("tp", "seq", None),
            P("tp"),
            P(),
            P(),
            P(),
            P("tp", None, None),
            P(("seq", "tp"), None),
            P(("seq", "tp"), None),
            P(("seq", "tp"), None),
        ),
        out_specs=(P("tp", None, "seq"), P("tp", None, "seq")),
        check_vma=False,
    )
```

```python
import functools

import jax
import jax.numpy as jnp
from jax import lax
from jax.experimental import pallas as pl
from jax.experimental.pallas import tpu as pltpu
from jax.sharding import PartitionSpec as P

HEADS = 16


masked_score = -1e30
norm_epsilon = 1e-06


def exchange_kernel(seq_size, tp_size, scale, query_ref, key_hbm, value_hbm, usable_ref,
                    fresh_ref, fresh_ok_ref, fresh_value_ref, ids_ref, sums_out,
                    ids_out, keys, values, sums, sums_land, ids_land,
                    load_sem, send_a, recv_a, send_b, recv_b):
    mesh_type = pl.DeviceIdType.MESH
    s = lax.axis_index("seq")
    t = lax.axis_index("tp")
    req_dev, rows, width = query_ref.shape
    heads = HEADS

    barrier = pltpu.get_barrier_semaphore()
    for u in range(seq_size):
        @pl.when(s != u)
        def _():
            pl.semaphore_signal(barrier, inc=1, device_id=(u, t), device_id_type=mesh_type)
    for u in range(tp_size):
        @pl.when(t != u)
        def _():
            pl.semaphore_signal(barrier, inc=1, device_id=(s, u), device_id_type=mesh_type)

    loads = []
    for r in range(req_dev):
        loads.append(pltpu.make_async_copy(key_hbm.at[r], keys.at[r], load_sem.at[0, r]))
        loads.append(pltpu.make_async_copy(value_hbm.at[r], values.at[r], load_sem.at[1, r]))
    for copy in loads:
        copy.start()

    head_of = lax.broadcasted_iota(jnp.int32, (rows, width), 1) // (width // heads)
    row_head = lax.broadcasted_iota(jnp.int32, (rows, width), 0) % heads
    own_head = head_of == row_head
    spread = (
        lax.broadcasted_iota(jnp.int32, (rows // heads, rows), 1) // heads
        == lax.broadcasted_iota(jnp.int32, (rows // heads, rows), 0)
    ).astype(jnp.float32)
    contract = (((1,), (1,)), ((), ()))
    for r in range(req_dev):
        loads[2 * r].wait()
        scores = lax.dot_general(
            query_ref[r], keys[r], contract, preferred_element_type=jnp.float32
        ) * scale
        usable = usable_ref[r, 0:1, :] > 0.5
        scores = jnp.where(usable, scores, masked_score)
        fresh = fresh_ref[r]
        fresh_ok = fresh_ok_ref[r] > 0.5
        top = jnp.maximum(
            jnp.max(scores, axis=1, keepdims=True), jnp.max(fresh, axis=1, keepdims=True)
        )
        weights = jnp.where(usable, jnp.exp(scores - top), 0.0)
        fresh_weights = jnp.where(fresh_ok, jnp.exp(fresh - top), 0.0)
        total = jnp.sum(weights, axis=1, keepdims=True) + jnp.sum(
            fresh_weights, axis=1, keepdims=True
        )
        loads[2 * r + 1].wait()
        wide = jnp.dot(
            weights.astype(jnp.bfloat16), values[r], preferred_element_type=jnp.float32
        ) + jnp.dot(
            fresh_weights.astype(jnp.bfloat16), fresh_value_ref[r],
            preferred_element_type=jnp.float32,
        )
        wide = jnp.where(own_head, wide, 0.0)
        steps = rows // heads
        sums[r, 0:steps, :] = jnp.sum(wide.reshape(steps, heads, width), axis=1)
        sums[r, steps : 2 * steps, :] = jnp.dot(
            spread, jnp.where(own_head, top, 0.0),
            precision=lax.Precision.HIGHEST, preferred_element_type=jnp.float32,
        )
        sums[r, 2 * steps : 3 * steps, :] = jnp.dot(
            spread, jnp.where(own_head, total, 0.0),
            precision=lax.Precision.HIGHEST, preferred_element_type=jnp.float32,
        )
        sums[r, 3 * steps :, :] = jnp.zeros((sums.shape[1] - 3 * steps, width), jnp.float32)

    pl.semaphore_wait(barrier, seq_size - 1 + tp_size - 1)

    def sums_copy(u, slot):
        return pltpu.make_async_remote_copy(
            sums, sums_land.at[slot], send_a.at[u], recv_a.at[slot],
            device_id=(u, t), device_id_type=mesh_type,
        )

    def along_tp(u, slot):
        return pltpu.make_async_remote_copy(
            ids_ref, ids_land.at[slot], send_b.at[u], recv_b.at[slot],
            device_id=(s, u), device_id_type=mesh_type,
        )

    pltpu.make_async_copy(sums, sums_land.at[s], recv_a.at[s]).start()
    for k in range(1, seq_size):
        sums_copy((s + k) % seq_size, s).start()
    pltpu.make_async_copy(ids_ref, ids_land.at[t], recv_b.at[t]).start()
    for k in range(1, tp_size):
        along_tp((t + k) % tp_size, t).start()

    pltpu.make_async_copy(sums, sums_land.at[s], recv_a.at[s]).wait()
    for k in range(1, seq_size):
        u = (s + k) % seq_size
        sums_copy(u, s).wait_send()
        sums_copy(u, u).wait_recv()
    pltpu.make_async_copy(ids_ref, ids_land.at[t], recv_b.at[t]).wait()
    for k in range(1, tp_size):
        u = (t + k) % tp_size
        along_tp(u, t).wait_send()
        along_tp(u, u).wait_recv()

    sums_out[...] = sums_land[...]
    ids_out[...] = ids_land[...]


def exchange(query, key_cache, value_cache, usable, fresh, fresh_ok, fresh_value, ids,
             seq_size, tp_size, scale):
    req_dev, rows, width = query.shape
    steps = rows // HEADS
    vmem = pl.BlockSpec(memory_space=pltpu.VMEM)
    return pl.pallas_call(
        functools.partial(exchange_kernel, seq_size, tp_size, scale),
        out_shape=(
            jax.ShapeDtypeStruct((seq_size, req_dev, 4 * steps, width), jnp.float32),
            jax.ShapeDtypeStruct((tp_size,) + ids.shape, ids.dtype),
        ),
        in_specs=[vmem, pl.BlockSpec(memory_space=pl.ANY), pl.BlockSpec(memory_space=pl.ANY)]
        + [vmem] * 5,
        out_specs=(vmem, vmem),
        scratch_shapes=[
            pltpu.VMEM(key_cache.shape, key_cache.dtype),
            pltpu.VMEM(value_cache.shape, value_cache.dtype),
            pltpu.VMEM((req_dev, 4 * steps, width), jnp.float32),
            pltpu.VMEM((seq_size, req_dev, 4 * steps, width), jnp.float32),
            pltpu.VMEM((tp_size,) + ids.shape, ids.dtype),
            pltpu.SemaphoreType.DMA((2, req_dev)),
            pltpu.SemaphoreType.DMA((seq_size,)),
            pltpu.SemaphoreType.DMA((seq_size,)),
            pltpu.SemaphoreType.DMA((tp_size,)),
            pltpu.SemaphoreType.DMA((tp_size,)),
        ],
        compiler_params=pltpu.CompilerParams(
            collective_id=0, has_side_effects=True, vmem_limit_bytes=48 * 1024 * 1024
        ),
    )(query, key_cache, value_cache, usable, fresh, fresh_ok, fresh_value, ids)


def expert_kernel(seq_size, tp_size, slices, sums_ref, hidden_ref, out_weight_hbm, gain_ref,
                  pick_in_ref, gate_hbm, up_hbm, down_hbm, pick_out_ref, out_ref, attn_ref,
                  normed_ref, out_weight_ref, gate_ref, up_ref, down_ref, load_sem, piece_ref,
                  context, everyone, part, recv, middle, outgoing, landing, send0, recv0,
                  send1, recv1, send3, recv3):
    mesh_type = pl.DeviceIdType.MESH
    s = lax.axis_index("seq")
    t = lax.axis_index("tp")
    g = t // slices
    j = t % slices
    chunk = recv.shape[2]
    halves = slices // seq_size
    src_seq = j // halves

    def dest(i):
        return (i // halves, g * slices + s * halves + i % halves)

    def is_self(i):
        return (i // halves == s) & (g * slices + s * halves + i % halves == t)

    barrier = pltpu.get_barrier_semaphore()
    for u in range(tp_size):
        @pl.when(t != u)
        def _():
            pl.semaphore_signal(barrier, inc=1, device_id=(s, u), device_id_type=mesh_type)
    for i in range(slices):
        @pl.when(i // halves != s)
        def _():
            pl.semaphore_signal(barrier, inc=1, device_id=dest(i), device_id_type=mesh_type)
    for k in range(slices):
        @pl.when((src_seq != s) & (k // halves != s))
        def _():
            pl.semaphore_signal(
                barrier, inc=1, device_id=(src_seq, g * slices + k), device_id_type=mesh_type
            )
    loads = [
        pltpu.make_async_copy(src_hbm, dst, load_sem.at[n])
        for n, (src_hbm, dst) in enumerate(
            [(out_weight_hbm, out_weight_ref), (gate_hbm, gate_ref), (up_hbm, up_ref),
             (down_hbm, down_ref)]
        )
    ]
    for copy in loads:
        copy.start()

    req_dev = sums_ref.shape[1]
    steps = sums_ref.shape[2] // 4
    context[...] = jnp.zeros_like(context)
    for r in range(req_dev):
        block_sums = [sums_ref[b, r, 0:steps, :] for b in range(seq_size)]
        block_max = [sums_ref[b, r, steps : 2 * steps, :] for b in range(seq_size)]
        block_totals = [sums_ref[b, r, 2 * steps : 3 * steps, :] for b in range(seq_size)]
        overall = block_max[0]
        for b in range(1, seq_size):
            overall = jnp.maximum(overall, block_max[b])
        numer = jnp.zeros_like(overall)
        denom = jnp.zeros_like(overall)
        for b in range(seq_size):
            factor = jnp.exp(block_max[b] - overall)
            numer = numer + factor * block_sums[b]
            denom = denom + factor * block_totals[b]
        context[r * steps : (r + 1) * steps, :] = numer / denom
    loads[0].wait()
    attention = jnp.dot(
        context[...].astype(jnp.bfloat16), out_weight_ref[...], preferred_element_type=jnp.float32
    )
    attn_ref[...] = attention
    residual = hidden_ref[...] + attention
    mean_square = jnp.mean(residual * residual, axis=1, keepdims=True)
    normed = (residual * lax.rsqrt(mean_square + norm_epsilon) * gain_ref[...]).astype(
        jnp.bfloat16
    )
    piece_ref[...] = normed
    normed_ref[...] = normed

    far = (seq_size - 1) * halves
    near = tp_size - 1 + far

    @pl.when(src_seq == s)
    def _():
        pl.semaphore_wait(barrier, near)

    @pl.when(src_seq != s)
    def _():
        pl.semaphore_wait(barrier, near + slices - halves)

    def gather(u, slot):
        return pltpu.make_async_remote_copy(
            piece_ref, everyone.at[slot], send0.at[u], recv0.at[slot],
            device_id=(s, u), device_id_type=mesh_type,
        )

    pltpu.make_async_copy(piece_ref, everyone.at[t], recv0.at[t]).start()
    for k in range(1, tp_size):
        gather((t + k) % tp_size, t).start()

    pltpu.make_async_copy(piece_ref, everyone.at[t], recv0.at[t]).wait()
    for k in range(1, tp_size):
        u = (t + k) % tp_size
        gather(u, t).wait_send()
        gather(u, u).wait_recv()

    for copy in loads[1:]:
        copy.wait()
    rows_in = everyone[...].reshape(-1, everyone.shape[2])
    buffer = jnp.dot(pick_in_ref[...], rows_in, preferred_element_type=jnp.float32).astype(
        jnp.bfloat16
    )
    contract = (((1,), (1,)), ((), ()))
    gate = lax.dot_general(buffer, gate_ref[...], contract, preferred_element_type=jnp.float32)
    upward = lax.dot_general(buffer, up_ref[...], contract, preferred_element_type=jnp.float32)
    inner = (jax.nn.gelu(gate) * upward).astype(jnp.bfloat16)
    part[...] = jnp.dot(inner, down_ref[...], preferred_element_type=jnp.float32).astype(
        part.dtype
    )

    def stage1(i):
        return pltpu.make_async_remote_copy(
            part.at[:, pl.ds(i * chunk, chunk)],
            recv.at[j],
            send1.at[i],
            recv1.at[j],
            device_id=dest(i),
            device_id_type=mesh_type,
        )

    for i in range(slices):
        @pl.when(is_self(i))
        def _():
            pltpu.make_async_copy(part.at[:, pl.ds(i * chunk, chunk)], recv.at[j], recv1.at[j]).start()

        @pl.when(jnp.logical_not(is_self(i)))
        def _():
            stage1(i).start()

    for i in range(slices):
        @pl.when(jnp.logical_not(is_self(i)))
        def _():
            stage1(i).wait_send()

    for k in range(slices):
        from_self = (src_seq == s) & (k == j)

        @pl.when(from_self)
        def _():
            pltpu.make_async_copy(part.at[:, pl.ds(0, chunk)], recv.at[k], recv1.at[k]).wait()

        @pl.when(jnp.logical_not(from_self))
        def _():
            pltpu.make_async_remote_copy(
                part.at[:, pl.ds(0, chunk)],
                recv.at[k],
                send1.at[0],
                recv1.at[k],
                device_id=(src_seq, g * slices + k),
                device_id_type=mesh_type,
            ).wait_recv()

    total = recv[0].astype(jnp.float32)
    for k in range(1, slices):
        total = total + recv[k].astype(jnp.float32)
    middle[...] = total.astype(middle.dtype)

    picked = jnp.dot(
        pick_out_ref[...].reshape(-1, pick_out_ref.shape[2]),
        middle[...],
        preferred_element_type=jnp.float32,
    )
    outgoing[...] = picked.reshape(outgoing.shape).astype(outgoing.dtype)

    def stage3(u):
        return pltpu.make_async_remote_copy(
            outgoing.at[u], landing.at[t], send3.at[u], recv3.at[t],
            device_id=(s, u), device_id_type=mesh_type,
        )

    pltpu.make_async_copy(outgoing.at[t], landing.at[t], recv3.at[t]).start()
    for k in range(1, tp_size):
        stage3((t + k) % tp_size).start()

    pltpu.make_async_copy(outgoing.at[t], landing.at[t], recv3.at[t]).wait()
    for k in range(1, tp_size):
        u = (t + k) % tp_size
        stage3(u).wait_send()
        pltpu.make_async_remote_copy(
            outgoing.at[u], landing.at[u], send3.at[u], recv3.at[u],
            device_id=(s, u), device_id_type=mesh_type,
        ).wait_recv()

    out_ref[...] = landing[...]


def run_experts(sums, hidden, out_weight, gain, pick_in, gate_weight, up_weight, down_weight,
                pick_out, seq_size, tp_size, slices):
    tokens, width = hidden.shape
    rows = pick_in.shape[0]
    chunk = width // slices
    vmem = pl.BlockSpec(memory_space=pltpu.VMEM)
    hbm = pl.BlockSpec(memory_space=pl.ANY)
    return pl.pallas_call(
        functools.partial(expert_kernel, seq_size, tp_size, slices),
        out_shape=(
            jax.ShapeDtypeStruct((tp_size, tokens, chunk), jnp.bfloat16),
            jax.ShapeDtypeStruct((tokens, width), jnp.float32),
            jax.ShapeDtypeStruct((tokens, width), jnp.bfloat16),
        ),
        in_specs=[vmem, vmem, hbm, vmem, vmem, hbm, hbm, hbm, vmem],
        out_specs=(vmem, vmem, vmem),
        scratch_shapes=[
            pltpu.VMEM(out_weight.shape, out_weight.dtype),
            pltpu.VMEM(gate_weight.shape, gate_weight.dtype),
            pltpu.VMEM(up_weight.shape, up_weight.dtype),
            pltpu.VMEM(down_weight.shape, down_weight.dtype),
            pltpu.SemaphoreType.DMA((4,)),
            pltpu.VMEM((tokens, width), jnp.bfloat16),
            pltpu.VMEM((tokens, width), jnp.float32),
            pltpu.VMEM((tp_size, tokens, width), jnp.bfloat16),
            pltpu.VMEM((rows, width), jnp.bfloat16),
            pltpu.VMEM((slices, rows, chunk), jnp.bfloat16),
            pltpu.VMEM((rows, chunk), jnp.bfloat16),
            pltpu.VMEM((tp_size, tokens, chunk), jnp.bfloat16),
            pltpu.VMEM((tp_size, tokens, chunk), jnp.bfloat16),
            pltpu.SemaphoreType.DMA((tp_size,)),
            pltpu.SemaphoreType.DMA((tp_size,)),
            pltpu.SemaphoreType.DMA((slices,)),
            pltpu.SemaphoreType.DMA((slices,)),
            pltpu.SemaphoreType.DMA((tp_size,)),
            pltpu.SemaphoreType.DMA((tp_size,)),
        ],
        compiler_params=pltpu.CompilerParams(
            collective_id=1, has_side_effects=True
        ),
    )(sums, hidden, out_weight, gain, pick_in, gate_weight, up_weight, down_weight, pick_out)


def body(
    hidden_in,
    new_query,
    new_key,
    new_value,
    key_cache,
    value_cache,
    lengths,
    out_weight,
    norm_gain,
    router_weight,
    expert_ids,
    gate_weight,
    up_weight,
    down_weight,
):
    req_dev, steps, width = hidden_in.shape
    block = key_cache.shape[1]
    head_size = width // HEADS
    scale = head_size ** (-0.5)
    seq_index = lax.axis_index("seq")
    tp_index = lax.axis_index("tp")
    seq_size = lax.axis_size("seq")
    tp_size = lax.axis_size("tp")
    rows = steps * HEADS
    own = req_dev * steps

    head_mask = (jnp.arange(width) // head_size)[None, :] == jnp.arange(HEADS)[:, None]
    q_wide = jnp.where(head_mask[None, None], new_query[:, :, None, :], 0).reshape(
        req_dev, rows, width
    )
    positions = seq_index * block + jnp.arange(block, dtype=jnp.int32)
    usable = (positions[None, :] < lengths[:, None]).astype(jnp.float32)
    usable = jnp.broadcast_to(usable[:, None, :], (req_dev, 8, block))
    fresh_scores = (
        jnp.einsum("rqd,rsd->rqs", q_wide, new_key, preferred_element_type=jnp.float32) * scale
    )
    causal = (
        (jnp.arange(rows)[:, None] // HEADS) >= jnp.arange(steps)[None, :]
    ) & (seq_index == 0)
    fresh_scores = jnp.where(causal, fresh_scores, masked_score)
    fresh_scores = jnp.pad(
        fresh_scores, ((0, 0), (0, 0), (0, 128 - steps)), constant_values=masked_score
    )
    fresh_ok = jnp.pad(
        jnp.broadcast_to(causal, (req_dev, rows, steps)).astype(jnp.float32),
        ((0, 0), (0, 0), (0, 128 - steps)),
    )
    fresh_value = jnp.pad(new_value, ((0, 0), (0, 128 - steps), (0, 0)))
    id_count = expert_ids.size
    id_rows = 8
    id_piece = jnp.pad(expert_ids.reshape(1, id_count), ((0, id_rows - 1), (0, 128 - id_count)))
    block_sums, all_id_pieces = exchange(
        q_wide, key_cache, value_cache, usable, fresh_scores, fresh_ok, fresh_value, id_piece,
        seq_size, tp_size, scale,
    )
    all_ids = all_id_pieces[:, 0, :id_count].reshape(tp_size * req_dev, steps, -1)
    feature_block = width // seq_size
    experts = router_weight.shape[1]
    topk = expert_ids.shape[2]
    requests = req_dev * tp_size
    capacity = (5 * requests * topk + 4 * experts - 1) // (4 * experts)
    expert_range = jnp.arange(experts, dtype=jnp.int32)
    slices = seq_size * tp_size // experts
    groups = tp_size // slices
    halves = slices // seq_size
    padded = 8 * ((steps * capacity + 7) // 8)
    tokens = 16 * ((own + 15) // 16)

    onehot = all_ids[..., None] == expert_range
    hits = jnp.sum(onehot.astype(jnp.int32), axis=2)
    earlier = jnp.cumsum(hits, axis=0) - hits
    all_slots = jnp.sum(jnp.where(onehot, earlier[:, :, None, :], 0), axis=3)
    row_of = jnp.arange(steps, dtype=jnp.int32)[None, :, None] * capacity + all_slots

    def rows_for(expert):
        hit = (all_ids == expert) & (all_slots < capacity)
        chosen_rows = jnp.any(
            hit[..., None] & (row_of[..., None] == jnp.arange(padded)), axis=2
        ).reshape(tp_size, own, padded)
        return jnp.pad(chosen_rows, ((0, 0), (0, tokens - own), (0, 0))).astype(jnp.bfloat16)

    mine = (seq_index * tp_size + tp_index) // slices
    pick_in = rows_for(mine).reshape(tp_size * tokens, padded).T
    held = ((tp_index % slices) // halves) * groups + tp_index // slices
    pick_out = rows_for(held)
    hidden = jnp.pad(
        hidden_in.astype(jnp.float32).reshape(own, width), ((0, tokens - own), (0, 0))
    )
    landed, attention, normed = run_experts(
        block_sums, hidden, out_weight, norm_gain.reshape(1, width), pick_in, gate_weight,
        up_weight, down_weight, pick_out, seq_size, tp_size, slices,
    )
    attention = attention[:own].reshape(req_dev, steps, width)
    normed = normed[:own].reshape(req_dev, steps, width)
    attn_out = lax.dynamic_slice_in_dim(
        attention, seq_index * feature_block, feature_block, 2
    ).astype(jnp.bfloat16)
    residual = hidden_in.astype(jnp.float32) + attention

    logits = jnp.einsum("rtd,de->rte", normed, router_weight, preferred_element_type=jnp.float32)
    own_hot = expert_ids[..., None] == expert_range
    chosen = jnp.sum(jnp.where(own_hot, logits[:, :, None, :], 0.0), axis=3)
    share = 1.0 / (1.0 + jnp.exp(chosen[:, :, ::-1] - chosen))
    own_slots = lax.dynamic_slice_in_dim(all_slots, tp_index * req_dev, req_dev, 0)
    weight = jnp.where(own_slots < capacity, share, 0.0)
    slot_expert = (jnp.arange(tp_size // halves) % (tp_size // (groups * halves))) * groups + (
        jnp.arange(tp_size // halves) // (tp_size // (groups * halves))
    )
    per_slot = jnp.sum(
        jnp.where(expert_ids[..., None] == slot_expert, weight[..., None], 0.0), axis=2
    ).reshape(own, tp_size // halves)
    landed = landed.astype(jnp.float32).reshape(tp_size // halves, halves, tokens, feature_block // halves)
    mixture = jnp.einsum(
        "ia,ahif->ihf", per_slot, landed[:, :, :own], precision=lax.Precision.HIGHEST
    ).reshape(req_dev, steps, feature_block)
    own_residual = lax.dynamic_slice_in_dim(residual, seq_index * feature_block, feature_block, 2)
    layer_out = (own_residual + mixture).astype(jnp.bfloat16)
    return (attn_out, layer_out)


def solution(mesh):

    return jax.shard_map(
        body,
        mesh=mesh,
        in_specs=(
            P("tp", None, None),
            P("tp", None, None),
            P("tp", None, None),
            P("tp", None, None),
            P("tp", "seq", None),
            P("tp", "seq", None),
            P("tp"),
            P(),
            P(),
            P(),
            P("tp", None, None),
            P(("seq", "tp"), None),
            P(("seq", "tp"), None),
            P(("seq", "tp"), None),
        ),
        out_specs=(P("tp", None, "seq"), P("tp", None, "seq")),
        check_vma=False,
    )
```

```python
import functools

import jax
import jax.numpy as jnp
from jax import lax
from jax.experimental import pallas as pl
from jax.experimental.pallas import tpu as pltpu
from jax.sharding import PartitionSpec as P

HEADS = 16


masked_score = -1e30
norm_epsilon = 1e-06


def exchange_kernel(seq_size, tp_size, scale, query_ref, key_hbm, value_hbm, usable_ref,
                    fresh_ref, fresh_ok_ref, fresh_value_ref, ids_ref, sums_out,
                    ids_out, keys, values, sums, sums_land, ids_land,
                    load_sem, send_a, recv_a, send_b, recv_b):
    mesh_type = pl.DeviceIdType.MESH
    s = lax.axis_index("seq")
    t = lax.axis_index("tp")
    req_dev, rows, width = query_ref.shape
    heads = HEADS

    barrier = pltpu.get_barrier_semaphore()
    for u in range(seq_size):
        @pl.when(s != u)
        def _():
            pl.semaphore_signal(barrier, inc=1, device_id=(u, t), device_id_type=mesh_type)
    for u in range(tp_size):
        @pl.when(t != u)
        def _():
            pl.semaphore_signal(barrier, inc=1, device_id=(s, u), device_id_type=mesh_type)

    loads = []
    for r in range(req_dev):
        loads.append(pltpu.make_async_copy(key_hbm.at[r], keys.at[r], load_sem.at[0, r]))
        loads.append(pltpu.make_async_copy(value_hbm.at[r], values.at[r], load_sem.at[1, r]))
    for copy in loads:
        copy.start()

    head_of = lax.broadcasted_iota(jnp.int32, (rows, width), 1) // (width // heads)
    row_head = lax.broadcasted_iota(jnp.int32, (rows, width), 0) % heads
    own_head = head_of == row_head
    spread = (
        lax.broadcasted_iota(jnp.int32, (rows // heads, rows), 1) // heads
        == lax.broadcasted_iota(jnp.int32, (rows // heads, rows), 0)
    ).astype(jnp.float32)
    contract = (((1,), (1,)), ((), ()))
    for r in range(req_dev):
        loads[2 * r].wait()
        scores = lax.dot_general(
            query_ref[r], keys[r], contract, preferred_element_type=jnp.float32
        ) * scale
        usable = usable_ref[r, 0:1, :] > 0.5
        scores = jnp.where(usable, scores, masked_score)
        fresh = fresh_ref[r]
        fresh_ok = fresh_ok_ref[r] > 0.5
        top = jnp.maximum(
            jnp.max(scores, axis=1, keepdims=True), jnp.max(fresh, axis=1, keepdims=True)
        )
        weights = jnp.where(usable, jnp.exp(scores - top), 0.0)
        fresh_weights = jnp.where(fresh_ok, jnp.exp(fresh - top), 0.0)
        total = jnp.sum(weights, axis=1, keepdims=True) + jnp.sum(
            fresh_weights, axis=1, keepdims=True
        )
        loads[2 * r + 1].wait()
        wide = jnp.dot(
            weights.astype(jnp.bfloat16), values[r], preferred_element_type=jnp.float32
        ) + jnp.dot(
            fresh_weights.astype(jnp.bfloat16), fresh_value_ref[r],
            preferred_element_type=jnp.float32,
        )
        wide = jnp.where(own_head, wide, 0.0)
        steps = rows // heads
        sums[r, 0:steps, :] = jnp.sum(wide.reshape(steps, heads, width), axis=1)
        sums[r, steps : 2 * steps, :] = jnp.dot(
            spread, jnp.where(own_head, top, 0.0),
            precision=lax.Precision.HIGHEST, preferred_element_type=jnp.float32,
        )
        sums[r, 2 * steps : 3 * steps, :] = jnp.dot(
            spread, jnp.where(own_head, total, 0.0),
            precision=lax.Precision.HIGHEST, preferred_element_type=jnp.float32,
        )
        sums[r, 3 * steps :, :] = jnp.zeros((sums.shape[1] - 3 * steps, width), jnp.float32)

    pl.semaphore_wait(barrier, seq_size - 1 + tp_size - 1)

    def sums_copy(u, slot):
        return pltpu.make_async_remote_copy(
            sums, sums_land.at[slot], send_a.at[u], recv_a.at[slot],
            device_id=(u, t), device_id_type=mesh_type,
        )

    def along_tp(u, slot):
        return pltpu.make_async_remote_copy(
            ids_ref, ids_land.at[slot], send_b.at[u], recv_b.at[slot],
            device_id=(s, u), device_id_type=mesh_type,
        )

    pltpu.make_async_copy(sums, sums_land.at[s], recv_a.at[s]).start()
    for k in range(1, seq_size):
        sums_copy((s + k) % seq_size, s).start()
    pltpu.make_async_copy(ids_ref, ids_land.at[t], recv_b.at[t]).start()
    for k in range(1, tp_size):
        along_tp((t + k) % tp_size, t).start()

    pltpu.make_async_copy(sums, sums_land.at[s], recv_a.at[s]).wait()
    for k in range(1, seq_size):
        u = (s + k) % seq_size
        sums_copy(u, s).wait_send()
        sums_copy(u, u).wait_recv()
    pltpu.make_async_copy(ids_ref, ids_land.at[t], recv_b.at[t]).wait()
    for k in range(1, tp_size):
        u = (t + k) % tp_size
        along_tp(u, t).wait_send()
        along_tp(u, u).wait_recv()

    sums_out[...] = sums_land[...]
    ids_out[...] = ids_land[...]


def exchange(query, key_cache, value_cache, usable, fresh, fresh_ok, fresh_value, ids,
             seq_size, tp_size, scale):
    req_dev, rows, width = query.shape
    steps = rows // HEADS
    vmem = pl.BlockSpec(memory_space=pltpu.VMEM)
    return pl.pallas_call(
        functools.partial(exchange_kernel, seq_size, tp_size, scale),
        out_shape=(
            jax.ShapeDtypeStruct((seq_size, req_dev, 4 * steps, width), jnp.float32),
            jax.ShapeDtypeStruct((tp_size,) + ids.shape, ids.dtype),
        ),
        in_specs=[vmem, pl.BlockSpec(memory_space=pl.ANY), pl.BlockSpec(memory_space=pl.ANY)]
        + [vmem] * 5,
        out_specs=(vmem, vmem),
        scratch_shapes=[
            pltpu.VMEM(key_cache.shape, key_cache.dtype),
            pltpu.VMEM(value_cache.shape, value_cache.dtype),
            pltpu.VMEM((req_dev, 4 * steps, width), jnp.float32),
            pltpu.VMEM((seq_size, req_dev, 4 * steps, width), jnp.float32),
            pltpu.VMEM((tp_size,) + ids.shape, ids.dtype),
            pltpu.SemaphoreType.DMA((2, req_dev)),
            pltpu.SemaphoreType.DMA((seq_size,)),
            pltpu.SemaphoreType.DMA((seq_size,)),
            pltpu.SemaphoreType.DMA((tp_size,)),
            pltpu.SemaphoreType.DMA((tp_size,)),
        ],
        compiler_params=pltpu.CompilerParams(
            collective_id=0, has_side_effects=True, vmem_limit_bytes=48 * 1024 * 1024
        ),
    )(query, key_cache, value_cache, usable, fresh, fresh_ok, fresh_value, ids)


def expert_kernel(seq_size, tp_size, slices, sums_ref, hidden_ref, out_weight_hbm, gain_ref,
                  pick_in_ref, gate_hbm, up_hbm, down_hbm, pick_out_ref, out_ref, attn_ref,
                  normed_ref, out_weight_ref, gate_ref, up_ref, down_ref, load_sem, piece_ref,
                  context, everyone, part, recv, middle, outgoing, landing, send0, recv0,
                  send1, recv1, send3, recv3):
    mesh_type = pl.DeviceIdType.MESH
    s = lax.axis_index("seq")
    t = lax.axis_index("tp")
    g = t // slices
    j = t % slices
    chunk = recv.shape[2]
    halves = slices // seq_size
    src_seq = j // halves

    def dest(i):
        return (i // halves, g * slices + s * halves + i % halves)

    def is_self(i):
        return (i // halves == s) & (g * slices + s * halves + i % halves == t)

    barrier = pltpu.get_barrier_semaphore()
    for u in range(tp_size):
        @pl.when(t != u)
        def _():
            pl.semaphore_signal(barrier, inc=1, device_id=(s, u), device_id_type=mesh_type)
    for i in range(slices):
        @pl.when(i // halves != s)
        def _():
            pl.semaphore_signal(barrier, inc=1, device_id=dest(i), device_id_type=mesh_type)
    for k in range(slices):
        @pl.when((src_seq != s) & (k // halves != s))
        def _():
            pl.semaphore_signal(
                barrier, inc=1, device_id=(src_seq, g * slices + k), device_id_type=mesh_type
            )
    loads = [
        pltpu.make_async_copy(src_hbm, dst, load_sem.at[n])
        for n, (src_hbm, dst) in enumerate(
            [(out_weight_hbm, out_weight_ref), (gate_hbm, gate_ref), (up_hbm, up_ref),
             (down_hbm, down_ref)]
        )
    ]
    for copy in loads:
        copy.start()

    req_dev = sums_ref.shape[1]
    steps = sums_ref.shape[2] // 4
    context[...] = jnp.zeros_like(context)
    for r in range(req_dev):
        block_sums = [sums_ref[b, r, 0:steps, :] for b in range(seq_size)]
        block_max = [sums_ref[b, r, steps : 2 * steps, :] for b in range(seq_size)]
        block_totals = [sums_ref[b, r, 2 * steps : 3 * steps, :] for b in range(seq_size)]
        overall = block_max[0]
        for b in range(1, seq_size):
            overall = jnp.maximum(overall, block_max[b])
        numer = jnp.zeros_like(overall)
        denom = jnp.zeros_like(overall)
        for b in range(seq_size):
            factor = jnp.exp(block_max[b] - overall)
            numer = numer + factor * block_sums[b]
            denom = denom + factor * block_totals[b]
        context[r * steps : (r + 1) * steps, :] = numer / denom
    loads[0].wait()
    attention = jnp.dot(
        context[...].astype(jnp.bfloat16), out_weight_ref[...], preferred_element_type=jnp.float32
    )
    attn_ref[...] = attention
    residual = hidden_ref[...] + attention
    mean_square = jnp.mean(residual * residual, axis=1, keepdims=True)
    normed = (residual * lax.rsqrt(mean_square + norm_epsilon) * gain_ref[...]).astype(
        jnp.bfloat16
    )
    piece_ref[...] = normed
    normed_ref[...] = normed

    far = (seq_size - 1) * halves
    near = tp_size - 1 + far

    @pl.when(src_seq == s)
    def _():
        pl.semaphore_wait(barrier, near)

    @pl.when(src_seq != s)
    def _():
        pl.semaphore_wait(barrier, near + slices - halves)

    def gather(u, slot):
        return pltpu.make_async_remote_copy(
            piece_ref, everyone.at[slot], send0.at[u], recv0.at[slot],
            device_id=(s, u), device_id_type=mesh_type,
        )

    pltpu.make_async_copy(piece_ref, everyone.at[t], recv0.at[t]).start()
    for k in range(1, tp_size):
        gather((t + k) % tp_size, t).start()

    pltpu.make_async_copy(piece_ref, everyone.at[t], recv0.at[t]).wait()
    for k in range(1, tp_size):
        u = (t + k) % tp_size
        gather(u, t).wait_send()
        gather(u, u).wait_recv()

    for copy in loads[1:]:
        copy.wait()
    rows_in = everyone[...].reshape(-1, everyone.shape[2])
    buffer = jnp.dot(pick_in_ref[...], rows_in, preferred_element_type=jnp.float32).astype(
        jnp.bfloat16
    )
    contract = (((1,), (1,)), ((), ()))
    gate = lax.dot_general(buffer, gate_ref[...], contract, preferred_element_type=jnp.float32)
    upward = lax.dot_general(buffer, up_ref[...], contract, preferred_element_type=jnp.float32)
    inner = (jax.nn.gelu(gate) * upward).astype(jnp.bfloat16)
    part[...] = jnp.dot(inner, down_ref[...], preferred_element_type=jnp.float32).astype(
        part.dtype
    )

    def stage1(i):
        return pltpu.make_async_remote_copy(
            part.at[:, pl.ds(pl.multiple_of(i * chunk, chunk), chunk)],
            recv.at[j],
            send1.at[i],
            recv1.at[j],
            device_id=dest(i),
            device_id_type=mesh_type,
        )

    for k in range(slices):
        i = (j + k) % slices

        @pl.when(is_self(i))
        def _():
            pltpu.make_async_copy(
                part.at[:, pl.ds(pl.multiple_of(i * chunk, chunk), chunk)], recv.at[j], recv1.at[j]
            ).start()

        @pl.when(jnp.logical_not(is_self(i)))
        def _():
            stage1(i).start()

    for i in range(slices):
        @pl.when(jnp.logical_not(is_self(i)))
        def _():
            stage1(i).wait_send()

    for k in range(slices):
        from_self = (src_seq == s) & (k == j)

        @pl.when(from_self)
        def _():
            pltpu.make_async_copy(part.at[:, pl.ds(0, chunk)], recv.at[k], recv1.at[k]).wait()

        @pl.when(jnp.logical_not(from_self))
        def _():
            pltpu.make_async_remote_copy(
                part.at[:, pl.ds(0, chunk)],
                recv.at[k],
                send1.at[0],
                recv1.at[k],
                device_id=(src_seq, g * slices + k),
                device_id_type=mesh_type,
            ).wait_recv()

    total = recv[0].astype(jnp.float32)
    for k in range(1, slices):
        total = total + recv[k].astype(jnp.float32)
    middle[...] = total.astype(middle.dtype)

    picked = jnp.dot(
        pick_out_ref[...].reshape(-1, pick_out_ref.shape[2]),
        middle[...],
        preferred_element_type=jnp.float32,
    )
    outgoing[...] = picked.reshape(outgoing.shape).astype(outgoing.dtype)

    def stage3(u):
        return pltpu.make_async_remote_copy(
            outgoing.at[u], landing.at[t], send3.at[u], recv3.at[t],
            device_id=(s, u), device_id_type=mesh_type,
        )

    pltpu.make_async_copy(outgoing.at[t], landing.at[t], recv3.at[t]).start()
    for k in range(1, tp_size):
        stage3((t + k) % tp_size).start()

    pltpu.make_async_copy(outgoing.at[t], landing.at[t], recv3.at[t]).wait()
    for k in range(1, tp_size):
        u = (t + k) % tp_size
        stage3(u).wait_send()
        pltpu.make_async_remote_copy(
            outgoing.at[u], landing.at[u], send3.at[u], recv3.at[u],
            device_id=(s, u), device_id_type=mesh_type,
        ).wait_recv()

    out_ref[...] = landing[...]


def run_experts(sums, hidden, out_weight, gain, pick_in, gate_weight, up_weight, down_weight,
                pick_out, seq_size, tp_size, slices):
    tokens, width = hidden.shape
    rows = pick_in.shape[0]
    chunk = width // slices
    vmem = pl.BlockSpec(memory_space=pltpu.VMEM)
    hbm = pl.BlockSpec(memory_space=pl.ANY)
    return pl.pallas_call(
        functools.partial(expert_kernel, seq_size, tp_size, slices),
        out_shape=(
            jax.ShapeDtypeStruct((tp_size, tokens, chunk), jnp.bfloat16),
            jax.ShapeDtypeStruct((tokens, width), jnp.float32),
            jax.ShapeDtypeStruct((tokens, width), jnp.bfloat16),
        ),
        in_specs=[vmem, vmem, hbm, vmem, vmem, hbm, hbm, hbm, vmem],
        out_specs=(vmem, vmem, vmem),
        scratch_shapes=[
            pltpu.VMEM(out_weight.shape, out_weight.dtype),
            pltpu.VMEM(gate_weight.shape, gate_weight.dtype),
            pltpu.VMEM(up_weight.shape, up_weight.dtype),
            pltpu.VMEM(down_weight.shape, down_weight.dtype),
            pltpu.SemaphoreType.DMA((4,)),
            pltpu.VMEM((tokens, width), jnp.bfloat16),
            pltpu.VMEM((tokens, width), jnp.float32),
            pltpu.VMEM((tp_size, tokens, width), jnp.bfloat16),
            pltpu.VMEM((rows, width), jnp.bfloat16),
            pltpu.VMEM((slices, rows, chunk), jnp.bfloat16),
            pltpu.VMEM((rows, chunk), jnp.bfloat16),
            pltpu.VMEM((tp_size, tokens, chunk), jnp.bfloat16),
            pltpu.VMEM((tp_size, tokens, chunk), jnp.bfloat16),
            pltpu.SemaphoreType.DMA((tp_size,)),
            pltpu.SemaphoreType.DMA((tp_size,)),
            pltpu.SemaphoreType.DMA((slices,)),
            pltpu.SemaphoreType.DMA((slices,)),
            pltpu.SemaphoreType.DMA((tp_size,)),
            pltpu.SemaphoreType.DMA((tp_size,)),
        ],
        compiler_params=pltpu.CompilerParams(
            collective_id=1, has_side_effects=True
        ),
    )(sums, hidden, out_weight, gain, pick_in, gate_weight, up_weight, down_weight, pick_out)


def body(
    hidden_in,
    new_query,
    new_key,
    new_value,
    key_cache,
    value_cache,
    lengths,
    out_weight,
    norm_gain,
    router_weight,
    expert_ids,
    gate_weight,
    up_weight,
    down_weight,
):
    req_dev, steps, width = hidden_in.shape
    block = key_cache.shape[1]
    head_size = width // HEADS
    scale = head_size ** (-0.5)
    seq_index = lax.axis_index("seq")
    tp_index = lax.axis_index("tp")
    seq_size = lax.axis_size("seq")
    tp_size = lax.axis_size("tp")
    rows = steps * HEADS
    own = req_dev * steps

    head_mask = (jnp.arange(width) // head_size)[None, :] == jnp.arange(HEADS)[:, None]
    q_wide = jnp.where(head_mask[None, None], new_query[:, :, None, :], 0).reshape(
        req_dev, rows, width
    )
    positions = seq_index * block + jnp.arange(block, dtype=jnp.int32)
    usable = (positions[None, :] < lengths[:, None]).astype(jnp.float32)
    usable = jnp.broadcast_to(usable[:, None, :], (req_dev, 8, block))
    fresh_scores = (
        jnp.einsum("rqd,rsd->rqs", q_wide, new_key, preferred_element_type=jnp.float32) * scale
    )
    causal = (
        (jnp.arange(rows)[:, None] // HEADS) >= jnp.arange(steps)[None, :]
    ) & (seq_index == 0)
    fresh_scores = jnp.where(causal, fresh_scores, masked_score)
    fresh_scores = jnp.pad(
        fresh_scores, ((0, 0), (0, 0), (0, 128 - steps)), constant_values=masked_score
    )
    fresh_ok = jnp.pad(
        jnp.broadcast_to(causal, (req_dev, rows, steps)).astype(jnp.float32),
        ((0, 0), (0, 0), (0, 128 - steps)),
    )
    fresh_value = jnp.pad(new_value, ((0, 0), (0, 128 - steps), (0, 0)))
    id_count = expert_ids.size
    id_rows = 8
    id_piece = jnp.pad(expert_ids.reshape(1, id_count), ((0, id_rows - 1), (0, 128 - id_count)))
    block_sums, all_id_pieces = exchange(
        q_wide, key_cache, value_cache, usable, fresh_scores, fresh_ok, fresh_value, id_piece,
        seq_size, tp_size, scale,
    )
    all_ids = all_id_pieces[:, 0, :id_count].reshape(tp_size * req_dev, steps, -1)
    feature_block = width // seq_size
    experts = router_weight.shape[1]
    topk = expert_ids.shape[2]
    requests = req_dev * tp_size
    capacity = (5 * requests * topk + 4 * experts - 1) // (4 * experts)
    expert_range = jnp.arange(experts, dtype=jnp.int32)
    slices = seq_size * tp_size // experts
    groups = tp_size // slices
    halves = slices // seq_size
    padded = 8 * ((steps * capacity + 7) // 8)
    tokens = 16 * ((own + 15) // 16)

    onehot = all_ids[..., None] == expert_range
    hits = jnp.sum(onehot.astype(jnp.int32), axis=2)
    earlier = jnp.cumsum(hits, axis=0) - hits
    all_slots = jnp.sum(jnp.where(onehot, earlier[:, :, None, :], 0), axis=3)
    row_of = jnp.arange(steps, dtype=jnp.int32)[None, :, None] * capacity + all_slots

    def rows_for(expert):
        hit = (all_ids == expert) & (all_slots < capacity)
        chosen_rows = jnp.any(
            hit[..., None] & (row_of[..., None] == jnp.arange(padded)), axis=2
        ).reshape(tp_size, own, padded)
        return jnp.pad(chosen_rows, ((0, 0), (0, tokens - own), (0, 0))).astype(jnp.bfloat16)

    mine = (seq_index * tp_size + tp_index) // slices
    pick_in = rows_for(mine).reshape(tp_size * tokens, padded).T
    held = ((tp_index % slices) // halves) * groups + tp_index // slices
    pick_out = rows_for(held)
    hidden = jnp.pad(
        hidden_in.astype(jnp.float32).reshape(own, width), ((0, tokens - own), (0, 0))
    )
    landed, attention, normed = run_experts(
        block_sums, hidden, out_weight, norm_gain.reshape(1, width), pick_in, gate_weight,
        up_weight, down_weight, pick_out, seq_size, tp_size, slices,
    )
    attention = attention[:own].reshape(req_dev, steps, width)
    normed = normed[:own].reshape(req_dev, steps, width)
    attn_out = lax.dynamic_slice_in_dim(
        attention, seq_index * feature_block, feature_block, 2
    ).astype(jnp.bfloat16)
    residual = hidden_in.astype(jnp.float32) + attention

    logits = jnp.einsum("rtd,de->rte", normed, router_weight, preferred_element_type=jnp.float32)
    own_hot = expert_ids[..., None] == expert_range
    chosen = jnp.sum(jnp.where(own_hot, logits[:, :, None, :], 0.0), axis=3)
    share = 1.0 / (1.0 + jnp.exp(chosen[:, :, ::-1] - chosen))
    own_slots = lax.dynamic_slice_in_dim(all_slots, tp_index * req_dev, req_dev, 0)
    weight = jnp.where(own_slots < capacity, share, 0.0)
    slot_expert = (jnp.arange(tp_size // halves) % (tp_size // (groups * halves))) * groups + (
        jnp.arange(tp_size // halves) // (tp_size // (groups * halves))
    )
    per_slot = jnp.sum(
        jnp.where(expert_ids[..., None] == slot_expert, weight[..., None], 0.0), axis=2
    ).reshape(own, tp_size // halves)
    landed = landed.astype(jnp.float32).reshape(tp_size // halves, halves, tokens, feature_block // halves)
    mixture = jnp.einsum(
        "ia,ahif->ihf", per_slot, landed[:, :, :own], precision=lax.Precision.HIGHEST
    ).reshape(req_dev, steps, feature_block)
    own_residual = lax.dynamic_slice_in_dim(residual, seq_index * feature_block, feature_block, 2)
    layer_out = (own_residual + mixture).astype(jnp.bfloat16)
    return (attn_out, layer_out)


def solution(mesh):

    return jax.shard_map(
        body,
        mesh=mesh,
        in_specs=(
            P("tp", None, None),
            P("tp", None, None),
            P("tp", None, None),
            P("tp", None, None),
            P("tp", "seq", None),
            P("tp", "seq", None),
            P("tp"),
            P(),
            P(),
            P(),
            P("tp", None, None),
            P(("seq", "tp"), None),
            P(("seq", "tp"), None),
            P(("seq", "tp"), None),
        ),
        out_specs=(P("tp", None, "seq"), P("tp", None, "seq")),
        check_vma=False,
    )
```

```python
import functools

import jax
import jax.numpy as jnp
from jax import lax
from jax.experimental import pallas as pl
from jax.experimental.pallas import tpu as pltpu
from jax.sharding import PartitionSpec as P

HEADS = 16


masked_score = -1e30
norm_epsilon = 1e-06


def exchange_kernel(seq_size, tp_size, scale, query_ref, key_hbm, value_hbm, usable_ref,
                    fresh_ref, fresh_ok_ref, fresh_value_ref, ids_ref, sums_out,
                    ids_out, keys, values, sums, sums_land, ids_land,
                    load_sem, send_a, recv_a, send_b, recv_b):
    mesh_type = pl.DeviceIdType.MESH
    s = lax.axis_index("seq")
    t = lax.axis_index("tp")
    req_dev, rows, width = query_ref.shape
    heads = HEADS

    barrier = pltpu.get_barrier_semaphore()
    for u in range(seq_size):
        @pl.when(s != u)
        def _():
            pl.semaphore_signal(barrier, inc=1, device_id=(u, t), device_id_type=mesh_type)
    for u in range(tp_size):
        @pl.when(t != u)
        def _():
            pl.semaphore_signal(barrier, inc=1, device_id=(s, u), device_id_type=mesh_type)

    loads = []
    for r in range(req_dev):
        loads.append(pltpu.make_async_copy(key_hbm.at[r], keys.at[r], load_sem.at[0, r]))
        loads.append(pltpu.make_async_copy(value_hbm.at[r], values.at[r], load_sem.at[1, r]))
    for copy in loads:
        copy.start()

    head_of = lax.broadcasted_iota(jnp.int32, (rows, width), 1) // (width // heads)
    row_head = lax.broadcasted_iota(jnp.int32, (rows, width), 0) % heads
    own_head = head_of == row_head
    spread = (
        lax.broadcasted_iota(jnp.int32, (rows // heads, rows), 1) // heads
        == lax.broadcasted_iota(jnp.int32, (rows // heads, rows), 0)
    ).astype(jnp.float32)
    contract = (((1,), (1,)), ((), ()))
    for r in range(req_dev):
        loads[2 * r].wait()
        scores = lax.dot_general(
            query_ref[r], keys[r], contract, preferred_element_type=jnp.float32
        ) * scale
        usable = usable_ref[r, 0:1, :] > 0.5
        scores = jnp.where(usable, scores, masked_score)
        fresh = fresh_ref[r]
        fresh_ok = fresh_ok_ref[r] > 0.5
        top = jnp.maximum(
            jnp.max(scores, axis=1, keepdims=True), jnp.max(fresh, axis=1, keepdims=True)
        )
        weights = jnp.where(usable, jnp.exp(scores - top), 0.0)
        fresh_weights = jnp.where(fresh_ok, jnp.exp(fresh - top), 0.0)
        total = jnp.sum(weights, axis=1, keepdims=True) + jnp.sum(
            fresh_weights, axis=1, keepdims=True
        )
        loads[2 * r + 1].wait()
        wide = jnp.dot(
            weights.astype(jnp.bfloat16), values[r], preferred_element_type=jnp.float32
        ) + jnp.dot(
            fresh_weights.astype(jnp.bfloat16), fresh_value_ref[r],
            preferred_element_type=jnp.float32,
        )
        wide = jnp.where(own_head, wide, 0.0)
        steps = rows // heads
        sums[r, 0:steps, :] = jnp.sum(wide.reshape(steps, heads, width), axis=1)
        sums[r, steps : 2 * steps, :] = jnp.dot(
            spread, jnp.where(own_head, top, 0.0),
            precision=lax.Precision.HIGHEST, preferred_element_type=jnp.float32,
        )
        sums[r, 2 * steps : 3 * steps, :] = jnp.dot(
            spread, jnp.where(own_head, total, 0.0),
            precision=lax.Precision.HIGHEST, preferred_element_type=jnp.float32,
        )
        sums[r, 3 * steps :, :] = jnp.zeros((sums.shape[1] - 3 * steps, width), jnp.float32)

    pl.semaphore_wait(barrier, seq_size - 1 + tp_size - 1)

    def sums_copy(u, slot):
        return pltpu.make_async_remote_copy(
            sums, sums_land.at[slot], send_a.at[u], recv_a.at[slot],
            device_id=(u, t), device_id_type=mesh_type,
        )

    def along_tp(u, slot):
        return pltpu.make_async_remote_copy(
            ids_ref, ids_land.at[slot], send_b.at[u], recv_b.at[slot],
            device_id=(s, u), device_id_type=mesh_type,
        )

    pltpu.make_async_copy(sums, sums_land.at[s], recv_a.at[s]).start()
    for k in range(1, seq_size):
        sums_copy((s + k) % seq_size, s).start()
    pltpu.make_async_copy(ids_ref, ids_land.at[t], recv_b.at[t]).start()
    for k in range(1, tp_size):
        along_tp((t + k) % tp_size, t).start()

    pltpu.make_async_copy(sums, sums_land.at[s], recv_a.at[s]).wait()
    for k in range(1, seq_size):
        u = (s + k) % seq_size
        sums_copy(u, s).wait_send()
        sums_copy(u, u).wait_recv()
    pltpu.make_async_copy(ids_ref, ids_land.at[t], recv_b.at[t]).wait()
    for k in range(1, tp_size):
        u = (t + k) % tp_size
        along_tp(u, t).wait_send()
        along_tp(u, u).wait_recv()

    sums_out[...] = sums_land[...]
    ids_out[...] = ids_land[...]


def exchange(query, key_cache, value_cache, usable, fresh, fresh_ok, fresh_value, ids,
             seq_size, tp_size, scale):
    req_dev, rows, width = query.shape
    steps = rows // HEADS
    vmem = pl.BlockSpec(memory_space=pltpu.VMEM)
    return pl.pallas_call(
        functools.partial(exchange_kernel, seq_size, tp_size, scale),
        out_shape=(
            jax.ShapeDtypeStruct((seq_size, req_dev, 4 * steps, width), jnp.float32),
            jax.ShapeDtypeStruct((tp_size,) + ids.shape, ids.dtype),
        ),
        in_specs=[vmem, pl.BlockSpec(memory_space=pl.ANY), pl.BlockSpec(memory_space=pl.ANY)]
        + [vmem] * 5,
        out_specs=(vmem, vmem),
        scratch_shapes=[
            pltpu.VMEM(key_cache.shape, key_cache.dtype),
            pltpu.VMEM(value_cache.shape, value_cache.dtype),
            pltpu.VMEM((req_dev, 4 * steps, width), jnp.float32),
            pltpu.VMEM((seq_size, req_dev, 4 * steps, width), jnp.float32),
            pltpu.VMEM((tp_size,) + ids.shape, ids.dtype),
            pltpu.SemaphoreType.DMA((2, req_dev)),
            pltpu.SemaphoreType.DMA((seq_size,)),
            pltpu.SemaphoreType.DMA((seq_size,)),
            pltpu.SemaphoreType.DMA((tp_size,)),
            pltpu.SemaphoreType.DMA((tp_size,)),
        ],
        compiler_params=pltpu.CompilerParams(
            collective_id=0, has_side_effects=True, vmem_limit_bytes=48 * 1024 * 1024
        ),
    )(query, key_cache, value_cache, usable, fresh, fresh_ok, fresh_value, ids)


def expert_kernel(seq_size, tp_size, slices, sums_ref, hidden_ref, out_weight_hbm, gain_ref,
                  pick_in_ref, gate_hbm, up_hbm, down_hbm, pick_out_ref, out_ref, attn_ref,
                  normed_ref, out_weight_ref, gate_ref, up_ref, down_ref, load_sem, piece_ref,
                  context, everyone, part, recv, middle, outgoing, landing, send0, recv0,
                  send1, recv1, send3, recv3):
    mesh_type = pl.DeviceIdType.MESH
    s = lax.axis_index("seq")
    t = lax.axis_index("tp")
    g = t // slices
    j = t % slices
    chunk = recv.shape[2]
    halves = slices // seq_size
    src_seq = j // halves

    def dest(i):
        return (i // halves, g * slices + s * halves + i % halves)

    def is_self(i):
        return (i // halves == s) & (g * slices + s * halves + i % halves == t)

    barrier = pltpu.get_barrier_semaphore()
    for u in range(tp_size):
        @pl.when(t != u)
        def _():
            pl.semaphore_signal(barrier, inc=1, device_id=(s, u), device_id_type=mesh_type)
    for i in range(slices):
        @pl.when(i // halves != s)
        def _():
            pl.semaphore_signal(barrier, inc=1, device_id=dest(i), device_id_type=mesh_type)
    for k in range(slices):
        @pl.when((src_seq != s) & (k // halves != s))
        def _():
            pl.semaphore_signal(
                barrier, inc=1, device_id=(src_seq, g * slices + k), device_id_type=mesh_type
            )
    loads = [
        pltpu.make_async_copy(src_hbm, dst, load_sem.at[n])
        for n, (src_hbm, dst) in enumerate(
            [(out_weight_hbm, out_weight_ref), (gate_hbm, gate_ref), (up_hbm, up_ref),
             (down_hbm, down_ref)]
        )
    ]
    for copy in loads:
        copy.start()

    req_dev = sums_ref.shape[1]
    steps = sums_ref.shape[2] // 4
    context[...] = jnp.zeros_like(context)
    for r in range(req_dev):
        block_sums = [sums_ref[b, r, 0:steps, :] for b in range(seq_size)]
        block_max = [sums_ref[b, r, steps : 2 * steps, :] for b in range(seq_size)]
        block_totals = [sums_ref[b, r, 2 * steps : 3 * steps, :] for b in range(seq_size)]
        overall = block_max[0]
        for b in range(1, seq_size):
            overall = jnp.maximum(overall, block_max[b])
        numer = jnp.zeros_like(overall)
        denom = jnp.zeros_like(overall)
        for b in range(seq_size):
            factor = jnp.exp(block_max[b] - overall)
            numer = numer + factor * block_sums[b]
            denom = denom + factor * block_totals[b]
        context[r * steps : (r + 1) * steps, :] = numer / denom
    loads[0].wait()
    attention = jnp.dot(
        context[...].astype(jnp.bfloat16), out_weight_ref[...], preferred_element_type=jnp.float32
    )
    attn_ref[...] = attention
    residual = hidden_ref[...] + attention
    mean_square = jnp.mean(residual * residual, axis=1, keepdims=True)
    normed = (residual * lax.rsqrt(mean_square + norm_epsilon) * gain_ref[...]).astype(
        jnp.bfloat16
    )
    piece_ref[...] = normed
    normed_ref[...] = normed

    far = (seq_size - 1) * halves
    near = tp_size - 1 + far

    @pl.when(src_seq == s)
    def _():
        pl.semaphore_wait(barrier, near)

    @pl.when(src_seq != s)
    def _():
        pl.semaphore_wait(barrier, near + slices - halves)

    def gather(u, slot):
        return pltpu.make_async_remote_copy(
            piece_ref, everyone.at[slot], send0.at[u], recv0.at[slot],
            device_id=(s, u), device_id_type=mesh_type,
        )

    pltpu.make_async_copy(piece_ref, everyone.at[t], recv0.at[t]).start()
    for k in range(1, tp_size):
        gather((t + k) % tp_size, t).start()

    pltpu.make_async_copy(piece_ref, everyone.at[t], recv0.at[t]).wait()
    for k in range(1, tp_size):
        u = (t + k) % tp_size
        gather(u, t).wait_send()
        gather(u, u).wait_recv()

    for copy in loads[1:]:
        copy.wait()
    rows_in = everyone[...].reshape(-1, everyone.shape[2])
    buffer = jnp.dot(pick_in_ref[...], rows_in, preferred_element_type=jnp.float32).astype(
        jnp.bfloat16
    )
    contract = (((1,), (1,)), ((), ()))
    gate = lax.dot_general(buffer, gate_ref[...], contract, preferred_element_type=jnp.float32)
    upward = lax.dot_general(buffer, up_ref[...], contract, preferred_element_type=jnp.float32)
    inner = (jax.nn.gelu(gate) * upward).astype(jnp.bfloat16)
    part[...] = jnp.dot(inner, down_ref[...], preferred_element_type=jnp.float32).astype(
        part.dtype
    )

    def stage1(i):
        return pltpu.make_async_remote_copy(
            part.at[:, pl.ds(i * chunk, chunk)],
            recv.at[j],
            send1.at[i],
            recv1.at[j],
            device_id=dest(i),
            device_id_type=mesh_type,
        )

    for i in range(slices):
        @pl.when(is_self(i))
        def _():
            pltpu.make_async_copy(part.at[:, pl.ds(i * chunk, chunk)], recv.at[j], recv1.at[j]).start()

        @pl.when(jnp.logical_not(is_self(i)))
        def _():
            stage1(i).start()

    for i in range(slices):
        @pl.when(jnp.logical_not(is_self(i)))
        def _():
            stage1(i).wait_send()

    for k in range(slices):
        from_self = (src_seq == s) & (k == j)

        @pl.when(from_self)
        def _():
            pltpu.make_async_copy(part.at[:, pl.ds(0, chunk)], recv.at[k], recv1.at[k]).wait()

        @pl.when(jnp.logical_not(from_self))
        def _():
            pltpu.make_async_remote_copy(
                part.at[:, pl.ds(0, chunk)],
                recv.at[k],
                send1.at[0],
                recv1.at[k],
                device_id=(src_seq, g * slices + k),
                device_id_type=mesh_type,
            ).wait_recv()

    total = recv[0].astype(jnp.float32)
    for k in range(1, slices):
        total = total + recv[k].astype(jnp.float32)
    middle[...] = total.astype(middle.dtype)

    picked = jnp.dot(
        pick_out_ref[...].reshape(-1, pick_out_ref.shape[2]),
        middle[...],
        preferred_element_type=jnp.float32,
    )
    outgoing[...] = picked.reshape(outgoing.shape).astype(outgoing.dtype)

    def stage3(u):
        return pltpu.make_async_remote_copy(
            outgoing.at[u], landing.at[t], send3.at[u], recv3.at[t],
            device_id=(s, u), device_id_type=mesh_type,
        )

    pltpu.make_async_copy(outgoing.at[t], landing.at[t], recv3.at[t]).start()
    for k in range(1, tp_size):
        stage3((t + k) % tp_size).start()

    pltpu.make_async_copy(outgoing.at[t], landing.at[t], recv3.at[t]).wait()
    for k in range(1, tp_size):
        u = (t + k) % tp_size
        stage3(u).wait_send()
        pltpu.make_async_remote_copy(
            outgoing.at[u], landing.at[u], send3.at[u], recv3.at[u],
            device_id=(s, u), device_id_type=mesh_type,
        ).wait_recv()

    out_ref[...] = landing[...]


def run_experts(sums, hidden, out_weight, gain, pick_in, gate_weight, up_weight, down_weight,
                pick_out, seq_size, tp_size, slices):
    tokens, width = hidden.shape
    rows = pick_in.shape[0]
    chunk = width // slices
    vmem = pl.BlockSpec(memory_space=pltpu.VMEM)
    hbm = pl.BlockSpec(memory_space=pl.ANY)
    return pl.pallas_call(
        functools.partial(expert_kernel, seq_size, tp_size, slices),
        out_shape=(
            jax.ShapeDtypeStruct((tp_size, tokens, chunk), jnp.bfloat16),
            jax.ShapeDtypeStruct((tokens, width), jnp.float32),
            jax.ShapeDtypeStruct((tokens, width), jnp.bfloat16),
        ),
        in_specs=[vmem, vmem, hbm, vmem, vmem, hbm, hbm, hbm, vmem],
        out_specs=(vmem, vmem, vmem),
        scratch_shapes=[
            pltpu.VMEM(out_weight.shape, out_weight.dtype),
            pltpu.VMEM(gate_weight.shape, gate_weight.dtype),
            pltpu.VMEM(up_weight.shape, up_weight.dtype),
            pltpu.VMEM(down_weight.shape, down_weight.dtype),
            pltpu.SemaphoreType.DMA((4,)),
            pltpu.VMEM((tokens, width), jnp.bfloat16),
            pltpu.VMEM((tokens, width), jnp.float32),
            pltpu.VMEM((tp_size, tokens, width), jnp.bfloat16),
            pltpu.VMEM((rows, width), jnp.bfloat16),
            pltpu.VMEM((slices, rows, chunk), jnp.bfloat16),
            pltpu.VMEM((rows, chunk), jnp.bfloat16),
            pltpu.VMEM((tp_size, tokens, chunk), jnp.bfloat16),
            pltpu.VMEM((tp_size, tokens, chunk), jnp.bfloat16),
            pltpu.SemaphoreType.DMA((tp_size,)),
            pltpu.SemaphoreType.DMA((tp_size,)),
            pltpu.SemaphoreType.DMA((slices,)),
            pltpu.SemaphoreType.DMA((slices,)),
            pltpu.SemaphoreType.DMA((tp_size,)),
            pltpu.SemaphoreType.DMA((tp_size,)),
        ],
        compiler_params=pltpu.CompilerParams(
            collective_id=1, has_side_effects=True
        ),
    )(sums, hidden, out_weight, gain, pick_in, gate_weight, up_weight, down_weight, pick_out)


def body(
    hidden_in,
    new_query,
    new_key,
    new_value,
    key_cache,
    value_cache,
    lengths,
    out_weight,
    norm_gain,
    router_weight,
    expert_ids,
    gate_weight,
    up_weight,
    down_weight,
):
    req_dev, steps, width = hidden_in.shape
    block = key_cache.shape[1]
    head_size = width // HEADS
    scale = head_size ** (-0.5)
    seq_index = lax.axis_index("seq")
    tp_index = lax.axis_index("tp")
    seq_size = lax.axis_size("seq")
    tp_size = lax.axis_size("tp")
    rows = steps * HEADS
    own = req_dev * steps

    head_mask = (jnp.arange(width) // head_size)[None, :] == jnp.arange(HEADS)[:, None]
    q_wide = jnp.where(head_mask[None, None], new_query[:, :, None, :], 0).reshape(
        req_dev, rows, width
    )
    positions = seq_index * block + jnp.arange(block, dtype=jnp.int32)
    usable = (positions[None, :] < lengths[:, None]).astype(jnp.float32)
    usable = jnp.broadcast_to(usable[:, None, :], (req_dev, 8, block))
    fresh_scores = (
        jnp.einsum("rqd,rsd->rqs", q_wide, new_key, preferred_element_type=jnp.float32) * scale
    )
    causal = (
        (jnp.arange(rows)[:, None] // HEADS) >= jnp.arange(steps)[None, :]
    ) & (seq_index == 0)
    fresh_scores = jnp.where(causal, fresh_scores, masked_score)
    fresh_scores = jnp.pad(
        fresh_scores, ((0, 0), (0, 0), (0, 128 - steps)), constant_values=masked_score
    )
    fresh_ok = jnp.pad(
        jnp.broadcast_to(causal, (req_dev, rows, steps)).astype(jnp.float32),
        ((0, 0), (0, 0), (0, 128 - steps)),
    )
    fresh_value = jnp.pad(new_value, ((0, 0), (0, 128 - steps), (0, 0)))
    id_count = expert_ids.size
    id_rows = 8
    id_piece = jnp.pad(expert_ids.reshape(1, id_count), ((0, id_rows - 1), (0, 128 - id_count)))
    block_sums, all_id_pieces = exchange(
        q_wide, key_cache, value_cache, usable, fresh_scores, fresh_ok, fresh_value, id_piece,
        seq_size, tp_size, scale,
    )
    all_ids = all_id_pieces[:, 0, :id_count].reshape(tp_size * req_dev, steps, -1)
    feature_block = width // seq_size
    experts = router_weight.shape[1]
    topk = expert_ids.shape[2]
    requests = req_dev * tp_size
    capacity = (5 * requests * topk + 4 * experts - 1) // (4 * experts)
    expert_range = jnp.arange(experts, dtype=jnp.int32)
    slices = seq_size * tp_size // experts
    groups = tp_size // slices
    halves = slices // seq_size
    padded = 8 * ((steps * capacity + 7) // 8)
    tokens = 16 * ((own + 15) // 16)

    onehot = all_ids[..., None] == expert_range
    hits = jnp.sum(onehot.astype(jnp.int32), axis=2)
    earlier = jnp.cumsum(hits, axis=0) - hits
    all_slots = jnp.sum(jnp.where(onehot, earlier[:, :, None, :], 0), axis=3)
    row_of = jnp.arange(steps, dtype=jnp.int32)[None, :, None] * capacity + all_slots

    def rows_for(expert):
        hit = (all_ids == expert) & (all_slots < capacity)
        chosen_rows = jnp.any(
            hit[..., None] & (row_of[..., None] == jnp.arange(padded)), axis=2
        ).reshape(tp_size, own, padded)
        return jnp.pad(chosen_rows, ((0, 0), (0, tokens - own), (0, 0))).astype(jnp.bfloat16)

    mine = (seq_index * tp_size + tp_index) // slices
    mine_hit = (all_ids == mine) & (all_slots < capacity)
    pick_in = jnp.any(
        mine_hit[None] & (row_of[None] == jnp.arange(padded)[:, None, None, None]), axis=3
    ).reshape(padded, tp_size, own)
    pick_in = jnp.pad(pick_in, ((0, 0), (0, 0), (0, tokens - own))).astype(jnp.bfloat16)
    pick_in = pick_in.reshape(padded, tp_size * tokens)
    held = ((tp_index % slices) // halves) * groups + tp_index // slices
    pick_out = rows_for(held)
    hidden = jnp.pad(
        hidden_in.astype(jnp.float32).reshape(own, width), ((0, tokens - own), (0, 0))
    )
    landed, attention, normed = run_experts(
        block_sums, hidden, out_weight, norm_gain.reshape(1, width), pick_in, gate_weight,
        up_weight, down_weight, pick_out, seq_size, tp_size, slices,
    )
    attention = attention[:own].reshape(req_dev, steps, width)
    normed = normed[:own].reshape(req_dev, steps, width)
    attn_out = lax.dynamic_slice_in_dim(
        attention, seq_index * feature_block, feature_block, 2
    ).astype(jnp.bfloat16)
    residual = hidden_in.astype(jnp.float32) + attention

    logits = jnp.einsum("rtd,de->rte", normed, router_weight, preferred_element_type=jnp.float32)
    own_hot = expert_ids[..., None] == expert_range
    chosen = jnp.sum(jnp.where(own_hot, logits[:, :, None, :], 0.0), axis=3)
    share = 1.0 / (1.0 + jnp.exp(chosen[:, :, ::-1] - chosen))
    own_slots = lax.dynamic_slice_in_dim(all_slots, tp_index * req_dev, req_dev, 0)
    weight = jnp.where(own_slots < capacity, share, 0.0)
    slot_expert = (jnp.arange(tp_size // halves) % (tp_size // (groups * halves))) * groups + (
        jnp.arange(tp_size // halves) // (tp_size // (groups * halves))
    )
    per_slot = jnp.sum(
        jnp.where(expert_ids[..., None] == slot_expert, weight[..., None], 0.0), axis=2
    ).reshape(own, tp_size // halves)
    landed = landed.astype(jnp.float32).reshape(tp_size // halves, halves, tokens, feature_block // halves)
    mixture = jnp.einsum(
        "ia,ahif->ihf", per_slot, landed[:, :, :own], precision=lax.Precision.HIGHEST
    ).reshape(req_dev, steps, feature_block)
    own_residual = lax.dynamic_slice_in_dim(residual, seq_index * feature_block, feature_block, 2)
    layer_out = (own_residual + mixture).astype(jnp.bfloat16)
    return (attn_out, layer_out)


def solution(mesh):

    return jax.shard_map(
        body,
        mesh=mesh,
        in_specs=(
            P("tp", None, None),
            P("tp", None, None),
            P("tp", None, None),
            P("tp", None, None),
            P("tp", "seq", None),
            P("tp", "seq", None),
            P("tp"),
            P(),
            P(),
            P(),
            P("tp", None, None),
            P(("seq", "tp"), None),
            P(("seq", "tp"), None),
            P(("seq", "tp"), None),
        ),
        out_specs=(P("tp", None, "seq"), P("tp", None, "seq")),
        check_vma=False,
    )
```

```python
import functools

import jax
import jax.numpy as jnp
from jax import lax
from jax.experimental import pallas as pl
from jax.experimental.pallas import tpu as pltpu
from jax.sharding import PartitionSpec as P

HEADS = 16


masked_score = -1e30
norm_epsilon = 1e-06


def exchange_kernel(seq_size, tp_size, scale, query_ref, key_hbm, value_hbm, usable_ref,
                    fresh_ref, fresh_ok_ref, fresh_value_ref, ids_ref, sums_out,
                    ids_out, keys, values, sums, sums_land, ids_land,
                    load_sem, send_a, recv_a, send_b, recv_b):
    mesh_type = pl.DeviceIdType.MESH
    s = lax.axis_index("seq")
    t = lax.axis_index("tp")
    req_dev, rows, width = query_ref.shape
    heads = HEADS

    barrier = pltpu.get_barrier_semaphore()
    for u in range(seq_size):
        @pl.when(s != u)
        def _():
            pl.semaphore_signal(barrier, inc=1, device_id=(u, t), device_id_type=mesh_type)
    for u in range(tp_size):
        @pl.when(t != u)
        def _():
            pl.semaphore_signal(barrier, inc=1, device_id=(s, u), device_id_type=mesh_type)

    loads = []
    for r in range(req_dev):
        loads.append(pltpu.make_async_copy(key_hbm.at[r], keys.at[r], load_sem.at[0, r]))
        loads.append(pltpu.make_async_copy(value_hbm.at[r], values.at[r], load_sem.at[1, r]))
    for copy in loads:
        copy.start()

    head_of = lax.broadcasted_iota(jnp.int32, (rows, width), 1) // (width // heads)
    row_head = lax.broadcasted_iota(jnp.int32, (rows, width), 0) % heads
    own_head = head_of == row_head
    spread = (
        lax.broadcasted_iota(jnp.int32, (rows // heads, rows), 1) // heads
        == lax.broadcasted_iota(jnp.int32, (rows // heads, rows), 0)
    ).astype(jnp.float32)
    contract = (((1,), (1,)), ((), ()))
    for r in range(req_dev):
        loads[2 * r].wait()
        scores = lax.dot_general(
            query_ref[r], keys[r], contract, preferred_element_type=jnp.float32
        ) * scale
        usable = usable_ref[r, 0:1, :] > 0.5
        scores = jnp.where(usable, scores, masked_score)
        fresh = fresh_ref[r]
        fresh_ok = fresh_ok_ref[r] > 0.5
        top = jnp.maximum(
            jnp.max(scores, axis=1, keepdims=True), jnp.max(fresh, axis=1, keepdims=True)
        )
        weights = jnp.where(usable, jnp.exp(scores - top), 0.0)
        fresh_weights = jnp.where(fresh_ok, jnp.exp(fresh - top), 0.0)
        total = jnp.sum(weights, axis=1, keepdims=True) + jnp.sum(
            fresh_weights, axis=1, keepdims=True
        )
        loads[2 * r + 1].wait()
        wide = jnp.dot(
            weights.astype(jnp.bfloat16), values[r], preferred_element_type=jnp.float32
        ) + jnp.dot(
            fresh_weights.astype(jnp.bfloat16), fresh_value_ref[r],
            preferred_element_type=jnp.float32,
        )
        wide = jnp.where(own_head, wide, 0.0)
        steps = rows // heads
        sums[r, 0:steps, :] = jnp.sum(wide.reshape(steps, heads, width), axis=1)
        sums[r, steps : 2 * steps, :] = jnp.dot(
            spread, jnp.where(own_head, top, 0.0),
            precision=lax.Precision.HIGHEST, preferred_element_type=jnp.float32,
        )
        sums[r, 2 * steps : 3 * steps, :] = jnp.dot(
            spread, jnp.where(own_head, total, 0.0),
            precision=lax.Precision.HIGHEST, preferred_element_type=jnp.float32,
        )

    pl.semaphore_wait(barrier, seq_size - 1 + tp_size - 1)

    def sums_copy(u, slot):
        return pltpu.make_async_remote_copy(
            sums, sums_land.at[slot], send_a.at[u], recv_a.at[slot],
            device_id=(u, t), device_id_type=mesh_type,
        )

    def along_tp(u, slot):
        return pltpu.make_async_remote_copy(
            ids_ref, ids_land.at[slot], send_b.at[u], recv_b.at[slot],
            device_id=(s, u), device_id_type=mesh_type,
        )

    pltpu.make_async_copy(sums, sums_land.at[s], recv_a.at[s]).start()
    for k in range(1, seq_size):
        sums_copy((s + k) % seq_size, s).start()
    pltpu.make_async_copy(ids_ref, ids_land.at[t], recv_b.at[t]).start()
    for k in range(1, tp_size):
        along_tp((t + k) % tp_size, t).start()

    pltpu.make_async_copy(sums, sums_land.at[s], recv_a.at[s]).wait()
    for k in range(1, seq_size):
        u = (s + k) % seq_size
        sums_copy(u, s).wait_send()
        sums_copy(u, u).wait_recv()
    pltpu.make_async_copy(ids_ref, ids_land.at[t], recv_b.at[t]).wait()
    for k in range(1, tp_size):
        u = (t + k) % tp_size
        along_tp(u, t).wait_send()
        along_tp(u, u).wait_recv()

    sums_out[...] = sums_land[...]
    ids_out[...] = ids_land[...]


def exchange(query, key_cache, value_cache, usable, fresh, fresh_ok, fresh_value, ids,
             seq_size, tp_size, scale):
    req_dev, rows, width = query.shape
    steps = rows // HEADS
    vmem = pl.BlockSpec(memory_space=pltpu.VMEM)
    return pl.pallas_call(
        functools.partial(exchange_kernel, seq_size, tp_size, scale),
        out_shape=(
            jax.ShapeDtypeStruct((seq_size, req_dev, 3 * steps, width), jnp.float32),
            jax.ShapeDtypeStruct((tp_size,) + ids.shape, ids.dtype),
        ),
        in_specs=[vmem, pl.BlockSpec(memory_space=pl.ANY), pl.BlockSpec(memory_space=pl.ANY)]
        + [vmem] * 5,
        out_specs=(vmem, vmem),
        scratch_shapes=[
            pltpu.VMEM(key_cache.shape, key_cache.dtype),
            pltpu.VMEM(value_cache.shape, value_cache.dtype),
            pltpu.VMEM((req_dev, 3 * steps, width), jnp.float32),
            pltpu.VMEM((seq_size, req_dev, 3 * steps, width), jnp.float32),
            pltpu.VMEM((tp_size,) + ids.shape, ids.dtype),
            pltpu.SemaphoreType.DMA((2, req_dev)),
            pltpu.SemaphoreType.DMA((seq_size,)),
            pltpu.SemaphoreType.DMA((seq_size,)),
            pltpu.SemaphoreType.DMA((tp_size,)),
            pltpu.SemaphoreType.DMA((tp_size,)),
        ],
        compiler_params=pltpu.CompilerParams(
            collective_id=0, has_side_effects=True, vmem_limit_bytes=48 * 1024 * 1024
        ),
    )(query, key_cache, value_cache, usable, fresh, fresh_ok, fresh_value, ids)


def expert_kernel(seq_size, tp_size, slices, sums_ref, hidden_ref, out_weight_hbm, gain_ref,
                  pick_in_ref, gate_hbm, up_hbm, down_hbm, pick_out_ref, out_ref, attn_ref,
                  normed_ref, out_weight_ref, gate_ref, up_ref, down_ref, load_sem, piece_ref,
                  context, everyone, part, recv, middle, outgoing, landing, send0, recv0,
                  send1, recv1, send3, recv3):
    mesh_type = pl.DeviceIdType.MESH
    s = lax.axis_index("seq")
    t = lax.axis_index("tp")
    g = t // slices
    j = t % slices
    chunk = recv.shape[2]
    halves = slices // seq_size
    src_seq = j // halves

    def dest(i):
        return (i // halves, g * slices + s * halves + i % halves)

    def is_self(i):
        return (i // halves == s) & (g * slices + s * halves + i % halves == t)

    barrier = pltpu.get_barrier_semaphore()
    for u in range(tp_size):
        @pl.when(t != u)
        def _():
            pl.semaphore_signal(barrier, inc=1, device_id=(s, u), device_id_type=mesh_type)
    for i in range(slices):
        @pl.when(i // halves != s)
        def _():
            pl.semaphore_signal(barrier, inc=1, device_id=dest(i), device_id_type=mesh_type)
    for k in range(slices):
        @pl.when((src_seq != s) & (k // halves != s))
        def _():
            pl.semaphore_signal(
                barrier, inc=1, device_id=(src_seq, g * slices + k), device_id_type=mesh_type
            )
    loads = [
        pltpu.make_async_copy(src_hbm, dst, load_sem.at[n])
        for n, (src_hbm, dst) in enumerate(
            [(out_weight_hbm, out_weight_ref), (gate_hbm, gate_ref), (up_hbm, up_ref),
             (down_hbm, down_ref)]
        )
    ]
    for copy in loads:
        copy.start()

    req_dev = sums_ref.shape[1]
    steps = sums_ref.shape[2] // 3
    context[...] = jnp.zeros_like(context)
    for r in range(req_dev):
        block_sums = [sums_ref[b, r, 0:steps, :] for b in range(seq_size)]
        block_max = [sums_ref[b, r, steps : 2 * steps, :] for b in range(seq_size)]
        block_totals = [sums_ref[b, r, 2 * steps : 3 * steps, :] for b in range(seq_size)]
        overall = block_max[0]
        for b in range(1, seq_size):
            overall = jnp.maximum(overall, block_max[b])
        numer = jnp.zeros_like(overall)
        denom = jnp.zeros_like(overall)
        for b in range(seq_size):
            factor = jnp.exp(block_max[b] - overall)
            numer = numer + factor * block_sums[b]
            denom = denom + factor * block_totals[b]
        context[r * steps : (r + 1) * steps, :] = numer / denom
    loads[0].wait()
    attention = jnp.dot(
        context[...].astype(jnp.bfloat16), out_weight_ref[...], preferred_element_type=jnp.float32
    )
    attn_ref[...] = attention
    residual = hidden_ref[...] + attention
    mean_square = jnp.mean(residual * residual, axis=1, keepdims=True)
    normed = (residual * lax.rsqrt(mean_square + norm_epsilon) * gain_ref[...]).astype(
        jnp.bfloat16
    )
    piece_ref[...] = normed
    normed_ref[...] = normed

    far = (seq_size - 1) * halves
    near = tp_size - 1 + far

    @pl.when(src_seq == s)
    def _():
        pl.semaphore_wait(barrier, near)

    @pl.when(src_seq != s)
    def _():
        pl.semaphore_wait(barrier, near + slices - halves)

    def gather(u, slot):
        return pltpu.make_async_remote_copy(
            piece_ref, everyone.at[slot], send0.at[u], recv0.at[slot],
            device_id=(s, u), device_id_type=mesh_type,
        )

    pltpu.make_async_copy(piece_ref, everyone.at[t], recv0.at[t]).start()
    for k in range(1, tp_size):
        gather((t + k) % tp_size, t).start()

    pltpu.make_async_copy(piece_ref, everyone.at[t], recv0.at[t]).wait()
    for k in range(1, tp_size):
        u = (t + k) % tp_size
        gather(u, t).wait_send()
        gather(u, u).wait_recv()

    for copy in loads[1:]:
        copy.wait()
    rows_in = everyone[...].reshape(-1, everyone.shape[2])
    buffer = jnp.dot(pick_in_ref[...], rows_in, preferred_element_type=jnp.float32).astype(
        jnp.bfloat16
    )
    contract = (((1,), (1,)), ((), ()))
    gate = lax.dot_general(buffer, gate_ref[...], contract, preferred_element_type=jnp.float32)
    upward = lax.dot_general(buffer, up_ref[...], contract, preferred_element_type=jnp.float32)
    inner = (jax.nn.gelu(gate) * upward).astype(jnp.bfloat16)
    part[...] = jnp.dot(inner, down_ref[...], preferred_element_type=jnp.float32).astype(
        part.dtype
    )

    def stage1(i):
        return pltpu.make_async_remote_copy(
            part.at[:, pl.ds(i * chunk, chunk)],
            recv.at[j],
            send1.at[i],
            recv1.at[j],
            device_id=dest(i),
            device_id_type=mesh_type,
        )

    for i in range(slices):
        @pl.when(is_self(i))
        def _():
            pltpu.make_async_copy(part.at[:, pl.ds(i * chunk, chunk)], recv.at[j], recv1.at[j]).start()

        @pl.when(jnp.logical_not(is_self(i)))
        def _():
            stage1(i).start()

    for i in range(slices):
        @pl.when(jnp.logical_not(is_self(i)))
        def _():
            stage1(i).wait_send()

    for k in range(slices):
        from_self = (src_seq == s) & (k == j)

        @pl.when(from_self)
        def _():
            pltpu.make_async_copy(part.at[:, pl.ds(0, chunk)], recv.at[k], recv1.at[k]).wait()

        @pl.when(jnp.logical_not(from_self))
        def _():
            pltpu.make_async_remote_copy(
                part.at[:, pl.ds(0, chunk)],
                recv.at[k],
                send1.at[0],
                recv1.at[k],
                device_id=(src_seq, g * slices + k),
                device_id_type=mesh_type,
            ).wait_recv()

    total = recv[0].astype(jnp.float32)
    for k in range(1, slices):
        total = total + recv[k].astype(jnp.float32)
    middle[...] = total.astype(middle.dtype)

    picked = jnp.dot(
        pick_out_ref[...].reshape(-1, pick_out_ref.shape[2]),
        middle[...],
        preferred_element_type=jnp.float32,
    )
    outgoing[...] = picked.reshape(outgoing.shape).astype(outgoing.dtype)

    def stage3(u):
        return pltpu.make_async_remote_copy(
            outgoing.at[u], landing.at[t], send3.at[u], recv3.at[t],
            device_id=(s, u), device_id_type=mesh_type,
        )

    pltpu.make_async_copy(outgoing.at[t], landing.at[t], recv3.at[t]).start()
    for k in range(1, tp_size):
        stage3((t + k) % tp_size).start()

    pltpu.make_async_copy(outgoing.at[t], landing.at[t], recv3.at[t]).wait()
    for k in range(1, tp_size):
        u = (t + k) % tp_size
        stage3(u).wait_send()
        pltpu.make_async_remote_copy(
            outgoing.at[u], landing.at[u], send3.at[u], recv3.at[u],
            device_id=(s, u), device_id_type=mesh_type,
        ).wait_recv()

    out_ref[...] = landing[...]


def run_experts(sums, hidden, out_weight, gain, pick_in, gate_weight, up_weight, down_weight,
                pick_out, seq_size, tp_size, slices):
    tokens, width = hidden.shape
    rows = pick_in.shape[0]
    chunk = width // slices
    vmem = pl.BlockSpec(memory_space=pltpu.VMEM)
    hbm = pl.BlockSpec(memory_space=pl.ANY)
    return pl.pallas_call(
        functools.partial(expert_kernel, seq_size, tp_size, slices),
        out_shape=(
            jax.ShapeDtypeStruct((tp_size, tokens, chunk), jnp.bfloat16),
            jax.ShapeDtypeStruct((tokens, width), jnp.float32),
            jax.ShapeDtypeStruct((tokens, width), jnp.bfloat16),
        ),
        in_specs=[vmem, vmem, hbm, vmem, vmem, hbm, hbm, hbm, vmem],
        out_specs=(vmem, vmem, vmem),
        scratch_shapes=[
            pltpu.VMEM(out_weight.shape, out_weight.dtype),
            pltpu.VMEM(gate_weight.shape, gate_weight.dtype),
            pltpu.VMEM(up_weight.shape, up_weight.dtype),
            pltpu.VMEM(down_weight.shape, down_weight.dtype),
            pltpu.SemaphoreType.DMA((4,)),
            pltpu.VMEM((tokens, width), jnp.bfloat16),
            pltpu.VMEM((tokens, width), jnp.float32),
            pltpu.VMEM((tp_size, tokens, width), jnp.bfloat16),
            pltpu.VMEM((rows, width), jnp.bfloat16),
            pltpu.VMEM((slices, rows, chunk), jnp.bfloat16),
            pltpu.VMEM((rows, chunk), jnp.bfloat16),
            pltpu.VMEM((tp_size, tokens, chunk), jnp.bfloat16),
            pltpu.VMEM((tp_size, tokens, chunk), jnp.bfloat16),
            pltpu.SemaphoreType.DMA((tp_size,)),
            pltpu.SemaphoreType.DMA((tp_size,)),
            pltpu.SemaphoreType.DMA((slices,)),
            pltpu.SemaphoreType.DMA((slices,)),
            pltpu.SemaphoreType.DMA((tp_size,)),
            pltpu.SemaphoreType.DMA((tp_size,)),
        ],
        compiler_params=pltpu.CompilerParams(
            collective_id=1, has_side_effects=True
        ),
    )(sums, hidden, out_weight, gain, pick_in, gate_weight, up_weight, down_weight, pick_out)


def body(
    hidden_in,
    new_query,
    new_key,
    new_value,
    key_cache,
    value_cache,
    lengths,
    out_weight,
    norm_gain,
    router_weight,
    expert_ids,
    gate_weight,
    up_weight,
    down_weight,
):
    req_dev, steps, width = hidden_in.shape
    block = key_cache.shape[1]
    head_size = width // HEADS
    scale = head_size ** (-0.5)
    seq_index = lax.axis_index("seq")
    tp_index = lax.axis_index("tp")
    seq_size = lax.axis_size("seq")
    tp_size = lax.axis_size("tp")
    rows = steps * HEADS
    own = req_dev * steps

    head_mask = (jnp.arange(width) // head_size)[None, :] == jnp.arange(HEADS)[:, None]
    q_wide = jnp.where(head_mask[None, None], new_query[:, :, None, :], 0).reshape(
        req_dev, rows, width
    )
    positions = seq_index * block + jnp.arange(block, dtype=jnp.int32)
    usable = (positions[None, :] < lengths[:, None]).astype(jnp.float32)
    usable = jnp.broadcast_to(usable[:, None, :], (req_dev, 8, block))
    fresh_scores = (
        jnp.einsum("rqd,rsd->rqs", q_wide, new_key, preferred_element_type=jnp.float32) * scale
    )
    causal = (
        (jnp.arange(rows)[:, None] // HEADS) >= jnp.arange(steps)[None, :]
    ) & (seq_index == 0)
    fresh_scores = jnp.where(causal, fresh_scores, masked_score)
    fresh_scores = jnp.pad(
        fresh_scores, ((0, 0), (0, 0), (0, 128 - steps)), constant_values=masked_score
    )
    fresh_ok = jnp.pad(
        jnp.broadcast_to(causal, (req_dev, rows, steps)).astype(jnp.float32),
        ((0, 0), (0, 0), (0, 128 - steps)),
    )
    fresh_value = jnp.pad(new_value, ((0, 0), (0, 128 - steps), (0, 0)))
    id_count = expert_ids.size
    id_rows = 8
    id_piece = jnp.pad(expert_ids.reshape(1, id_count), ((0, id_rows - 1), (0, 128 - id_count)))
    block_sums, all_id_pieces = exchange(
        q_wide, key_cache, value_cache, usable, fresh_scores, fresh_ok, fresh_value, id_piece,
        seq_size, tp_size, scale,
    )
    all_ids = all_id_pieces[:, 0, :id_count].reshape(tp_size * req_dev, steps, -1)
    feature_block = width // seq_size
    experts = router_weight.shape[1]
    topk = expert_ids.shape[2]
    requests = req_dev * tp_size
    capacity = (5 * requests * topk + 4 * experts - 1) // (4 * experts)
    expert_range = jnp.arange(experts, dtype=jnp.int32)
    slices = seq_size * tp_size // experts
    groups = tp_size // slices
    halves = slices // seq_size
    padded = 8 * ((steps * capacity + 7) // 8)
    tokens = 16 * ((own + 15) // 16)

    onehot = all_ids[..., None] == expert_range
    hits = jnp.sum(onehot.astype(jnp.int32), axis=2)
    earlier = jnp.cumsum(hits, axis=0) - hits
    all_slots = jnp.sum(jnp.where(onehot, earlier[:, :, None, :], 0), axis=3)
    row_of = jnp.arange(steps, dtype=jnp.int32)[None, :, None] * capacity + all_slots

    def rows_for(expert):
        hit = (all_ids == expert) & (all_slots < capacity)
        chosen_rows = jnp.any(
            hit[..., None] & (row_of[..., None] == jnp.arange(padded)), axis=2
        ).reshape(tp_size, own, padded)
        return jnp.pad(chosen_rows, ((0, 0), (0, tokens - own), (0, 0))).astype(jnp.bfloat16)

    mine = (seq_index * tp_size + tp_index) // slices
    pick_in = rows_for(mine).reshape(tp_size * tokens, padded).T
    held = ((tp_index % slices) // halves) * groups + tp_index // slices
    pick_out = rows_for(held)
    hidden = jnp.pad(
        hidden_in.astype(jnp.float32).reshape(own, width), ((0, tokens - own), (0, 0))
    )
    landed, attention, normed = run_experts(
        block_sums, hidden, out_weight, norm_gain.reshape(1, width), pick_in, gate_weight,
        up_weight, down_weight, pick_out, seq_size, tp_size, slices,
    )
    attention = attention[:own].reshape(req_dev, steps, width)
    normed = normed[:own].reshape(req_dev, steps, width)
    attn_out = lax.dynamic_slice_in_dim(
        attention, seq_index * feature_block, feature_block, 2
    ).astype(jnp.bfloat16)
    residual = hidden_in.astype(jnp.float32) + attention

    logits = jnp.einsum("rtd,de->rte", normed, router_weight, preferred_element_type=jnp.float32)
    own_hot = expert_ids[..., None] == expert_range
    chosen = jnp.sum(jnp.where(own_hot, logits[:, :, None, :], 0.0), axis=3)
    share = 1.0 / (1.0 + jnp.exp(chosen[:, :, ::-1] - chosen))
    own_slots = lax.dynamic_slice_in_dim(all_slots, tp_index * req_dev, req_dev, 0)
    weight = jnp.where(own_slots < capacity, share, 0.0)
    slot_expert = (jnp.arange(tp_size // halves) % (tp_size // (groups * halves))) * groups + (
        jnp.arange(tp_size // halves) // (tp_size // (groups * halves))
    )
    per_slot = jnp.sum(
        jnp.where(expert_ids[..., None] == slot_expert, weight[..., None], 0.0), axis=2
    ).reshape(own, tp_size // halves)
    landed = landed.astype(jnp.float32).reshape(tp_size // halves, halves, tokens, feature_block // halves)
    mixture = jnp.einsum(
        "ia,ahif->ihf", per_slot, landed[:, :, :own], precision=lax.Precision.HIGHEST
    ).reshape(req_dev, steps, feature_block)
    own_residual = lax.dynamic_slice_in_dim(residual, seq_index * feature_block, feature_block, 2)
    layer_out = (own_residual + mixture).astype(jnp.bfloat16)
    return (attn_out, layer_out)


def solution(mesh):

    return jax.shard_map(
        body,
        mesh=mesh,
        in_specs=(
            P("tp", None, None),
            P("tp", None, None),
            P("tp", None, None),
            P("tp", None, None),
            P("tp", "seq", None),
            P("tp", "seq", None),
            P("tp"),
            P(),
            P(),
            P(),
            P("tp", None, None),
            P(("seq", "tp"), None),
            P(("seq", "tp"), None),
            P(("seq", "tp"), None),
        ),
        out_specs=(P("tp", None, "seq"), P("tp", None, "seq")),
        check_vma=False,
    )
```
